32 devices in a mesh: grp: 2 (over y), energy: 4 (over z), atom: 2 (over x), kz: 2 (over core).
Axes of the slice: x: 2, y: 2, z: 4, core: 2. Of those that a mesh axis runs over, the one named last changes fastest.
Arguments:
- green: float32 [8, 32, 512, 512], P(('grp', 'kz'), 'energy', 'atom'), parts along dimension 0, may hold values from -6 to 6
- couplings: float32 [4, 512, 512], P('atom'), may hold values from -0.25 to 0.25
- occupation: float32 [3], replicated, may hold values from 0.05 to 2
- offsets: int32 [3], replicated, may hold values from 1 to 16, as said below
- owners: int32 [3], replicated, may hold values from 0 to 3
Outputs:
- sigma: float32 [1024, 32, 512], P(('grp', 'atom', 'kz'), 'energy'), parts along dimension 0
The draws below stay inside these ranges and needn't reach their ends.
There are 2 independent parts, one for each index of `grp`. The reference program is written for one: setup_inputs(seed, part) draws one part's arguments, and reference() takes and returns one part's arrays. A program takes and returns all parts, laid end to end along the dimension named above; an argument that names none is the same for every part. Nothing has to cross between parts.
Inputs may be any that keep to these rules, and one draw needn't show every extreme that they name: `offsets`: one mode's offset is exactly 16.
All inputs are finite; a program needn't handle non-finite values.
Results may differ from the reference program's by a relative error of at most 0.0001.
Values sent between devices are 32-bit elements; how exact they have to be, the bound alone decides.
No kernel may reach another device: no remote copies, remote signals or barrier semaphores. Data moves between devices by JAX's collectives and lax.ppermute only.
A program may use at most 192 MiB of HBM per device.

```python
import math
import jax
import jax.numpy as jnp
from jax import lax

B = 512
MODES = 3
E_DEV = 8
NE = 32
KPTS = 4
NCOUP = 4


def draw_offsets(key, part):
    rest_key = jax.random.fold_in(key, 12)
    order_key = jax.random.fold_in(key, 13)
    leading = jnp.full((1,), 2 * E_DEV, dtype=jnp.int32)
    others = jax.random.randint(rest_key, (MODES - 1,), 1, 2 * E_DEV + 1).astype(jnp.int32)
    values = jnp.concatenate([leading, others]).astype(jnp.int32)
    return jax.random.permutation(order_key, values).astype(jnp.int32)


def shard_levels(stream_key, extent, shards, low, largest):
    loudness, own = 1.0, jax.random.fold_in(stream_key, 6)
    for axis_at, blocks in shards:
        heights = jnp.exp(jax.random.uniform(jax.random.fold_in(own, axis_at), (blocks,), jnp.float32, low / len(shards), largest / len(shards)))
        loudness = loudness * jnp.repeat(heights, extent[axis_at] // blocks).reshape([-1 if axis == axis_at else 1 for axis in range(len(extent))])
    return loudness


def scatter_about(own_key, dims, width, limit, shards=(), kind=jnp.bfloat16):
    drawn = jax.random.normal(own_key, dims, jnp.float32) * width
    if len(shards) > 0:
        drawn = shard_levels(own_key, dims, shards, -0.22, 0.18) * drawn
    return jnp.clip(drawn, min=-limit, max=limit).astype(kind)


def setup_inputs(seed: int = 0, part: int = 0) -> dict:
    arg_keys = jax.random.split(jax.random.key(seed), 6)
    part_splits = jax.random.split(jax.random.fold_in(arg_keys[5], part), 6)
    return {
        "green": scatter_about(part_splits[0], (KPTS, NE, B, B), 1.0, 6.0, ((0, 2), (1, 4), (2, 2)), jnp.float32),
        "couplings": scatter_about(arg_keys[1], (NCOUP, B, B), B ** -0.5, 0.25, ((0, 2),), jnp.float32),
        "occupation": jnp.clip(jnp.exp(jax.random.uniform(arg_keys[2], (MODES,), jnp.float32, math.log(0.05), math.log(2.0))), 0.05, 2.0),
        "offsets": draw_offsets(jax.random.fold_in(arg_keys[5], 71), part),
        "owners": jax.random.randint(arg_keys[4], (MODES,), 0, NCOUP).astype(jnp.int32),
    }


def reference(green, couplings, occupation, offsets, owners):
    summed = jnp.sum(green, axis=0)
    total = jnp.zeros((B, NE, B), jnp.float32)
    for mode in range(MODES):
        coupling = couplings[owners[mode]]
        upper = jnp.roll(summed, -offsets[mode], axis=0)
        lower = jnp.roll(summed, offsets[mode], axis=0)
        weight = occupation[mode]
        combined = ((1.0 + weight) * upper + weight * lower) / KPTS
        product = jnp.einsum("ebc,dc->ebd", combined, coupling, precision=lax.Precision.HIGHEST)
        total = total + jnp.einsum("ab,ebd->aed", coupling, product, precision=lax.Precision.HIGHEST)
    return total
```

```python
import functools

import jax
import jax.numpy as jnp
from jax import lax
from jax.experimental import pallas as pl
from jax.experimental.pallas import tpu as pltpu
from jax.sharding import PartitionSpec as P

MODES = 3
REACH = 2
PIECES = 4


def halves(x):
    high = lax.reduce_precision(x, exponent_bits=8, mantissa_bits=7)
    return high.astype(jnp.bfloat16), (x - high).astype(jnp.bfloat16)


def split_dot(n_groups, n_parts, grid_total, edev, far, line, ints, weights, right_high, right_low, left, *refs):
    sources = [
        [refs[(g * 2 + h) * n_parts : (g * 2 + h + 1) * n_parts] for h in range(2)]
        for g in range(n_groups)
    ]
    outs = refs[n_groups * 2 * n_parts : -3]
    planes, inner, sems = refs[-3:]
    rows = planes.shape[1]
    half_planes = edev // 2
    place, core, blocks = ints[MODES], ints[MODES + 1], grid_total // edev
    energy = ints[MODES + 2]
    target = blocks - 1 - place if far else place
    scales = []
    for mode in range(MODES):
        for side in range(2):
            step = ints[mode] if side == 0 else -ints[mode]
            source = lax.rem(target * edev + energy + step + grid_total, grid_total)
            block = lax.div(source, edev)
            plane = lax.rem(source, edev)
            rel = block - place
            if far:
                valid = rel == 0
            elif line:
                valid = jnp.abs(rel) <= REACH
            else:
                rel = lax.rem(rel + REACH + blocks, blocks) - REACH
                valid = rel <= REACH
            group = jnp.where(valid, rel + n_groups // 2, n_groups // 2)
            half = lax.div(plane, half_planes)
            other = jnp.where(half == core, 0, 1)
            at = lax.rem(plane, half_planes)
            slot = mode * 2 + side
            for g in range(n_groups):
                for h in range(2):

                    @pl.when((group == g) & (other == h))
                    def _(g=g, h=h):
                        first = 0
                        for ref in sources[g][h]:
                            size = ref.shape[1]
                            pltpu.make_async_copy(
                                ref.at[at], planes.at[slot, pl.ds(first, size)], sems.at[slot]
                            ).start()
                            first += size

            scales.append(jnp.where(valid, weights[slot], 0.0))
    for mode in range(MODES):
        for side in range(2):
            slot = mode * 2 + side
            pltpu.make_async_copy(planes.at[slot], planes.at[slot], sems.at[slot]).wait()
        combined = scales[2 * mode] * planes[2 * mode] + scales[2 * mode + 1] * planes[2 * mode + 1]
        high = combined.astype(jnp.bfloat16)
        low = (combined - high.astype(jnp.float32)).astype(jnp.bfloat16)
        dot = functools.partial(jnp.dot, preferred_element_type=jnp.float32)
        product = dot(high, right_high[mode]) + dot(low, right_high[mode]) + dot(high, right_low[mode])
        high = product.astype(jnp.bfloat16)
        low = (product - high.astype(jnp.float32)).astype(jnp.bfloat16)
        inner[pl.ds(3 * mode * rows, rows)] = high
        inner[pl.ds((3 * mode + 1) * rows, rows)] = low
        inner[pl.ds((3 * mode + 2) * rows, rows)] = high
    size = outs[0].shape[0]
    for index, out in enumerate(outs):
        out[...] = jnp.dot(
            left[pl.ds(index * size, size)], inner[...], preferred_element_type=jnp.float32
        )


def sandwich(ints, weights, right, left, groups, grid_total, edev, far, line, out_rows):
    order = right[0].shape[-1]
    flat = [part for group in groups for half in group for part in half]
    rows = sum(part.shape[1] for part in groups[0][0])
    n_out = left.shape[0] // out_rows
    flops = 2 * 3 * MODES * (rows * order * order + left.shape[0] * rows * order)
    return pl.pallas_call(
        functools.partial(split_dot, len(groups), len(groups[0][0]), grid_total, edev, far, line),
        out_shape=[jax.ShapeDtypeStruct((out_rows, order), jnp.float32)] * n_out,
        in_specs=[pl.BlockSpec(memory_space=pltpu.SMEM)] * 2
        + [pl.BlockSpec(memory_space=pltpu.VMEM)] * 3
        + [pl.BlockSpec(memory_space=pl.ANY)] * len(flat),
        out_specs=[pl.BlockSpec(memory_space=pltpu.VMEM)] * n_out,
        scratch_shapes=[
            pltpu.VMEM((2 * MODES, rows, order), jnp.float32),
            pltpu.VMEM((3 * MODES * rows, order), jnp.bfloat16),
            pltpu.SemaphoreType.DMA((2 * MODES,)),
        ],
        compiler_params=pltpu.CompilerParams(vmem_limit_bytes=40 << 20),
        cost_estimate=pl.CostEstimate(
            flops=flops, bytes_accessed=4 * (2 * MODES * rows * order + left.shape[0] * order), transcendentals=0
        ),
        name="far_sandwich" if far else "near_sandwich",
    )(ints, weights, right[0], right[1], left, *flat)


def gather_up(terms, count, ints, *refs):
    out = refs[-1]
    core = ints[MODES + 1]
    for own in range(2):

        @pl.when(core == own)
        def _(own=own):
            at = 0
            for half in range(2):
                where = own if half == 0 else 1 - own
                for j in range(count):
                    total = refs[at][...]
                    for ref in refs[at + 1 : at + terms]:
                        total = total + ref[...]
                    at += terms
                    out[:, where * count + j, :] = total


def shards(green, couplings, occupation, offsets, owners):
    momenta_here, edev, brows, order = green.shape
    n, atoms, cores = lax.axis_size("energy"), lax.axis_size("atom"), lax.axis_size("kz")
    parts = lax.axis_size("grp")
    momenta = momenta_here * cores
    grid_total = n * edev
    place, atom, core, part = (lax.axis_index(a) for a in ("energy", "atom", "kz", "grp"))
    line = n == 2 * REACH
    half = edev // cores
    swap = [(i, (i + 1) % cores) for i in range(cores)]

    split = green.reshape(momenta_here, cores, half, brows, order)
    mine = lax.dynamic_index_in_dim(split, core, 1, keepdims=False)
    theirs = lax.dynamic_index_in_dim(split, (core + 1) % cores, 1, keepdims=False)
    size = brows // PIECES
    own = []
    for piece in range(PIECES):
        rows = slice(piece * size, (piece + 1) * size)
        sent = lax.ppermute(jnp.sum(theirs[:, :, rows], axis=0), "kz", swap)
        own.append(jnp.sum(mine[:, :, rows], axis=0) + sent)

    def shift(arrays, axis, pairs):
        return [lax.ppermute(a, axis, pairs) for a in arrays]

    if line:
        up = [[(i, i + 1) for i in range(d, n - 1)] for d in range(REACH)]
        down = [[(i, i - 1) for i in range(n - 1 - d, 0, -1)] for d in range(REACH)]
    else:
        up = [[(i, (i + 1) % n) for i in range(n)]] * REACH
        down = [[(i, (i - 1) % n) for i in range(n)]] * REACH
    streams = {0: own}
    for d in range(1, REACH + 1):
        streams[-d] = shift(streams[1 - d], "energy", up[d - 1])
        streams[d] = shift(streams[d - 1], "energy", down[d - 1])

    table_rows = couplings.shape[0]
    strip = order // (parts * cores)
    slice_of = lax.dynamic_slice(
        couplings, (0, (part * cores + core) * strip, 0), (table_rows, strip, order)
    )
    tables = [couplings]
    for s in range(1, atoms):
        piece = lax.ppermute(slice_of, "atom", [(i, (i + s) % atoms) for i in range(atoms)])
        over = [piece] + [
            lax.ppermute(piece, "grp", [(i, (i + d) % parts) for i in range(parts)]) for d in range(1, parts)
        ]
        over = jnp.stack(over, 0)
        over = jnp.stack(
            [lax.dynamic_index_in_dim(over, (part - g) % parts, 0, keepdims=False) for g in range(parts)], 0
        )
        both = [over] + [
            lax.ppermute(over, "kz", [(i, (i + d) % cores) for i in range(cores)]) for d in range(1, cores)
        ]
        both = jnp.stack(both, 0)
        both = jnp.stack(
            [lax.dynamic_index_in_dim(both, (core - c) % cores, 0, keepdims=False) for c in range(cores)], 1
        )
        tables.append(both.transpose(2, 0, 1, 3, 4).reshape(table_rows, order, order))
    table = jnp.concatenate(tables, 0)
    coupling = jnp.stack(
        [
            lax.dynamic_index_in_dim(
                table,
                ((atom - owners[m] // table_rows) % atoms) * table_rows + owners[m] % table_rows,
                0,
                keepdims=False,
            )
            for m in range(MODES)
        ],
        0,
    )
    right = halves(coupling.swapaxes(1, 2))
    out_rows = order // (atoms * cores)
    apart = coupling.reshape(MODES, atoms, cores, out_rows, atoms, brows)
    apart = jnp.take(apart, (core + jnp.arange(cores)) % cores, axis=2)

    def left_of(x):
        high, low = halves(x)
        stacked = jnp.stack([high, high, low], 1)
        return stacked.transpose(2, 0, 1, 3).reshape(x.shape[1], -1)

    near = lax.dynamic_index_in_dim(apart, atom, 4, keepdims=False)
    near = jnp.take(near, (atom + jnp.arange(atoms)) % atoms, axis=1)
    left_near = left_of(near.reshape(MODES, order, brows))
    weights = jnp.stack([1.0 + occupation, occupation], 1).reshape(-1) / momenta

    def ints_of(energy):
        return jnp.concatenate(
            [offsets, jnp.stack([place, core, core * half + energy]).astype(jnp.int32)]
        )

    both_halves = {d: (streams[d], shift(streams[d], "kz", swap)) for d in streams}

    beyond = []
    if line:
        whole = list(own), list(both_halves[0][1])
        for s in range(1, atoms):
            got = shift(own, "atom", [(i, (i + s) % atoms) for i in range(atoms)])
            whole[0].extend(got)
            whole[1].extend(shift(got, "kz", swap))
        far = lax.dynamic_index_in_dim(apart, atom, 1, keepdims=False)
        far = jnp.take(far, (atom - jnp.arange(atoms)) % atoms, axis=3)
        left_far = left_of(far.reshape(MODES, cores * out_rows, order))
        ends = [
            [(a * cores + k, b * cores + (k + t) % cores) for a, b in ((0, n - 1), (n - 1, 0)) for k in range(cores)]
            for t in range(cores)
        ]
        for energy in range(half):
            sums = sandwich(
                ints_of(energy), weights, right, left_far, [whole], grid_total, edev, True, line, out_rows
            )
            beyond.append(sums)
        flat, last = lax.optimization_barrier((beyond, (streams[-REACH], streams[REACH])))
        streams[-REACH], streams[REACH] = last
        both_halves[-REACH] = (streams[-REACH], both_halves[-REACH][1])
        both_halves[REACH] = (streams[REACH], both_halves[REACH][1])
        beyond = [
            [lax.ppermute(flat[e][t], ("energy", "kz"), ends[t]) for t in range(cores)] for e in range(half)
        ]

    groups = [both_halves[d] for d in range(-REACH, REACH + 1)]
    terms = [[[] for _ in range(half)] for _ in range(cores)]
    for energy in range(half):
        sums = sandwich(
            ints_of(energy), weights, right, left_near, groups, grid_total, edev, False, line, out_rows
        )
        for s in range(atoms):
            for t in range(cores):
                block = sums[s * cores + t]
                if s or t:
                    pairs = [
                        (i * cores + k, ((i + s) % atoms) * cores + (k + t) % cores)
                        for i in range(atoms)
                        for k in range(cores)
                    ]
                    block = lax.ppermute(block, ("atom", "kz"), pairs)
                terms[t][energy].append(block)
        for t in range(cores):
            if beyond:
                terms[t][energy].append(beyond[energy][t])
    flat = [x for t in range(cores) for e in range(half) for x in terms[t][e]]
    count = len(terms[0][0])
    step = min(out_rows, 32)
    return pl.pallas_call(
        functools.partial(gather_up, count, half),
        grid=(out_rows // step,),
        out_shape=jax.ShapeDtypeStruct((out_rows, edev, order), jnp.float32),
        in_specs=[pl.BlockSpec(memory_space=pltpu.SMEM)]
        + [pl.BlockSpec((step, order), lambda i: (i, 0))] * len(flat),
        out_specs=pl.BlockSpec((step, edev, order), lambda i: (i, 0, 0)),
        name="gather_up",
    )(ints_of(0), *flat)


def solution(mesh):
    return jax.shard_map(
        shards,
        mesh=mesh,
        in_specs=(P(("grp", "kz"), "energy", "atom", None), P("atom", None, None), P(), P(), P()),
        out_specs=P(("grp", "atom", "kz"), "energy", None),
        check_vma=False,
    )
```

```python
import functools

import jax
import jax.numpy as jnp
from jax import lax
from jax.experimental import pallas as pl
from jax.experimental.pallas import tpu as pltpu
from jax.sharding import PartitionSpec as P

MODES = 3
REACH = 2
PIECES = 2
CHUNKS = 2


def halves(x):
    high = lax.reduce_precision(x, exponent_bits=8, mantissa_bits=7)
    return high.astype(jnp.bfloat16), (x - high).astype(jnp.bfloat16)


def split_dot(n_groups, n_parts, n_atoms, grid_total, edev, far, line, ints, weights, right_high, right_low, left, *refs):
    sources = [
        [refs[(g * 2 + h) * n_parts : (g * 2 + h + 1) * n_parts] for h in range(2)]
        for g in range(n_groups)
    ]
    outs = refs[n_groups * 2 * n_parts : -3]
    planes, inner, sems = refs[-3:]
    count, size = outs[0].shape[:2]
    rows = planes.shape[2]
    half_planes = edev // 2
    place, core, atom, atoms = ints[MODES], ints[MODES + 1], ints[MODES + 2], ints[MODES + 3]
    base, blocks = ints[MODES + 4], grid_total // edev
    target = blocks - 1 - place if far else place

    def source_of(energy, mode, side):
        step = ints[mode] if side == 0 else -ints[mode]
        source = lax.rem(target * edev + base + energy + step + grid_total, grid_total)
        rel = lax.div(source, edev) - place
        if far:
            valid = rel == 0
        elif line:
            valid = jnp.abs(rel) <= REACH
        else:
            rel = lax.rem(rel + REACH + blocks, blocks) - REACH
            valid = rel <= REACH
        group = jnp.where(valid, rel + n_groups // 2, n_groups // 2)
        return valid, group, lax.rem(source, edev)

    def fetch(energy, buffer):
        for mode in range(MODES):
            for side in range(2):
                _, group, plane = source_of(energy, mode, side)
                other = jnp.where(lax.div(plane, half_planes) == core, 0, 1)
                at = lax.rem(plane, half_planes)
                slot = mode * 2 + side
                for g in range(n_groups):
                    for h in range(2):

                        @pl.when((group == g) & (other == h))
                        def _(g=g, h=h, at=at, slot=slot):
                            first = 0
                            for ref in sources[g][h]:
                                depth = ref.shape[1]
                                start = first
                                if far:
                                    per = rows // n_atoms
                                    start = pl.multiple_of(
                                        lax.rem(atom - first // per + atoms, atoms) * per + first % per, 8
                                    )
                                pltpu.make_async_copy(
                                    ref.at[at], planes.at[buffer, slot, pl.ds(start, depth)], sems.at[buffer, slot]
                                ).start()
                                first += depth

    fetch(0, 0)

    @pl.loop(0, count)
    def _(energy):
        buffer = lax.rem(energy, 2)

        @pl.when(energy + 1 < count)
        def _():
            fetch(energy + 1, 1 - buffer)

        dot = functools.partial(jnp.dot, preferred_element_type=jnp.float32)
        for mode in range(MODES):
            scales = []
            for side in range(2):
                slot = mode * 2 + side
                held = planes.at[buffer, slot]
                pltpu.make_async_copy(held, held, sems.at[buffer, slot]).wait()
                scales.append(jnp.where(source_of(energy, mode, side)[0], weights[slot], 0.0))
            combined = scales[0] * planes[buffer, 2 * mode] + scales[1] * planes[buffer, 2 * mode + 1]
            high = combined.astype(jnp.bfloat16)
            low = (combined - high.astype(jnp.float32)).astype(jnp.bfloat16)
            product = dot(high, right_high[mode]) + dot(low, right_high[mode]) + dot(high, right_low[mode])
            high = product.astype(jnp.bfloat16)
            low = (product - high.astype(jnp.float32)).astype(jnp.bfloat16)
            inner[mode, pl.ds(0, rows)] = high
            inner[mode, pl.ds(rows, rows)] = low
            inner[mode, pl.ds(2 * rows, rows)] = high
        for index, out in enumerate(outs):
            s, t = index // 2, index % 2
            block = lax.rem(core + t, 2)
            if not far:
                block = block + 2 * lax.rem(atom + s, atoms)
            where = pl.ds(pl.multiple_of(block * size, 8), size)
            total = dot(left[0, where], inner[0])
            for mode in range(1, MODES):
                total = total + dot(left[mode, where], inner[mode])
            out[energy] = total


def sandwich(ints, weights, right, left, groups, n_atoms, grid_total, edev, far, line, out_rows, count):
    order = right[0].shape[-1]
    flat = [part for group in groups for half in group for part in half]
    rows = sum(part.shape[1] for part in groups[0][0])
    n_out = left.shape[1] // out_rows
    flops = count * 2 * 3 * MODES * (rows * order * order + left.shape[1] * rows * order)
    return pl.pallas_call(
        functools.partial(split_dot, len(groups), len(groups[0][0]), n_atoms, grid_total, edev, far, line),
        out_shape=[jax.ShapeDtypeStruct((count, out_rows, order), jnp.float32)] * n_out,
        in_specs=[pl.BlockSpec(memory_space=pltpu.SMEM)] * 2
        + [pl.BlockSpec(memory_space=pltpu.VMEM)] * 3
        + [pl.BlockSpec(memory_space=pl.ANY)] * len(flat),
        out_specs=[pl.BlockSpec(memory_space=pltpu.VMEM)] * n_out,
        scratch_shapes=[
            pltpu.VMEM((2, 2 * MODES, rows, order), jnp.float32),
            pltpu.VMEM((MODES, 3 * rows, order), jnp.bfloat16),
            pltpu.SemaphoreType.DMA((2, 2 * MODES)),
        ],
        compiler_params=pltpu.CompilerParams(vmem_limit_bytes=40 << 20),
        cost_estimate=pl.CostEstimate(
            flops=flops,
            bytes_accessed=count * 4 * (2 * MODES * rows * order + left.shape[1] * order),
            transcendentals=0,
        ),
        name="far_sandwich" if far else "near_sandwich",
    )(ints, weights, right[0], right[1], left, *flat)


def gather_up(layout, count, ints, *refs):
    out = refs[-1]
    core = ints[MODES + 1]
    for own in range(2):

        @pl.when(core == own)
        def _(own=own):
            at = 0
            for half, chunks in enumerate(layout):
                where = own if half == 0 else 1 - own
                terms = []
                for size in chunks:
                    rows = []
                    for _ in range(size):
                        rows.extend((at, k) for k in range(refs[at].shape[0]))
                        at += 1
                    terms.append(rows)
                for j in range(count):
                    total = None
                    for rows in terms:
                        ref, k = rows[j]
                        total = refs[ref][k] if total is None else total + refs[ref][k]
                    out[:, where * count + j, :] = total


def shards(green, couplings, occupation, offsets, owners):
    momenta_here, edev, brows, order = green.shape
    n, atoms, cores = lax.axis_size("energy"), lax.axis_size("atom"), lax.axis_size("kz")
    momenta = momenta_here * cores
    grid_total = n * edev
    place, atom, core = (lax.axis_index(a) for a in ("energy", "atom", "kz"))
    line = n == 2 * REACH
    half = edev // cores
    swap = [(i, (i + 1) % cores) for i in range(cores)]
    around = [[(i, (i + s) % atoms) for i in range(atoms)] for s in range(atoms)]

    def shift(arrays, axis, pairs):
        return [lax.ppermute(a, axis, pairs) for a in arrays]

    size = brows // PIECES

    def summed(owner, piece):
        held = lax.dynamic_slice(
            green, (0, owner * half, piece * size, 0), (momenta_here, half, size, order)
        )
        return jnp.sum(held, axis=0)

    sent = shift([summed((core + 1) % cores, piece) for piece in range(PIECES)], "kz", swap)
    own = [summed(core, piece) + sent[piece] for piece in range(PIECES)]

    if line:
        up = [[(i, i + 1) for i in range(d, n - 1)] for d in range(REACH)]
        down = [[(i, i - 1) for i in range(n - 1 - d, 0, -1)] for d in range(REACH)]
    else:
        up = [[(i, (i + 1) % n) for i in range(n)]] * REACH
        down = [[(i, (i - 1) % n) for i in range(n)]] * REACH
    streams = {0: own}
    for d in range(1, REACH + 1):
        with jax.named_scope(f"hop{d}"):
            streams[-d], streams[d] = [], []
            for piece in range(PIECES):
                streams[-d].append(lax.ppermute(streams[1 - d][piece], "energy", up[d - 1]))
                streams[d].append(lax.ppermute(streams[d - 1][piece], "energy", down[d - 1]))

    table_rows = couplings.shape[0]
    strip = order // cores
    couplings, ready = lax.optimization_barrier((couplings, own))
    mine = lax.dynamic_slice(couplings, (0, core * strip, 0), (table_rows, strip, order))
    others = []
    with jax.named_scope("table"):
        for s in range(1, atoms):
            got = lax.ppermute(mine, "atom", around[s])
            others.append((got, lax.ppermute(got, "kz", swap)))

    def pick(m):
        row = owners[m] % table_rows
        behind = (atom - owners[m] // table_rows) % atoms
        value = lax.dynamic_index_in_dim(couplings, row, 0, keepdims=False)
        for s, (got, other) in enumerate(others, 1):
            got = lax.dynamic_index_in_dim(got, row, 0, keepdims=False)
            other = lax.dynamic_index_in_dim(other, row, 0, keepdims=False)
            first, second = jnp.where(core == 0, got, other), jnp.where(core == 0, other, got)
            value = jnp.where(behind == s, jnp.concatenate([first, second], 0), value)
        return value

    coupling = jnp.stack([pick(m) for m in range(MODES)], 0)
    right = halves(coupling.swapaxes(1, 2))
    out_rows = order // (atoms * cores)

    def left_of(x):
        high, low = halves(x)
        return jnp.concatenate([high, high, low], 2)

    left_near = left_of(lax.dynamic_slice(coupling, (0, 0, atom * brows), (MODES, order, brows)))
    weights = jnp.stack([1.0 + occupation, occupation], 1).reshape(-1) / momenta

    def ints_of(energy):
        return jnp.concatenate(
            [offsets, jnp.stack([place, core, atom, jnp.int32(atoms), core * half + energy]).astype(jnp.int32)]
        )

    with jax.named_scope("pair"):
        both_halves = {d: (streams[d], shift(streams[d], "kz", swap)) for d in (0, -1, 1)}

    beyond = []
    if line:
        with jax.named_scope("rows"):
            whole = list(own), list(both_halves[0][1])
            for s in range(1, atoms):
                got = shift(own, "atom", around[s])
                whole[0].extend(got)
                whole[1].extend(shift(got, "kz", swap))
        left_far = left_of(lax.dynamic_slice(coupling, (0, atom * cores * out_rows, 0), (MODES, cores * out_rows, order)))
        sums = sandwich(
            ints_of(0), weights, right, left_far, [whole], atoms, grid_total, edev, True, line, out_rows, half
        )
        sums, streams[-REACH], streams[REACH] = lax.optimization_barrier((sums, streams[-REACH], streams[REACH]))
        with jax.named_scope("ends"):
            for t in range(cores):
                pairs = [
                    (a * cores + k, b * cores + (k + t) % cores)
                    for a, b in ((0, n - 1), (n - 1, 0))
                    for k in range(cores)
                ]
                beyond.append(lax.ppermute(sums[t], ("energy", "kz"), pairs))
    with jax.named_scope("pair"):
        for d in (-REACH, REACH):
            both_halves[d] = (streams[d], shift(streams[d], "kz", swap))

    groups = [both_halves[d] for d in range(-REACH, REACH + 1)]
    count = half // CHUNKS
    terms = [[[] for _ in range(atoms)] for _ in range(cores)]
    for chunk in range(CHUNKS):
        sums = sandwich(
            ints_of(chunk * count), weights, right, left_near, groups, atoms, grid_total, edev, False, line, out_rows, count
        )
        with jax.named_scope("sums"):
            for s in range(atoms - 1, -1, -1):
                for t in range(cores):
                    block = sums[s * cores + t]
                    if s or t:
                        pairs = [
                            (i * cores + k, ((i + s) % atoms) * cores + (k + t) % cores)
                            for i in range(atoms)
                            for k in range(cores)
                        ]
                        block = lax.ppermute(block, ("atom", "kz"), pairs)
                    terms[t][s].append(block)
    for t in range(cores):
        if beyond:
            terms[t].append([beyond[t]])
    flat = [x for t in range(cores) for term in terms[t] for x in term]
    layout = [[len(term) for term in terms[t]] for t in range(cores)]
    step = min(out_rows, 32)
    return pl.pallas_call(
        functools.partial(gather_up, layout, half),
        grid=(out_rows // step,),
        out_shape=jax.ShapeDtypeStruct((out_rows, edev, order), jnp.float32),
        in_specs=[pl.BlockSpec(memory_space=pltpu.SMEM)]
        + [pl.BlockSpec((x.shape[0], step, order), lambda i: (0, i, 0)) for x in flat],
        out_specs=pl.BlockSpec((step, edev, order), lambda i: (i, 0, 0)),
        name="gather_up",
    )(ints_of(0), *flat)


def solution(mesh):
    return jax.shard_map(
        shards,
        mesh=mesh,
        in_specs=(P(("grp", "kz"), "energy", "atom", None), P("atom", None, None), P(), P(), P()),
        out_specs=P(("grp", "atom", "kz"), "energy", None),
        check_vma=False,
    )
```

```python
import functools

import jax
import jax.numpy as jnp
from jax import lax
from jax.experimental import pallas as pl
from jax.experimental.pallas import tpu as pltpu
from jax.sharding import PartitionSpec as P


MODES = 3
REACH = 2
PIECES = 2


def chunks_of(half):
    return [1, 1, half - 2] if half > 2 else [1] * half


def halves(x):
    high = lax.reduce_precision(x, exponent_bits=8, mantissa_bits=7)
    return high.astype(jnp.bfloat16), (x - high).astype(jnp.bfloat16)


def add_momenta(where, green, *refs):
    out = refs[-1]
    total = green[0, 0]
    for k in range(1, green.shape[0]):
        total = total + green[k, 0]
    for ref in refs[:-1]:
        total = total + ref[0]
    out[0] = total


def split_dot(n_groups, n_parts, n_atoms, momenta, base, grid_total, edev, far, line, steps, occupation, right_high, right_low, left, *refs):
    sources = [
        [refs[(g * 2 + h) * n_parts : (g * 2 + h + 1) * n_parts] for h in range(2)]
        for g in range(n_groups)
    ]
    outs = refs[n_groups * 2 * n_parts : -3]
    planes, inner, sems = refs[-3:]
    count, size = outs[0].shape[:2]
    rows = planes.shape[2]
    half_planes = edev // 2
    place, core, atom = (lax.axis_index(a) for a in ("energy", "kz", "atom"))
    blocks = grid_total // edev
    target = blocks - 1 - place if far else place
    base = base + core * half_planes

    def source_of(energy, mode, side):
        step = steps[mode] if side == 0 else -steps[mode]
        source = lax.rem(target * edev + base + energy + step + grid_total, grid_total)
        rel = lax.div(source, edev) - place
        if far:
            valid = rel == 0
        elif line:
            valid = jnp.abs(rel) <= REACH
        else:
            rel = lax.rem(rel + REACH + blocks, blocks) - REACH
            valid = rel <= REACH
        group = jnp.where(valid, rel + n_groups // 2, n_groups // 2)
        return valid, group, lax.rem(source, edev)

    def fetch(energy, buffer):
        for mode in range(MODES):
            for side in range(2):
                _, group, plane = source_of(energy, mode, side)
                other = jnp.where(lax.div(plane, half_planes) == core, 0, 1)
                at = lax.rem(plane, half_planes)
                slot = mode * 2 + side
                for g in range(n_groups):
                    for h in range(2):

                        @pl.when((group == g) & (other == h))
                        def _(g=g, h=h, at=at, slot=slot):
                            first = 0
                            for ref in sources[g][h]:
                                depth = ref.shape[1]
                                start = first
                                if far:
                                    per = rows // n_atoms
                                    start = pl.multiple_of(
                                        lax.rem(atom - first // per + n_atoms, n_atoms) * per + first % per, 8
                                    )
                                pltpu.make_async_copy(
                                    ref.at[at], planes.at[buffer, slot, pl.ds(start, depth)], sems.at[buffer, slot]
                                ).start()
                                first += depth

    fetch(0, 0)

    @pl.loop(0, count)
    def _(energy):
        buffer = lax.rem(energy, 2)

        @pl.when(energy + 1 < count)
        def _():
            fetch(energy + 1, 1 - buffer)

        dot = functools.partial(jnp.dot, preferred_element_type=jnp.float32)
        for mode in range(MODES):
            scales = []
            for side in range(2):
                slot = mode * 2 + side
                held = planes.at[buffer, slot]
                pltpu.make_async_copy(held, held, sems.at[buffer, slot]).wait()
                scales.append(jnp.where(source_of(energy, mode, side)[0], (occupation[mode] + (1.0 - side)) * (1.0 / momenta), 0.0))
            combined = scales[0] * planes[buffer, 2 * mode] + scales[1] * planes[buffer, 2 * mode + 1]
            high = combined.astype(jnp.bfloat16)
            low = (combined - high.astype(jnp.float32)).astype(jnp.bfloat16)
            product = dot(high, right_high[mode]) + dot(low, right_high[mode]) + dot(high, right_low[mode])
            high = product.astype(jnp.bfloat16)
            low = (product - high.astype(jnp.float32)).astype(jnp.bfloat16)
            inner[mode, pl.ds(0, rows)] = high
            inner[mode, pl.ds(rows, rows)] = low
            inner[mode, pl.ds(2 * rows, rows)] = high
        for index, out in enumerate(outs):
            s, t = index // 2, index % 2
            block = lax.rem(core + t, 2)
            if not far:
                block = block + 2 * lax.rem(atom + s, n_atoms)
            where = pl.ds(pl.multiple_of(block * size, 8), size)
            total = dot(left[0, where], inner[0])
            for mode in range(1, MODES):
                total = total + dot(left[mode, where], inner[mode])
            out[energy] = total


def sandwich(steps, occupation, right, left, groups, n_atoms, momenta, base, grid_total, edev, far, line, out_rows, count):
    order = right[0].shape[-1]
    flat = [part for group in groups for half in group for part in half]
    rows = sum(part.shape[1] for part in groups[0][0])
    n_out = left.shape[1] // out_rows
    flops = count * 2 * 3 * MODES * (rows * order * order + left.shape[1] * rows * order)
    return pl.pallas_call(
        functools.partial(split_dot, len(groups), len(groups[0][0]), n_atoms, momenta, base, grid_total, edev, far, line),
        out_shape=[jax.ShapeDtypeStruct((count, out_rows, order), jnp.float32)] * n_out,
        in_specs=[pl.BlockSpec(memory_space=pltpu.SMEM)] * 2
        + [pl.BlockSpec(memory_space=pltpu.VMEM)] * 3
        + [pl.BlockSpec(memory_space=pl.ANY)] * len(flat),
        out_specs=[pl.BlockSpec(memory_space=pltpu.VMEM)] * n_out,
        scratch_shapes=[
            pltpu.VMEM((2, 2 * MODES, rows, order), jnp.float32),
            pltpu.VMEM((MODES, 3 * rows, order), jnp.bfloat16),
            pltpu.SemaphoreType.DMA((2, 2 * MODES)),
        ],
        compiler_params=pltpu.CompilerParams(vmem_limit_bytes=40 << 20),
        cost_estimate=pl.CostEstimate(
            flops=flops,
            bytes_accessed=count * 4 * (2 * MODES * rows * order + left.shape[1] * order),
            transcendentals=0,
        ),
        name="far_sandwich" if far else "near_sandwich",
    )(steps, occupation, right[0], right[1], left, *flat)


def gather_up(layout, count, *refs):
    out = refs[-1]
    core = lax.axis_index("kz")
    for own in range(2):

        @pl.when(core == own)
        def _(own=own):
            at = 0
            for half, chunks in enumerate(layout):
                where = own if half == 0 else 1 - own
                terms = []
                for size in chunks:
                    rows = []
                    for _ in range(size):
                        rows.extend((at, k) for k in range(refs[at].shape[0]))
                        at += 1
                    terms.append(rows)
                for j in range(count):
                    total = None
                    for rows in terms:
                        ref, k = rows[j]
                        total = refs[ref][k] if total is None else total + refs[ref][k]
                    out[:, where * count + j, :] = total


def shards(green, couplings, occupation, offsets, owners):
    momenta_here, edev, brows, order = green.shape
    n, atoms, cores = lax.axis_size("energy"), lax.axis_size("atom"), lax.axis_size("kz")
    momenta = momenta_here * cores
    grid_total = n * edev
    _, atom, core = (lax.axis_index(a) for a in ("energy", "atom", "kz"))
    line = n == 2 * REACH
    half = edev // cores
    swap = [(i, (i + 1) % cores) for i in range(cores)]
    around = [[(i, (i + s) % atoms) for i in range(atoms)] for s in range(atoms)]

    size = brows // PIECES

    def summed(theirs, piece, *more):
        def first(e, where):
            return 0, where[0] * half + e, piece, 0

        where = ((core + 1) % cores if theirs else core).reshape(1)
        spec = pl.BlockSpec((1, size, order), lambda e, where: (e, 0, 0))
        return pl.pallas_call(
            add_momenta,
            out_shape=jax.ShapeDtypeStruct((half, size, order), jnp.float32),
            grid_spec=pltpu.PrefetchScalarGridSpec(
                num_scalar_prefetch=1,
                grid=(half,),
                in_specs=[pl.BlockSpec((momenta_here, 1, size, order), first)] + [spec] * len(more),
                out_specs=spec,
            ),
            cost_estimate=pl.CostEstimate(
                flops=momenta_here * half * size * order,
                bytes_accessed=4 * (momenta_here + 1 + len(more)) * half * size * order,
                transcendentals=0,
            ),
            name="add_momenta",
        )(where, green, *more)

    own = []
    for piece in range(PIECES):
        given = summed(True, piece)
        given = lax.ppermute(given, "kz", swap)
        own.append(summed(False, piece, given))

    if line:
        up = [[(i, i + 1) for i in range(d, n - 1)] for d in range(REACH)]
        down = [[(i, i - 1) for i in range(n - 1 - d, 0, -1)] for d in range(REACH)]
    else:
        up = [[(i, (i + 1) % n) for i in range(n)]] * REACH
        down = [[(i, (i - 1) % n) for i in range(n)]] * REACH
    streams = {0: own}
    for d in range(1, REACH + 1):
        streams[-d] = [lax.ppermute(x, "energy", up[d - 1]) for x in streams[1 - d]]
        streams[d] = [lax.ppermute(x, "energy", down[d - 1]) for x in streams[d - 1]]
    groups = [(streams[d], [lax.ppermute(x, "kz", swap) for x in streams[d]]) for d in range(-REACH, REACH + 1)]

    table_rows = couplings.shape[0]
    strip = order // cores
    mine = lax.dynamic_slice(couplings, (0, core * strip, 0), (table_rows, strip, order))
    others = []
    for s in range(1, atoms):
        got = lax.ppermute(mine, "atom", around[s])
        others.append((got, lax.ppermute(got, "kz", swap)))
    rows_of = lax.rem(owners, jnp.int32(table_rows))
    behind_of = lax.rem(atom - lax.div(owners, jnp.int32(table_rows)) + atoms, jnp.int32(atoms))

    def pick(m):
        row, behind = rows_of[m], behind_of[m]

        def at(table):
            return lax.dynamic_slice(table, (row, 0, 0), (1,) + table.shape[1:])[0]

        value = at(couplings)
        for s, (got, other) in enumerate(others, 1):
            first = jnp.where(core == 0, at(got), at(other))
            second = jnp.where(core == 0, at(other), at(got))
            value = jnp.where(behind == s, jnp.concatenate([first, second], 0), value)
        return value

    coupling = jnp.stack([pick(m) for m in range(MODES)], 0)
    right = halves(coupling.swapaxes(1, 2))
    out_rows = order // (atoms * cores)

    def left_of(x):
        high, low = halves(x)
        return jnp.concatenate([high, high, low], 2)

    left_near = left_of(lax.dynamic_slice(coupling, (0, 0, atom * brows), (MODES, order, brows)))

    beyond = []
    if line:
        left_far = left_of(lax.dynamic_slice(coupling, (0, atom * cores * out_rows, 0), (MODES, cores * out_rows, order)))
        got = [lax.ppermute(x, "atom", around[s]) for s in range(1, atoms) for x in own]
        got, right, left_far, left_near = lax.optimization_barrier((got, right, left_far, left_near))
        whole = (
            list(own) + got,
            groups[REACH][1] + [lax.ppermute(x, "kz", swap) for x in got],
        )
        sums = sandwich(
            offsets, occupation, right, left_far, [whole], atoms, momenta, 0, grid_total, edev, True, line, out_rows, half
        )
        for t in range(cores):
            pairs = [
                (a * cores + k, b * cores + (k + t) % cores)
                for a, b in ((0, n - 1), (n - 1, 0))
                for k in range(cores)
            ]
            beyond.append(lax.ppermute(sums[t], ("energy", "kz"), pairs))

    terms = [[[] for _ in range(atoms)] for _ in range(cores)]
    base = 0
    for count in chunks_of(half):
        sums = sandwich(
            offsets, occupation, right, left_near, groups, atoms, momenta, base, grid_total, edev, False, line, out_rows, count
        )
        base += count
        for s in range(atoms - 1, -1, -1):
            for t in range(cores):
                block = sums[s * cores + t]
                if s or t:
                    pairs = [
                        (i * cores + k, ((i + s) % atoms) * cores + (k + t) % cores)
                        for i in range(atoms)
                        for k in range(cores)
                    ]
                    block = lax.ppermute(block, ("atom", "kz"), pairs)
                terms[t][s].append(block)
    for t in range(cores):
        if beyond:
            terms[t].append([beyond[t]])
    flat = [x for t in range(cores) for term in terms[t] for x in term]
    layout = [[len(term) for term in terms[t]] for t in range(cores)]
    step = min(out_rows, 32)
    return pl.pallas_call(
        functools.partial(gather_up, layout, half),
        grid=(out_rows // step,),
        out_shape=jax.ShapeDtypeStruct((out_rows, edev, order), jnp.float32),
        in_specs=[pl.BlockSpec((x.shape[0], step, order), lambda i: (0, i, 0)) for x in flat],
        out_specs=pl.BlockSpec((step, edev, order), lambda i: (i, 0, 0)),
        name="gather_up",
    )(*flat)


def solution(mesh):
    return jax.shard_map(
        shards,
        mesh=mesh,
        in_specs=(P(("grp", "kz"), "energy", "atom", None), P("atom", None, None), P(), P(), P()),
        out_specs=P(("grp", "atom", "kz"), "energy", None),
        check_vma=False,
    )
```

```python
import functools

import jax
import jax.numpy as jnp
from jax import lax
from jax.experimental import pallas as pl
from jax.experimental.pallas import tpu as pltpu
from jax.sharding import PartitionSpec as P


MODES = 3
REACH = 2
PIECES = 2


def chunks_of(half):
    return [1, 1, half - 2] if half > 2 else [1] * half


def halves(x):
    high = lax.reduce_precision(x, exponent_bits=8, mantissa_bits=7)
    return high.astype(jnp.bfloat16), (x - high).astype(jnp.bfloat16)


def add_momenta(theirs, first, green, *refs):
    out, held, total, arrived, left = refs[-5:]
    given = refs[:-5]
    momenta, count, size = green.shape[0], held.shape[0], held.shape[2]
    core = lax.axis_index("kz")
    base = (1 - core if theirs else core) * count
    for e in range(count):
        for k in range(momenta):
            pltpu.make_async_copy(green.at[k, base + e, pl.ds(first, size)], held.at[e, k], arrived.at[e]).start()
        for ref in given:
            pltpu.make_async_copy(ref.at[e], held.at[e, momenta], arrived.at[e]).start()
    for e in range(count):
        pltpu.make_async_copy(held.at[e], held.at[e], arrived.at[e]).wait()
        value = held[e, 0]
        for k in range(1, held.shape[1]):
            value = value + held[e, k]
        total[e] = value
        pltpu.make_async_copy(total.at[e], out.at[e], left.at[e]).start()
    for e in range(count):
        pltpu.make_async_copy(total.at[e], out.at[e], left.at[e]).wait()


def split_dot(n_groups, n_parts, n_atoms, momenta, base, grid_total, edev, far, line, steps, occupation, right_high, right_low, left, *refs):
    sources = [
        [refs[(g * 2 + h) * n_parts : (g * 2 + h + 1) * n_parts] for h in range(2)]
        for g in range(n_groups)
    ]
    outs = refs[n_groups * 2 * n_parts : -3]
    planes, inner, sems = refs[-3:]
    count, size = outs[0].shape[:2]
    rows = planes.shape[2]
    half_planes = edev // 2
    place, core, atom = (lax.axis_index(a) for a in ("energy", "kz", "atom"))
    blocks = grid_total // edev
    target = blocks - 1 - place if far else place
    base = base + core * half_planes

    def source_of(energy, mode, side):
        step = steps[mode] if side == 0 else -steps[mode]
        source = lax.rem(target * edev + base + energy + step + grid_total, grid_total)
        rel = lax.div(source, edev) - place
        if far:
            valid = rel == 0
        elif line:
            valid = jnp.abs(rel) <= REACH
        else:
            rel = lax.rem(rel + REACH + blocks, blocks) - REACH
            valid = rel <= REACH
        group = jnp.where(valid, rel + n_groups // 2, n_groups // 2)
        return valid, group, lax.rem(source, edev)

    def fetch(energy, buffer):
        for mode in range(MODES):
            for side in range(2):
                _, group, plane = source_of(energy, mode, side)
                other = jnp.where(lax.div(plane, half_planes) == core, 0, 1)
                at = lax.rem(plane, half_planes)
                slot = mode * 2 + side
                for g in range(n_groups):
                    for h in range(2):

                        @pl.when((group == g) & (other == h))
                        def _(g=g, h=h, at=at, slot=slot):
                            first = 0
                            for ref in sources[g][h]:
                                depth = ref.shape[1]
                                start = first
                                if far:
                                    per = rows // n_atoms
                                    start = pl.multiple_of(
                                        lax.rem(atom - first // per + n_atoms, n_atoms) * per + first % per, 8
                                    )
                                pltpu.make_async_copy(
                                    ref.at[at], planes.at[buffer, slot, pl.ds(start, depth)], sems.at[buffer, slot]
                                ).start()
                                first += depth

    fetch(0, 0)

    @pl.loop(0, count)
    def _(energy):
        buffer = lax.rem(energy, 2)

        @pl.when(energy + 1 < count)
        def _():
            fetch(energy + 1, 1 - buffer)

        dot = functools.partial(jnp.dot, preferred_element_type=jnp.float32)
        for mode in range(MODES):
            scales = []
            for side in range(2):
                slot = mode * 2 + side
                held = planes.at[buffer, slot]
                pltpu.make_async_copy(held, held, sems.at[buffer, slot]).wait()
                scales.append(jnp.where(source_of(energy, mode, side)[0], (occupation[mode] + (1.0 - side)) * (1.0 / momenta), 0.0))
            combined = scales[0] * planes[buffer, 2 * mode] + scales[1] * planes[buffer, 2 * mode + 1]
            high = combined.astype(jnp.bfloat16)
            low = (combined - high.astype(jnp.float32)).astype(jnp.bfloat16)
            product = dot(high, right_high[mode]) + dot(low, right_high[mode]) + dot(high, right_low[mode])
            high = product.astype(jnp.bfloat16)
            low = (product - high.astype(jnp.float32)).astype(jnp.bfloat16)
            inner[mode, pl.ds(0, rows)] = high
            inner[mode, pl.ds(rows, rows)] = low
            inner[mode, pl.ds(2 * rows, rows)] = high
        for index, out in enumerate(outs):
            s, t = index // 2, index % 2
            block = lax.rem(core + t, 2)
            if not far:
                block = block + 2 * lax.rem(atom + s, n_atoms)
            where = pl.ds(pl.multiple_of(block * size, 8), size)
            total = dot(left[0, where], inner[0])
            for mode in range(1, MODES):
                total = total + dot(left[mode, where], inner[mode])
            out[energy] = total


def sandwich(steps, occupation, right, left, groups, n_atoms, momenta, base, grid_total, edev, far, line, out_rows, count):
    order = right[0].shape[-1]
    flat = [part for group in groups for half in group for part in half]
    rows = sum(part.shape[1] for part in groups[0][0])
    n_out = left.shape[1] // out_rows
    flops = count * 2 * 3 * MODES * (rows * order * order + left.shape[1] * rows * order)
    return pl.pallas_call(
        functools.partial(split_dot, len(groups), len(groups[0][0]), n_atoms, momenta, base, grid_total, edev, far, line),
        out_shape=[jax.ShapeDtypeStruct((count, out_rows, order), jnp.float32)] * n_out,
        in_specs=[pl.BlockSpec(memory_space=pltpu.SMEM)] * 2
        + [pl.BlockSpec(memory_space=pltpu.VMEM)] * 3
        + [pl.BlockSpec(memory_space=pl.ANY)] * len(flat),
        out_specs=[pl.BlockSpec(memory_space=pltpu.VMEM)] * n_out,
        scratch_shapes=[
            pltpu.VMEM((2, 2 * MODES, rows, order), jnp.float32),
            pltpu.VMEM((MODES, 3 * rows, order), jnp.bfloat16),
            pltpu.SemaphoreType.DMA((2, 2 * MODES)),
        ],
        compiler_params=pltpu.CompilerParams(vmem_limit_bytes=40 << 20),
        cost_estimate=pl.CostEstimate(
            flops=flops,
            bytes_accessed=count * 4 * (2 * MODES * rows * order + left.shape[1] * order),
            transcendentals=0,
        ),
        name="far_sandwich" if far else "near_sandwich",
    )(steps, occupation, right[0], right[1], left, *flat)


def gather_up(layout, count, *refs):
    out = refs[-1]
    core = lax.axis_index("kz")
    for own in range(2):

        @pl.when(core == own)
        def _(own=own):
            at = 0
            for half, chunks in enumerate(layout):
                where = own if half == 0 else 1 - own
                terms = []
                for size in chunks:
                    rows = []
                    for _ in range(size):
                        rows.extend((at, k) for k in range(refs[at].shape[0]))
                        at += 1
                    terms.append(rows)
                for j in range(count):
                    total = None
                    for rows in terms:
                        ref, k = rows[j]
                        total = refs[ref][k] if total is None else total + refs[ref][k]
                    out[:, where * count + j, :] = total


def shards(green, couplings, occupation, offsets, owners):
    momenta_here, edev, brows, order = green.shape
    n, atoms, cores = lax.axis_size("energy"), lax.axis_size("atom"), lax.axis_size("kz")
    momenta = momenta_here * cores
    grid_total = n * edev
    _, atom, core = (lax.axis_index(a) for a in ("energy", "atom", "kz"))
    line = n == 2 * REACH
    half = edev // cores
    swap = [(i, (i + 1) % cores) for i in range(cores)]
    around = [[(i, (i + s) % atoms) for i in range(atoms)] for s in range(atoms)]

    size = brows // PIECES

    def summed(theirs, piece, *more):
        return pl.pallas_call(
            functools.partial(add_momenta, theirs, piece * size),
            out_shape=jax.ShapeDtypeStruct((half, size, order), jnp.float32),
            in_specs=[pl.BlockSpec(memory_space=pl.ANY)] * (1 + len(more)),
            out_specs=pl.BlockSpec(memory_space=pl.ANY),
            scratch_shapes=[
                pltpu.VMEM((half, momenta_here + len(more), size, order), jnp.float32),
                pltpu.VMEM((half, size, order), jnp.float32),
                pltpu.SemaphoreType.DMA((half,)),
                pltpu.SemaphoreType.DMA((half,)),
            ],
            cost_estimate=pl.CostEstimate(
                flops=momenta_here * half * size * order,
                bytes_accessed=4 * (momenta_here + 1 + len(more)) * half * size * order,
                transcendentals=0,
            ),
            name="add_momenta",
        )(green, *more)

    own = []
    for piece in range(PIECES):
        given = summed(True, piece)
        given = lax.ppermute(given, "kz", swap)
        own.append(summed(False, piece, given))

    if line:
        up = [[(i, i + 1) for i in range(d, n - 1)] for d in range(REACH)]
        down = [[(i, i - 1) for i in range(n - 1 - d, 0, -1)] for d in range(REACH)]
    else:
        up = [[(i, (i + 1) % n) for i in range(n)]] * REACH
        down = [[(i, (i - 1) % n) for i in range(n)]] * REACH
    streams = {0: own}
    for d in range(1, REACH + 1):
        streams[-d] = [lax.ppermute(x, "energy", up[d - 1]) for x in streams[1 - d]]
        streams[d] = [lax.ppermute(x, "energy", down[d - 1]) for x in streams[d - 1]]
    groups = [(streams[d], [lax.ppermute(x, "kz", swap) for x in streams[d]]) for d in range(-REACH, REACH + 1)]

    table_rows = couplings.shape[0]
    strip = order // cores
    mine = lax.dynamic_slice(couplings, (0, core * strip, 0), (table_rows, strip, order))
    others = []
    for s in range(1, atoms):
        got = lax.ppermute(mine, "atom", around[s])
        others.append((got, lax.ppermute(got, "kz", swap)))
    rows_of = lax.rem(owners, jnp.int32(table_rows))
    behind_of = lax.rem(atom - lax.div(owners, jnp.int32(table_rows)) + atoms, jnp.int32(atoms))

    def pick(m):
        row, behind = rows_of[m], behind_of[m]

        def at(table):
            return lax.dynamic_slice(table, (row, 0, 0), (1,) + table.shape[1:])[0]

        value = at(couplings)
        for s, (got, other) in enumerate(others, 1):
            first = jnp.where(core == 0, at(got), at(other))
            second = jnp.where(core == 0, at(other), at(got))
            value = jnp.where(behind == s, jnp.concatenate([first, second], 0), value)
        return value

    coupling = jnp.stack([pick(m) for m in range(MODES)], 0)
    right = halves(coupling.swapaxes(1, 2))
    out_rows = order // (atoms * cores)

    def left_of(x):
        high, low = halves(x)
        return jnp.concatenate([high, high, low], 2)

    left_near = left_of(lax.dynamic_slice(coupling, (0, 0, atom * brows), (MODES, order, brows)))

    beyond = []
    if line:
        left_far = left_of(
            lax.dynamic_slice(coupling, (0, atom * cores * out_rows, 0), (MODES, cores * out_rows, order))
        )
        got = [lax.ppermute(x, "atom", around[s]) for s in range(1, atoms) for x in own]
        got, right, left_far, left_near = lax.optimization_barrier((got, right, left_far, left_near))
        whole = (
            list(own) + got,
            groups[REACH][1] + [lax.ppermute(x, "kz", swap) for x in got],
        )
        sums = sandwich(
            offsets, occupation, right, left_far, [whole], atoms, momenta, 0, grid_total, edev, True, line, out_rows, half
        )
        for t in range(cores):
            pairs = [
                (a * cores + k, b * cores + (k + t) % cores)
                for a, b in ((0, n - 1), (n - 1, 0))
                for k in range(cores)
            ]
            beyond.append(lax.ppermute(sums[t], ("energy", "kz"), pairs))

    terms = [[[] for _ in range(atoms)] for _ in range(cores)]
    base = 0
    for count in chunks_of(half):
        sums = sandwich(
            offsets, occupation, right, left_near, groups, atoms, momenta, base, grid_total, edev, False, line, out_rows, count
        )
        base += count
        for s in range(atoms - 1, -1, -1):
            for t in range(cores):
                block = sums[s * cores + t]
                if s or t:
                    pairs = [
                        (i * cores + k, ((i + s) % atoms) * cores + (k + t) % cores)
                        for i in range(atoms)
                        for k in range(cores)
                    ]
                    block = lax.ppermute(block, ("atom", "kz"), pairs)
                terms[t][s].append(block)
    for t in range(cores):
        if beyond:
            terms[t].append([beyond[t]])
    flat = [x for t in range(cores) for term in terms[t] for x in term]
    layout = [[len(term) for term in terms[t]] for t in range(cores)]
    step = min(out_rows, 32)
    return pl.pallas_call(
        functools.partial(gather_up, layout, half),
        grid=(out_rows // step,),
        out_shape=jax.ShapeDtypeStruct((out_rows, edev, order), jnp.float32),
        in_specs=[pl.BlockSpec((x.shape[0], step, order), lambda i: (0, i, 0)) for x in flat],
        out_specs=pl.BlockSpec((step, edev, order), lambda i: (i, 0, 0)),
        name="gather_up",
    )(*flat)


def solution(mesh):
    return jax.shard_map(
        shards,
        mesh=mesh,
        in_specs=(P(("grp", "kz"), "energy", "atom", None), P("atom", None, None), P(), P(), P()),
        out_specs=P(("grp", "atom", "kz"), "energy", None),
        check_vma=False,
    )
```

```python
import functools

import jax
import jax.numpy as jnp
from jax import lax
from jax.experimental import pallas as pl
from jax.experimental.pallas import tpu as pltpu
from jax.sharding import PartitionSpec as P


MODES = 3
REACH = 2
PIECES = 2


def chunks_of(half):
    return [1, 1, half - 2] if half > 2 else [1] * half


def halves(x):
    high = lax.reduce_precision(x, exponent_bits=8, mantissa_bits=7)
    return high.astype(jnp.bfloat16), (x - high).astype(jnp.bfloat16)


def add_momenta(theirs, first, green, *refs):
    out, held, total, arrived, left = refs[-5:]
    given = refs[:-5]
    momenta, count, size = green.shape[0], held.shape[0], held.shape[2]
    core = lax.axis_index("kz")
    base = (1 - core if theirs else core) * count
    for e in range(count):
        for k in range(momenta):
            pltpu.make_async_copy(green.at[k, base + e, pl.ds(first, size)], held.at[e, k], arrived.at[e]).start()
        for ref in given:
            pltpu.make_async_copy(ref.at[e], held.at[e, momenta], arrived.at[e]).start()
    for e in range(count):
        pltpu.make_async_copy(held.at[e], held.at[e], arrived.at[e]).wait()
        value = held[e, 0]
        for k in range(1, held.shape[1]):
            value = value + held[e, k]
        total[e] = value
        pltpu.make_async_copy(total.at[e], out.at[e], left.at[e]).start()
    for e in range(count):
        pltpu.make_async_copy(total.at[e], out.at[e], left.at[e]).wait()


def split_dot(n_groups, n_parts, n_atoms, momenta, base, grid_total, edev, far, line, steps, occupation, right_high, right_low, left, *refs):
    sources = [
        [refs[(g * 2 + h) * n_parts : (g * 2 + h + 1) * n_parts] for h in range(2)]
        for g in range(n_groups)
    ]
    outs = refs[n_groups * 2 * n_parts : -3]
    planes, inner, sems = refs[-3:]
    count, size = outs[0].shape[:2]
    rows = planes.shape[2]
    half_planes = edev // 2
    place, core, atom = (lax.axis_index(a) for a in ("energy", "kz", "atom"))
    blocks = grid_total // edev
    target = blocks - 1 - place if far else place
    base = base + core * half_planes

    def source_of(energy, mode, side):
        step = steps[mode] if side == 0 else -steps[mode]
        source = lax.rem(target * edev + base + energy + step + grid_total, grid_total)
        rel = lax.div(source, edev) - place
        if far:
            valid = rel == 0
        elif line:
            valid = jnp.abs(rel) <= REACH
        else:
            rel = lax.rem(rel + REACH + blocks, blocks) - REACH
            valid = rel <= REACH
        group = jnp.where(valid, rel + n_groups // 2, n_groups // 2)
        return valid, group, lax.rem(source, edev)

    def fetch(energy, buffer):
        for mode in range(MODES):
            for side in range(2):
                _, group, plane = source_of(energy, mode, side)
                other = jnp.where(lax.div(plane, half_planes) == core, 0, 1)
                at = lax.rem(plane, half_planes)
                slot = mode * 2 + side
                for g in range(n_groups):
                    for h in range(2):

                        @pl.when((group == g) & (other == h))
                        def _(g=g, h=h, at=at, slot=slot):
                            first = 0
                            for ref in sources[g][h]:
                                depth = ref.shape[1]
                                start = first
                                if far:
                                    per = rows // n_atoms
                                    start = pl.multiple_of(
                                        lax.rem(atom - first // per + n_atoms, n_atoms) * per + first % per, 8
                                    )
                                pltpu.make_async_copy(
                                    ref.at[at], planes.at[buffer, slot, pl.ds(start, depth)], sems.at[buffer, slot]
                                ).start()
                                first += depth

    fetch(0, 0)

    @pl.loop(0, count)
    def _(energy):
        buffer = lax.rem(energy, 2)

        @pl.when(energy + 1 < count)
        def _():
            fetch(energy + 1, 1 - buffer)

        dot = functools.partial(jnp.dot, preferred_element_type=jnp.float32)
        for mode in range(MODES):
            scales = []
            for side in range(2):
                slot = mode * 2 + side
                held = planes.at[buffer, slot]
                pltpu.make_async_copy(held, held, sems.at[buffer, slot]).wait()
                scales.append(jnp.where(source_of(energy, mode, side)[0], (occupation[mode] + (1.0 - side)) * (1.0 / momenta), 0.0))
            combined = scales[0] * planes[buffer, 2 * mode] + scales[1] * planes[buffer, 2 * mode + 1]
            high = combined.astype(jnp.bfloat16)
            low = (combined - high.astype(jnp.float32)).astype(jnp.bfloat16)
            product = dot(high, right_high[mode]) + dot(low, right_high[mode]) + dot(high, right_low[mode])
            high = product.astype(jnp.bfloat16)
            low = (product - high.astype(jnp.float32)).astype(jnp.bfloat16)
            inner[mode, pl.ds(0, rows)] = high
            inner[mode, pl.ds(rows, rows)] = low
            inner[mode, pl.ds(2 * rows, rows)] = high
        for index, out in enumerate(outs):
            s, t = index // 2, index % 2
            block = lax.rem(core + t, 2)
            if not far:
                block = block + 2 * lax.rem(atom + s, n_atoms)
            where = pl.ds(pl.multiple_of(block * size, 8), size)
            total = dot(left[0, where], inner[0])
            for mode in range(1, MODES):
                total = total + dot(left[mode, where], inner[mode])
            out[energy] = total


def sandwich(steps, occupation, right, left, groups, n_atoms, momenta, base, grid_total, edev, far, line, out_rows, count):
    order = right[0].shape[-1]
    flat = [part for group in groups for half in group for part in half]
    rows = sum(part.shape[1] for part in groups[0][0])
    n_out = left.shape[1] // out_rows
    flops = count * 2 * 3 * MODES * (rows * order * order + left.shape[1] * rows * order)
    return pl.pallas_call(
        functools.partial(split_dot, len(groups), len(groups[0][0]), n_atoms, momenta, base, grid_total, edev, far, line),
        out_shape=[jax.ShapeDtypeStruct((count, out_rows, order), jnp.float32)] * n_out,
        in_specs=[pl.BlockSpec(memory_space=pltpu.SMEM)] * 2
        + [pl.BlockSpec(memory_space=pltpu.VMEM)] * 3
        + [pl.BlockSpec(memory_space=pltpu.HBM)] * len(flat),
        out_specs=[pl.BlockSpec(memory_space=pltpu.VMEM)] * n_out,
        scratch_shapes=[
            pltpu.VMEM((2, 2 * MODES, rows, order), jnp.float32),
            pltpu.VMEM((MODES, 3 * rows, order), jnp.bfloat16),
            pltpu.SemaphoreType.DMA((2, 2 * MODES)),
        ],
        compiler_params=pltpu.CompilerParams(vmem_limit_bytes=40 << 20),
        cost_estimate=pl.CostEstimate(
            flops=flops,
            bytes_accessed=count * 4 * (2 * MODES * rows * order + left.shape[1] * order),
            transcendentals=0,
        ),
        name="far_sandwich" if far else "near_sandwich",
    )(steps, occupation, right[0], right[1], left, *flat)


def gather_up(layout, count, *refs):
    out = refs[-1]
    core = lax.axis_index("kz")
    for own in range(2):

        @pl.when(core == own)
        def _(own=own):
            for half, energies in enumerate(layout):
                where = (own if half == 0 else 1 - own) * count
                for j, terms in enumerate(energies):
                    total = None
                    for ref, row in terms:
                        value = refs[ref][:, where + j, :] if row is None else refs[ref][row]
                        total = value if total is None else total + value
                    out[:, where + j, :] = total


def gathered(layout, count, arrays, before=None):
    terms = [[[(arrays.index(x), row) for x, row in entry] for entry in energies] for energies in layout]
    arrays = list(arrays)
    out_rows, order = arrays[0].shape[1:]
    step = min(out_rows, 32)
    whole = pl.BlockSpec((step, 2 * count, order), lambda i: (i, 0, 0))
    specs = [pl.BlockSpec((x.shape[0], step, order), lambda i: (0, i, 0)) for x in arrays]
    if before is not None:
        terms = [[entry + [(len(arrays), None)] for entry in energies] for energies in terms]
        arrays, specs = arrays + [before], specs + [whole]
    size = 4 * sum(x.size for x in arrays) + 4 * 2 * count * out_rows * order
    return pl.pallas_call(
        functools.partial(gather_up, terms, count),
        grid=(out_rows // step,),
        out_shape=jax.ShapeDtypeStruct((out_rows, 2 * count, order), jnp.float32),
        in_specs=specs,
        out_specs=whole,
        cost_estimate=pl.CostEstimate(flops=size // 4, bytes_accessed=size, transcendentals=0),
    )(*arrays)


class Terms(list):
    def index(self, x):
        return next(i for i, y in enumerate(self) if y is x)


def shards(green, couplings, occupation, offsets, owners):
    momenta_here, edev, brows, order = green.shape
    n, atoms, cores = lax.axis_size("energy"), lax.axis_size("atom"), lax.axis_size("kz")
    momenta = momenta_here * cores
    grid_total = n * edev
    _, atom, core = (lax.axis_index(a) for a in ("energy", "atom", "kz"))
    line = n == 2 * REACH
    half = edev // cores
    swap = [(i, (i + 1) % cores) for i in range(cores)]
    around = [[(i, (i + s) % atoms) for i in range(atoms)] for s in range(atoms)]

    size = brows // PIECES

    def summed(theirs, piece, *more):
        return pl.pallas_call(
            functools.partial(add_momenta, theirs, piece * size),
            out_shape=jax.ShapeDtypeStruct((half, size, order), jnp.float32),
            in_specs=[pl.BlockSpec(memory_space=pltpu.HBM)] * (1 + len(more)),
            out_specs=pl.BlockSpec(memory_space=pltpu.HBM),
            scratch_shapes=[
                pltpu.VMEM((half, momenta_here + len(more), size, order), jnp.float32),
                pltpu.VMEM((half, size, order), jnp.float32),
                pltpu.SemaphoreType.DMA((half,)),
                pltpu.SemaphoreType.DMA((half,)),
            ],
            cost_estimate=pl.CostEstimate(
                flops=momenta_here * half * size * order,
                bytes_accessed=4 * (momenta_here + 1 + len(more)) * half * size * order,
                transcendentals=0,
            ),
            name="add_momenta",
        )(green, *more)

    own = []
    for piece in range(PIECES):
        given = summed(True, piece)
        given = lax.ppermute(given, "kz", swap)
        own.append(summed(False, piece, given))

    if line:
        up = [[(i, i + 1) for i in range(d, n - 1)] for d in range(REACH)]
        down = [[(i, i - 1) for i in range(n - 1 - d, 0, -1)] for d in range(REACH)]
    else:
        up = [[(i, (i + 1) % n) for i in range(n)]] * REACH
        down = [[(i, (i - 1) % n) for i in range(n)]] * REACH
    streams = {0: own}
    for d in range(1, REACH + 1):
        streams[-d] = [lax.ppermute(x, "energy", up[d - 1]) for x in streams[1 - d]]
        streams[d] = [lax.ppermute(x, "energy", down[d - 1]) for x in streams[d - 1]]
    groups = []
    for d in range(-REACH, REACH + 1):
        axes, pairs = "kz", swap
        if line and abs(d) == REACH:
            axes = ("energy", "kz")
            pairs = [
                (i * cores + k, i * cores + (k + 1) % cores) for i in range(n) if 0 <= i + d < n for k in range(cores)
            ]
        groups.append((streams[d], [lax.ppermute(x, axes, pairs) for x in streams[d]]))

    table_rows = couplings.shape[0]
    strip = order // cores
    mine = lax.dynamic_slice(couplings, (0, core * strip, 0), (table_rows, strip, order))
    others = []
    for s in range(1, atoms):
        got = lax.ppermute(mine, "atom", around[s])
        others.append((got, lax.ppermute(got, "kz", swap)))
    rows_of = lax.rem(owners, jnp.int32(table_rows))
    behind_of = lax.rem(atom - lax.div(owners, jnp.int32(table_rows)) + atoms, jnp.int32(atoms))

    def pick(m):
        row, behind = rows_of[m], behind_of[m]

        def at(table):
            return lax.dynamic_slice(table, (row, 0, 0), (1,) + table.shape[1:])[0]

        value = at(couplings)
        for s, (got, other) in enumerate(others, 1):
            first = jnp.where(core == 0, at(got), at(other))
            second = jnp.where(core == 0, at(other), at(got))
            value = jnp.where(behind == s, jnp.concatenate([first, second], 0), value)
        return value

    coupling = jnp.stack([pick(m) for m in range(MODES)], 0)
    right = halves(coupling.swapaxes(1, 2))
    out_rows = order // (atoms * cores)

    def left_of(x):
        high, low = halves(x)
        return jnp.concatenate([high, high, low], 2)

    left_near = left_of(lax.dynamic_slice(coupling, (0, 0, atom * brows), (MODES, order, brows)))

    beyond = []
    if line:
        left_far = left_of(
            lax.dynamic_slice(coupling, (0, atom * cores * out_rows, 0), (MODES, cores * out_rows, order))
        )
        got = [lax.ppermute(x, "atom", around[s]) for s in range(1, atoms) for x in own]
        got, right, left_far, left_near = lax.optimization_barrier((got, right, left_far, left_near))
        whole = (
            list(own) + got,
            groups[REACH][1] + [lax.ppermute(x, "kz", swap) for x in got],
        )
        sums = sandwich(
            offsets, occupation, right, left_far, [whole], atoms, momenta, 0, grid_total, edev, True, line, out_rows, half
        )
        both = jnp.concatenate([sums[0], lax.ppermute(sums[1], "kz", swap)], 0)
        beyond.append(lax.ppermute(both, "energy", [(0, n - 1), (n - 1, 0)]))

    terms = [[[] for _ in range(atoms)] for _ in range(cores)]
    base = 0
    for count in chunks_of(half):
        sums = sandwich(
            offsets, occupation, right, left_near, groups, atoms, momenta, base, grid_total, edev, False, line, out_rows, count
        )
        base += count
        for s in range(atoms - 1, -1, -1):
            for t in range(cores):
                block = sums[s * cores + t]
                if s or t:
                    pairs = [
                        (i * cores + k, ((i + s) % atoms) * cores + (k + t) % cores)
                        for i in range(atoms)
                        for k in range(cores)
                    ]
                    block = lax.ppermute(block, ("atom", "kz"), pairs)
                terms[t][s].append(block)
    chunks = chunks_of(half)
    entries = [[[] for _ in range(half)] for _ in range(cores)]
    late = [[[] for _ in range(half)] for _ in range(cores)]
    early, last = Terms(beyond), Terms()
    for t in range(cores):
        for s in range(atoms):
            first = 0
            for chunk, block in enumerate(terms[t][s]):
                held = (last, late) if s and chunk == len(chunks) - 1 else (early, entries)
                held[0].append(block)
                for row in range(chunks[chunk]):
                    held[1][t][first + row].append((block, row))
                first += chunks[chunk]
        for j in range(half):
            for block in beyond:
                entries[t][j].append((block, t * half + j))
    total = gathered(entries, half, early)
    return gathered(late, half, last, total)


def solution(mesh):
    return jax.shard_map(
        shards,
        mesh=mesh,
        in_specs=(P(("grp", "kz"), "energy", "atom", None), P("atom", None, None), P(), P(), P()),
        out_specs=P(("grp", "atom", "kz"), "energy", None),
        check_vma=False,
    )
```

```python
import functools

import jax
import jax.numpy as jnp
from jax import lax
from jax.experimental import pallas as pl
from jax.experimental.pallas import tpu as pltpu
from jax.sharding import PartitionSpec as P


MODES = 3
REACH = 2
PIECES = 2


def chunks_of(half):
    return [1] * half


def halves(x):
    high = x.astype(jnp.bfloat16)
    return high, (x - high.astype(jnp.float32)).astype(jnp.bfloat16)


def side_by_side(out, x):
    high, low = halves(x)
    depth = x.shape[1]
    out[0, :, pl.ds(0, depth)] = high
    out[0, :, pl.ds(depth, depth)] = high
    out[0, :, pl.ds(2 * depth, depth)] = low


def prepare_far(coupling, right_high, right_low, left):
    right_high[0], right_low[0] = halves(coupling[0].T)
    rows = left.shape[1]
    first = pl.multiple_of(lax.axis_index("atom") * rows, 8)
    side_by_side(left, coupling[0, pl.ds(first, rows), :])


def prepare_near(coupling, left):
    depth = left.shape[2] // 3
    first = pl.multiple_of(lax.axis_index("atom") * depth, 128)
    side_by_side(left, coupling[0, :, pl.ds(first, depth)])


def prepared(kernel, coupling, shapes):
    order = coupling.shape[-1]
    return pl.pallas_call(
        kernel,
        grid=(MODES,),
        out_shape=[jax.ShapeDtypeStruct((MODES,) + shape, jnp.bfloat16) for shape in shapes],
        in_specs=[pl.BlockSpec((1, order, order), lambda m: (m, 0, 0))],
        out_specs=[pl.BlockSpec((1,) + shape, lambda m: (m, 0, 0)) for shape in shapes],
        cost_estimate=pl.CostEstimate(
            flops=8 * coupling.size,
            bytes_accessed=4 * coupling.size + 2 * MODES * sum(a * b for a, b in shapes),
            transcendentals=0,
        ),
    )(coupling)


def add_momenta(theirs, first, green, *refs):
    out, held, total, arrived, left = refs[-5:]
    given = refs[:-5]
    momenta, count, size = green.shape[0], held.shape[0], held.shape[2]
    core = lax.axis_index("kz")
    base = (1 - core if theirs else core) * count
    for e in range(count):
        for k in range(momenta):
            pltpu.make_async_copy(green.at[k, base + e, pl.ds(first, size)], held.at[e, k], arrived.at[e]).start()
        for ref in given:
            pltpu.make_async_copy(ref.at[e], held.at[e, momenta], arrived.at[e]).start()
    for e in range(count):
        pltpu.make_async_copy(held.at[e], held.at[e], arrived.at[e]).wait()
        value = held[e, 0]
        for k in range(1, held.shape[1]):
            value = value + held[e, k]
        total[e] = value
        pltpu.make_async_copy(total.at[e], out.at[e], left.at[e]).start()
    for e in range(count):
        pltpu.make_async_copy(total.at[e], out.at[e], left.at[e]).wait()


def split_dot(n_groups, n_parts, n_atoms, momenta, base, grid_total, edev, far, line, steps, occupation, right_high, right_low, left, *refs):
    sources = [
        [refs[(g * 2 + h) * n_parts : (g * 2 + h + 1) * n_parts] for h in range(2)]
        for g in range(n_groups)
    ]
    outs = refs[n_groups * 2 * n_parts : -3]
    planes, inner, sems = refs[-3:]
    count, size = outs[0].shape[:2]
    rows = planes.shape[2]
    half_planes = edev // 2
    place, core, atom = (lax.axis_index(a) for a in ("energy", "kz", "atom"))
    blocks = grid_total // edev
    target = blocks - 1 - place if far else place
    base = base + core * half_planes

    def source_of(energy, mode, side):
        step = steps[mode] if side == 0 else -steps[mode]
        source = lax.rem(target * edev + base + energy + step + grid_total, grid_total)
        rel = lax.div(source, edev) - place
        if far:
            valid = rel == 0
        elif line:
            valid = jnp.abs(rel) <= REACH
        else:
            rel = lax.rem(rel + REACH + blocks, blocks) - REACH
            valid = rel <= REACH
        group = jnp.where(valid, rel + n_groups // 2, n_groups // 2)
        return valid, group, lax.rem(source, edev)

    def fetch(energy, buffer):
        for mode in range(MODES):
            for side in range(2):
                _, group, plane = source_of(energy, mode, side)
                other = jnp.where(lax.div(plane, half_planes) == core, 0, 1)
                at = lax.rem(plane, half_planes)
                slot = mode * 2 + side
                for g in range(n_groups):

                    @pl.when(group == g)
                    def _(g=g, at=at, slot=slot, other=other):
                        for h in range(2):

                            @pl.when(other == h)
                            def _(h=h):
                                first = 0
                                for ref in sources[g][h]:
                                    depth = ref.shape[1]
                                    start = first
                                    if far:
                                        per = rows // n_atoms
                                        behind = lax.rem(atom - first // per + n_atoms, n_atoms)
                                        start = pl.multiple_of(behind * per + first % per, 8)
                                    pltpu.make_async_copy(
                                        ref.at[at], planes.at[buffer, slot, pl.ds(start, depth)], sems.at[buffer, slot]
                                    ).start()
                                    first += depth

    fetch(0, 0)

    @pl.loop(0, count)
    def _(energy):
        buffer = lax.rem(energy, 2)

        if count > 1:

            @pl.when(energy + 1 < count)
            def _():
                fetch(energy + 1, 1 - buffer)

        dot = functools.partial(jnp.dot, preferred_element_type=jnp.float32)
        for mode in range(MODES):
            scales = []
            for side in range(2):
                slot = mode * 2 + side
                held = planes.at[buffer, slot]
                pltpu.make_async_copy(held, held, sems.at[buffer, slot]).wait()
                scales.append(jnp.where(source_of(energy, mode, side)[0], (occupation[mode] + (1.0 - side)) * (1.0 / momenta), 0.0))
            combined = scales[0] * planes[buffer, 2 * mode] + scales[1] * planes[buffer, 2 * mode + 1]
            high = combined.astype(jnp.bfloat16)
            low = (combined - high.astype(jnp.float32)).astype(jnp.bfloat16)
            product = dot(high, right_high[mode]) + dot(low, right_high[mode]) + dot(high, right_low[mode])
            high = product.astype(jnp.bfloat16)
            low = (product - high.astype(jnp.float32)).astype(jnp.bfloat16)
            inner[mode, pl.ds(0, rows)] = high
            inner[mode, pl.ds(rows, rows)] = low
            inner[mode, pl.ds(2 * rows, rows)] = high
        for index, out in enumerate(outs):
            s, t = index // 2, index % 2
            block = lax.rem(core + t, 2)
            if not far:
                block = block + 2 * lax.rem(atom + s, n_atoms)
            where = pl.ds(pl.multiple_of(block * size, 8), size)
            total = dot(left[0, where], inner[0])
            for mode in range(1, MODES):
                total = total + dot(left[mode, where], inner[mode])
            out[energy] = total


def sandwich(steps, occupation, right, left, groups, n_atoms, momenta, base, grid_total, edev, far, line, out_rows, count):
    order = right[0].shape[-1]
    flat = [part for group in groups for half in group for part in half]
    rows = sum(part.shape[1] for part in groups[0][0])
    n_out = left.shape[1] // out_rows
    buffers = min(count, 2)
    held = 4 * (2 * MODES * buffers + 6) * rows * order + 2 * 3 * MODES * rows * order + (6 << 20)
    held += 4 * left.shape[1] * order * (count + 3) + 4 * MODES * order * order + 2 * left.size
    flops = count * 2 * 3 * MODES * (rows * order * order + left.shape[1] * rows * order)
    return pl.pallas_call(
        functools.partial(split_dot, len(groups), len(groups[0][0]), n_atoms, momenta, base, grid_total, edev, far, line),
        out_shape=[jax.ShapeDtypeStruct((count, out_rows, order), jnp.float32)] * n_out,
        in_specs=[pl.BlockSpec(memory_space=pltpu.SMEM)] * 2
        + [pl.BlockSpec(memory_space=pltpu.VMEM)] * 3
        + [pl.BlockSpec(memory_space=pltpu.HBM)] * len(flat),
        out_specs=[pl.BlockSpec(memory_space=pltpu.VMEM)] * n_out,
        scratch_shapes=[
            pltpu.VMEM((buffers, 2 * MODES, rows, order), jnp.float32),
            pltpu.VMEM((MODES, 3 * rows, order), jnp.bfloat16),
            pltpu.SemaphoreType.DMA((2, 2 * MODES)),
        ],
        compiler_params=pltpu.CompilerParams(vmem_limit_bytes=held),
        cost_estimate=pl.CostEstimate(
            flops=flops,
            bytes_accessed=count * 4 * (2 * MODES * rows * order + left.shape[1] * order),
            transcendentals=0,
        ),
        name="far_sandwich" if far else "near_sandwich",
    )(steps, occupation, right[0], right[1], left, *flat)


def gather_up(layout, count, before, *refs):
    out = refs[-1]
    core = lax.axis_index("kz")
    for own in range(2):

        @pl.when(core == own)
        def _(own=own):
            if before:
                out[...] = refs[-2][...]
            for half, energies in enumerate(layout):
                where = (own if half == 0 else 1 - own) * count
                for j, terms in enumerate(energies):
                    total = out[:, where + j, :] if before else None
                    for ref, row in terms:
                        total = refs[ref][row] if total is None else total + refs[ref][row]
                    if terms:
                        out[:, where + j, :] = total


def gathered(layout, count, arrays, before=None):
    terms = [[[(arrays.index(x), row) for x, row in entry] for entry in energies] for energies in layout]
    arrays = list(arrays)
    out_rows, order = arrays[0].shape[1:]
    step = min(out_rows, 32)
    whole = pl.BlockSpec((step, 2 * count, order), lambda i: (i, 0, 0))
    specs = [pl.BlockSpec((x.shape[0], step, order), lambda i: (0, i, 0)) for x in arrays]
    if before is not None:
        arrays, specs = arrays + [before], specs + [whole]
    size = 4 * sum(x.size for x in arrays) + 4 * 2 * count * out_rows * order
    return pl.pallas_call(
        functools.partial(gather_up, terms, count, before is not None),
        grid=(out_rows // step,),
        out_shape=jax.ShapeDtypeStruct((out_rows, 2 * count, order), jnp.float32),
        in_specs=specs,
        out_specs=whole,
        cost_estimate=pl.CostEstimate(flops=size // 4, bytes_accessed=size, transcendentals=0),
    )(*arrays)


class Terms(list):
    def index(self, x):
        return next(i for i, y in enumerate(self) if y is x)


def shards(green, couplings, occupation, offsets, owners):
    momenta_here, edev, brows, order = green.shape
    n, atoms, cores = lax.axis_size("energy"), lax.axis_size("atom"), lax.axis_size("kz")
    momenta = momenta_here * cores
    grid_total = n * edev
    parts = lax.axis_size("grp")
    atom, core, part = (lax.axis_index(a) for a in ("atom", "kz", "grp"))
    line = n == 2 * REACH
    half = edev // cores
    swap = [(i, (i + 1) % cores) for i in range(cores)]
    around = [[(i, (i + s) % atoms) for i in range(atoms)] for s in range(atoms)]

    size = brows // PIECES

    def summed(theirs, piece, *more):
        return pl.pallas_call(
            functools.partial(add_momenta, theirs, piece * size),
            out_shape=jax.ShapeDtypeStruct((half, size, order), jnp.float32),
            in_specs=[pl.BlockSpec(memory_space=pltpu.HBM)] * (1 + len(more)),
            out_specs=pl.BlockSpec(memory_space=pltpu.HBM),
            scratch_shapes=[
                pltpu.VMEM((half, momenta_here + len(more), size, order), jnp.float32),
                pltpu.VMEM((half, size, order), jnp.float32),
                pltpu.SemaphoreType.DMA((half,)),
                pltpu.SemaphoreType.DMA((half,)),
            ],
            cost_estimate=pl.CostEstimate(
                flops=momenta_here * half * size * order,
                bytes_accessed=4 * (momenta_here + 1 + len(more)) * half * size * order,
                transcendentals=0,
            ),
            name="add_momenta",
        )(green, *more)

    own = []
    for piece in range(PIECES):
        given = summed(True, piece)
        given = lax.ppermute(given, "kz", swap)
        own.append(summed(False, piece, given))

    if line:
        up = [[(i, i + 1) for i in range(d, n - 1)] for d in range(REACH)]
        down = [[(i, i - 1) for i in range(n - 1 - d, 0, -1)] for d in range(REACH)]
    else:
        up = [[(i, (i + 1) % n) for i in range(n)]] * REACH
        down = [[(i, (i - 1) % n) for i in range(n)]] * REACH
    streams = {0: own}
    for d in range(1, REACH + 1):
        streams[-d] = [lax.ppermute(x, "energy", up[d - 1]) for x in streams[1 - d]]
        streams[d] = [lax.ppermute(x, "energy", down[d - 1]) for x in streams[d - 1]]
    groups = []
    for d in range(-REACH, REACH + 1):
        axes, pairs = "kz", swap
        if line and abs(d) == REACH:
            axes = ("energy", "kz")
            pairs = [
                (i * cores + k, i * cores + (k + 1) % cores) for i in range(n) if 0 <= i + d < n for k in range(cores)
            ]
        groups.append((streams[d], [lax.ppermute(x, axes, pairs) for x in streams[d]]))

    table_rows = couplings.shape[0]
    strip = order // (cores * parts)
    mine = lax.dynamic_slice(couplings, (0, (part * cores + core) * strip, 0), (table_rows, strip, order))
    others = []
    for s in range(1, atoms):
        got = lax.ppermute(mine, "atom", around[s])
        ahead = [got] + [
            lax.ppermute(got, "grp", [(i, (i + d) % parts) for i in range(parts)]) for d in range(1, parts)
        ]
        others.append([(x, lax.ppermute(x, "kz", swap)) for x in ahead])
    rows_of = lax.rem(owners, jnp.int32(table_rows))
    behind_of = lax.rem(atom - lax.div(owners, jnp.int32(table_rows)) + atoms, jnp.int32(atoms))

    def pick(m):
        row, behind = rows_of[m], behind_of[m]

        def at(table):
            return lax.dynamic_slice(table, (row, 0, 0), (1,) + table.shape[1:])[0]

        value = at(couplings)
        for s, pieces in enumerate(others, 1):
            strips = []
            for g in range(parts):
                for k in range(cores):
                    chosen = None
                    for d, (same, other) in enumerate(pieces):
                        piece = jnp.where(core == k, at(same), at(other))
                        chosen = piece if d == 0 else jnp.where((g + d) % parts == part, piece, chosen)
                    strips.append(chosen)
            value = jnp.where(behind == s, jnp.concatenate(strips, 0), value)
        return value

    coupling = jnp.stack([pick(m) for m in range(MODES)], 0)
    out_rows = order // (atoms * cores)
    *right, left_far = prepared(prepare_far, coupling, [(order, order), (order, order), (cores * out_rows, 3 * order)])
    (left_near,) = prepared(prepare_near, coupling, [(order, 3 * brows)])

    beyond = []
    if line:
        got = [lax.ppermute(x, "atom", around[s]) for s in range(1, atoms) for x in own]
        whole = (
            list(own) + got,
            groups[REACH][1] + [lax.ppermute(x, "kz", swap) for x in got],
        )
        sums = sandwich(
            offsets, occupation, right, left_far, [whole], atoms, momenta, 0, grid_total, edev, True, line, out_rows, half
        )
        both = jnp.concatenate([sums[0], lax.ppermute(sums[1], "kz", swap)], 0)
        beyond.append(lax.ppermute(both, "energy", [(0, n - 1), (n - 1, 0)]))

    terms = [[[] for _ in range(atoms)] for _ in range(cores)]
    base = 0
    for count in chunks_of(half):
        sums = sandwich(
            offsets, occupation, right, left_near, groups, atoms, momenta, base, grid_total, edev, False, line, out_rows, count
        )
        base += count
        for s in range(atoms - 1, -1, -1):
            for t in range(cores):
                block = sums[s * cores + t]
                if s or t:
                    pairs = [
                        (i * cores + k, ((i + s) % atoms) * cores + (k + t) % cores)
                        for i in range(atoms)
                        for k in range(cores)
                    ]
                    block = lax.ppermute(block, ("atom", "kz"), pairs)
                terms[t][s].append(block)
    chunks = chunks_of(half)
    entries = [[[] for _ in range(half)] for _ in range(cores)]
    late = [[[] for _ in range(half)] for _ in range(cores)]
    early, last = Terms(beyond), Terms()
    for t in range(cores):
        for s in range(atoms):
            first = 0
            for chunk, block in enumerate(terms[t][s]):
                held = (last, late) if s and chunk == len(chunks) - 1 else (early, entries)
                held[0].append(block)
                for row in range(chunks[chunk]):
                    held[1][t][first + row].append((block, row))
                first += chunks[chunk]
        for j in range(half):
            for block in beyond:
                entries[t][j].append((block, t * half + j))
    total = gathered(entries, half, early)
    return gathered(late, half, last, total)


def solution(mesh):
    return jax.shard_map(
        shards,
        mesh=mesh,
        in_specs=(P(("grp", "kz"), "energy", "atom", None), P("atom", None, None), P(), P(), P()),
        out_specs=P(("grp", "atom", "kz"), "energy", None),
        check_vma=False,
    )
```

```python
import functools

import jax
import jax.numpy as jnp
from jax import lax
from jax.experimental import pallas as pl
from jax.experimental.pallas import tpu as pltpu
from jax.sharding import PartitionSpec as P


MODES = 3
REACH = 2
PIECES = 2


def chunks_of(half):
    return [1] * half


def halves(x):
    high = x.astype(jnp.bfloat16)
    return high, (x - high.astype(jnp.float32)).astype(jnp.bfloat16)


def side_by_side(out, x):
    high, low = halves(x)
    depth = x.shape[1]
    out[0, :, pl.ds(0, depth)] = high
    out[0, :, pl.ds(depth, depth)] = high
    out[0, :, pl.ds(2 * depth, depth)] = low


def prepare_far(coupling, right_high, right_low, left):
    right_high[0], right_low[0] = halves(coupling[0].T)
    rows = left.shape[1]
    first = pl.multiple_of(lax.axis_index("atom") * rows, 8)
    side_by_side(left, coupling[0, pl.ds(first, rows), :])


def prepare_near(coupling, left):
    depth = left.shape[2] // 3
    first = pl.multiple_of(lax.axis_index("atom") * depth, 128)
    side_by_side(left, coupling[0, :, pl.ds(first, depth)])


def prepared(kernel, coupling, shapes):
    order = coupling.shape[-1]
    return pl.pallas_call(
        kernel,
        grid=(MODES,),
        out_shape=[jax.ShapeDtypeStruct((MODES,) + shape, jnp.bfloat16) for shape in shapes],
        in_specs=[pl.BlockSpec((1, order, order), lambda m: (m, 0, 0))],
        out_specs=[pl.BlockSpec((1,) + shape, lambda m: (m, 0, 0)) for shape in shapes],
        cost_estimate=pl.CostEstimate(
            flops=8 * coupling.size,
            bytes_accessed=4 * coupling.size + 2 * MODES * sum(a * b for a, b in shapes),
            transcendentals=0,
        ),
    )(coupling)


def add_momenta(theirs, first, green, *refs):
    out, held, total, arrived, left = refs[-6:-1]
    given = refs[:-6]
    momenta, count, size = green.shape[0], held.shape[0], held.shape[2]
    core = lax.axis_index("kz")
    base = (1 - core if theirs else core) * count
    for e in range(count):
        for k in range(momenta):
            pltpu.make_async_copy(green.at[k, base + e, pl.ds(first, size)], held.at[e, k], arrived.at[e]).start()
        for ref in given:
            pltpu.make_async_copy(ref.at[e], held.at[e, momenta], arrived.at[e]).start()
    for e in range(count):
        pltpu.make_async_copy(held.at[e], held.at[e], arrived.at[e]).wait()
        value = held[e, 0]
        for k in range(1, held.shape[1]):
            value = value + held[e, k]
        total[e] = value
        pltpu.make_async_copy(total.at[e], out.at[e], left.at[e]).start()
    for e in range(count):
        pltpu.make_async_copy(total.at[e], out.at[e], left.at[e]).wait()


def split_dot(n_groups, n_parts, n_atoms, momenta, base, grid_total, edev, far, line, steps, occupation, right_high, right_low, left, *refs):
    sources = [
        [refs[(g * 2 + h) * n_parts : (g * 2 + h + 1) * n_parts] for h in range(2)]
        for g in range(n_groups)
    ]
    outs = refs[n_groups * 2 * n_parts : -3]
    planes, inner, sems = refs[-3:]
    count, size = outs[0].shape[:2]
    rows = planes.shape[2]
    half_planes = edev // 2
    place, core, atom = (lax.axis_index(a) for a in ("energy", "kz", "atom"))
    blocks = grid_total // edev
    target = blocks - 1 - place if far else place
    base = base + core * half_planes

    def source_of(energy, mode, side):
        step = steps[mode] if side == 0 else -steps[mode]
        source = lax.rem(target * edev + base + energy + step + grid_total, grid_total)
        rel = lax.div(source, edev) - place
        if far:
            valid = rel == 0
        elif line:
            valid = jnp.abs(rel) <= REACH
        else:
            rel = lax.rem(rel + REACH + blocks, blocks) - REACH
            valid = rel <= REACH
        group = jnp.where(valid, rel + n_groups // 2, n_groups // 2)
        return valid, group, lax.rem(source, edev)

    def fetch(energy, buffer):
        for mode in range(MODES):
            for side in range(2):
                _, group, plane = source_of(energy, mode, side)
                other = jnp.where(lax.div(plane, half_planes) == core, 0, 1)
                at = lax.rem(plane, half_planes)
                slot = mode * 2 + side
                for g in range(n_groups):

                    @pl.when(group == g)
                    def _(g=g, at=at, slot=slot, other=other):
                        for h in range(2):

                            @pl.when(other == h)
                            def _(h=h):
                                first = 0
                                for ref in sources[g][h]:
                                    depth = ref.shape[1]
                                    start = first
                                    if far:
                                        per = rows // n_atoms
                                        behind = lax.rem(atom - first // per + n_atoms, n_atoms)
                                        start = pl.multiple_of(behind * per + first % per, 8)
                                    pltpu.make_async_copy(
                                        ref.at[at], planes.at[buffer, slot, pl.ds(start, depth)], sems.at[buffer, slot]
                                    ).start()
                                    first += depth

    fetch(0, 0)

    @pl.loop(0, count)
    def _(energy):
        buffer = lax.rem(energy, 2)

        if count > 1:

            @pl.when(energy + 1 < count)
            def _():
                fetch(energy + 1, 1 - buffer)

        dot = functools.partial(jnp.dot, preferred_element_type=jnp.float32)
        for mode in range(MODES):
            scales = []
            for side in range(2):
                slot = mode * 2 + side
                held = planes.at[buffer, slot]
                pltpu.make_async_copy(held, held, sems.at[buffer, slot]).wait()
                scales.append(jnp.where(source_of(energy, mode, side)[0], (occupation[mode] + (1.0 - side)) * (1.0 / momenta), 0.0))
            combined = scales[0] * planes[buffer, 2 * mode] + scales[1] * planes[buffer, 2 * mode + 1]
            high = combined.astype(jnp.bfloat16)
            low = (combined - high.astype(jnp.float32)).astype(jnp.bfloat16)
            product = dot(high, right_high[mode]) + dot(low, right_high[mode]) + dot(high, right_low[mode])
            high = product.astype(jnp.bfloat16)
            low = (product - high.astype(jnp.float32)).astype(jnp.bfloat16)
            inner[mode, pl.ds(0, rows)] = high
            inner[mode, pl.ds(rows, rows)] = low
            inner[mode, pl.ds(2 * rows, rows)] = high
        for index, out in enumerate(outs):
            s, t = index // 2, index % 2
            block = lax.rem(core + t, 2)
            if not far:
                block = block + 2 * lax.rem(atom + s, n_atoms)
            where = pl.ds(pl.multiple_of(block * size, 8), size)
            total = dot(left[0, where], inner[0])
            for mode in range(1, MODES):
                total = total + dot(left[mode, where], inner[mode])
            out[energy] = total


def sandwich(steps, occupation, right, left, groups, n_atoms, momenta, base, grid_total, edev, far, line, out_rows, count):
    order = right[0].shape[-1]
    flat = [part for group in groups for half in group for part in half]
    rows = sum(part.shape[1] for part in groups[0][0])
    n_out = left.shape[1] // out_rows
    buffers = min(count, 2)
    held = 4 * (2 * MODES * buffers + 6) * rows * order + 2 * 3 * MODES * rows * order + (6 << 20)
    held += 4 * left.shape[1] * order * (count + 3) + 4 * MODES * order * order + 2 * left.size
    flops = count * 2 * 3 * MODES * (rows * order * order + left.shape[1] * rows * order)
    return pl.pallas_call(
        functools.partial(split_dot, len(groups), len(groups[0][0]), n_atoms, momenta, base, grid_total, edev, far, line),
        out_shape=[jax.ShapeDtypeStruct((count, out_rows, order), jnp.float32)] * n_out,
        in_specs=[pl.BlockSpec(memory_space=pltpu.SMEM)] * 2
        + [pl.BlockSpec(memory_space=pltpu.VMEM)] * 3
        + [pl.BlockSpec(memory_space=pltpu.HBM)] * len(flat),
        out_specs=[pl.BlockSpec(memory_space=pltpu.VMEM)] * n_out,
        scratch_shapes=[
            pltpu.VMEM((buffers, 2 * MODES, rows, order), jnp.float32),
            pltpu.VMEM((MODES, 3 * rows, order), jnp.bfloat16),
            pltpu.SemaphoreType.DMA((2, 2 * MODES)),
        ],
        compiler_params=pltpu.CompilerParams(vmem_limit_bytes=held),
        cost_estimate=pl.CostEstimate(
            flops=flops,
            bytes_accessed=count * 4 * (2 * MODES * rows * order + left.shape[1] * order),
            transcendentals=0,
        ),
        name="far_sandwich" if far else "near_sandwich",
    )(steps, occupation, right[0], right[1], left, *flat)


def gather_early(layout, count, *refs):
    out = refs[-1]
    core = lax.axis_index("kz")
    for own in range(2):

        @pl.when(core == own)
        def _(own=own):
            for half, energies in enumerate(layout):
                where = (own if half == 0 else 1 - own) * count
                for j, terms in enumerate(energies):
                    total = None
                    for ref, row in terms:
                        total = refs[ref][row] if total is None else total + refs[ref][row]
                    out[:, where + j, :] = total


def gather_late(layout, count, whole, *refs):
    out, total, sems = refs[-3:]
    full = refs[-3 - whole : -3]
    core = lax.axis_index("kz")
    step = total.shape[0] // sems.shape[0]
    for part in range(sems.shape[0]):
        rows = pl.ds(part * step, step)
        value = full[0][rows]
        for ref in full[1:]:
            value = value + ref[rows]
        total[rows] = value
        for own in range(2):

            @pl.when(core == own)
            def _(own=own, rows=rows):
                for half, energies in enumerate(layout):
                    where = (own if half == 0 else 1 - own) * count
                    for j, terms in enumerate(energies):
                        if terms:
                            value = total[rows, where + j, :]
                            for ref, row in terms:
                                value = value + refs[ref][row, rows]
                            total[rows, where + j, :] = value

        pltpu.make_async_copy(total.at[rows], out.at[rows], sems.at[part]).start()
    for part in range(sems.shape[0]):
        rows = pl.ds(part * step, step)
        pltpu.make_async_copy(total.at[rows], out.at[rows], sems.at[part]).wait()


def gathered(layout, count, arrays, before=()):
    terms = [[[(arrays.index(x), row) for x, row in entry] for entry in energies] for energies in layout]
    out_rows, order = arrays[0].shape[1:]
    arrays = list(arrays) + list(before)
    shape = (out_rows, 2 * count, order)
    size = 4 * sum(x.size for x in arrays) + 4 * 2 * count * out_rows * order
    vmem = pl.BlockSpec(memory_space=pltpu.VMEM)
    if before:
        parts = 4 if out_rows % 32 == 0 else 1
        kernel = functools.partial(gather_late, terms, count, len(before))
        scratch = [pltpu.VMEM(shape, jnp.float32), pltpu.SemaphoreType.DMA((parts,))]
    else:
        kernel, scratch = functools.partial(gather_early, terms, count), []
    return pl.pallas_call(
        kernel,
        out_shape=jax.ShapeDtypeStruct(shape, jnp.float32),
        in_specs=[vmem] * len(arrays),
        out_specs=pl.BlockSpec(memory_space=pltpu.HBM) if before else vmem,
        scratch_shapes=scratch,
        cost_estimate=pl.CostEstimate(flops=size // 4, bytes_accessed=size, transcendentals=0),
    )(*arrays)


class Terms(list):
    def index(self, x):
        return next(i for i, y in enumerate(self) if y is x)


def shards(green, couplings, occupation, offsets, owners):
    momenta_here, edev, brows, order = green.shape
    n, atoms, cores = lax.axis_size("energy"), lax.axis_size("atom"), lax.axis_size("kz")
    momenta = momenta_here * cores
    grid_total = n * edev
    parts = lax.axis_size("grp")
    atom, core, part = (lax.axis_index(a) for a in ("atom", "kz", "grp"))
    line = n == 2 * REACH
    half = edev // cores
    swap = [(i, (i + 1) % cores) for i in range(cores)]
    around = [[(i, (i + s) % atoms) for i in range(atoms)] for s in range(atoms)]

    size = brows // PIECES

    def summed(theirs, piece, *more):
        return pl.pallas_call(
            functools.partial(add_momenta, theirs, piece * size),
            out_shape=jax.ShapeDtypeStruct((half, size, order), jnp.float32),
            in_specs=[pl.BlockSpec(memory_space=pltpu.HBM)] * (1 + len(more)),
            out_specs=pl.BlockSpec(memory_space=pltpu.HBM),
            scratch_shapes=[
                pltpu.VMEM((half, momenta_here + len(more), size, order), jnp.float32),
                pltpu.VMEM((half, size, order), jnp.float32),
                pltpu.SemaphoreType.DMA((half,)),
                pltpu.SemaphoreType.DMA((half,)),
                pltpu.VMEM((48 << 10, 256), jnp.float32),
            ],
            compiler_params=pltpu.CompilerParams(vmem_limit_bytes=60 << 20),
            cost_estimate=pl.CostEstimate(
                flops=momenta_here * half * size * order,
                bytes_accessed=4 * (momenta_here + 1 + len(more)) * half * size * order,
                transcendentals=0,
            ),
            name="add_momenta",
        )(green, *more)

    own = []
    for piece in range(PIECES):
        given = summed(True, piece)
        given = lax.ppermute(given, "kz", swap)
        own.append(summed(False, piece, given))

    if line:
        up = [[(i, i + 1) for i in range(d, n - 1)] for d in range(REACH)]
        down = [[(i, i - 1) for i in range(n - 1 - d, 0, -1)] for d in range(REACH)]
    else:
        up = [[(i, (i + 1) % n) for i in range(n)]] * REACH
        down = [[(i, (i - 1) % n) for i in range(n)]] * REACH
    streams = {0: own}
    for d in range(1, REACH + 1):
        streams[-d] = [lax.ppermute(x, "energy", up[d - 1]) for x in streams[1 - d]]
        streams[d] = [lax.ppermute(x, "energy", down[d - 1]) for x in streams[d - 1]]
    groups = []
    for d in range(-REACH, REACH + 1):
        axes, pairs = "kz", swap
        if line and abs(d) == REACH:
            axes = ("energy", "kz")
            pairs = [
                (i * cores + k, i * cores + (k + 1) % cores) for i in range(n) if 0 <= i + d < n for k in range(cores)
            ]
        groups.append((streams[d], [lax.ppermute(x, axes, pairs) for x in streams[d]]))

    table_rows = couplings.shape[0]
    strip = order // (cores * parts)
    mine = lax.dynamic_slice(couplings, (0, (part * cores + core) * strip, 0), (table_rows, strip, order))
    others = []
    for s in range(1, atoms):
        got = lax.ppermute(mine, "atom", around[s])
        ahead = [got] + [
            lax.ppermute(got, "grp", [(i, (i + d) % parts) for i in range(parts)]) for d in range(1, parts)
        ]
        others.append([(x, lax.ppermute(x, "kz", swap)) for x in ahead])
    rows_of = lax.rem(owners, jnp.int32(table_rows))
    behind_of = lax.rem(atom - lax.div(owners, jnp.int32(table_rows)) + atoms, jnp.int32(atoms))

    def pick(m):
        row, behind = rows_of[m], behind_of[m]

        def at(table):
            return lax.dynamic_slice(table, (row, 0, 0), (1,) + table.shape[1:])[0]

        value = at(couplings)
        for s, pieces in enumerate(others, 1):
            strips = []
            for g in range(parts):
                for k in range(cores):
                    chosen = None
                    for d, (same, other) in enumerate(pieces):
                        piece = jnp.where(core == k, at(same), at(other))
                        chosen = piece if d == 0 else jnp.where((g + d) % parts == part, piece, chosen)
                    strips.append(chosen)
            value = jnp.where(behind == s, jnp.concatenate(strips, 0), value)
        return value

    coupling = jnp.stack([pick(m) for m in range(MODES)], 0)
    out_rows = order // (atoms * cores)
    *right, left_far = prepared(prepare_far, coupling, [(order, order), (order, order), (cores * out_rows, 3 * order)])
    (left_near,) = prepared(prepare_near, coupling, [(order, 3 * brows)])

    beyond = []
    if line:
        got = [lax.ppermute(x, "atom", around[s]) for s in range(1, atoms) for x in own]
        whole = (
            list(own) + got,
            groups[REACH][1] + [lax.ppermute(x, "kz", swap) for x in got],
        )
        sums = sandwich(
            offsets, occupation, right, left_far, [whole], atoms, momenta, 0, grid_total, edev, True, line, out_rows, half
        )
        swapped = lax.ppermute(sums[1], "kz", swap)
        both = jnp.concatenate(
            [jnp.where(core == 0, sums[0], swapped), jnp.where(core == 0, swapped, sums[0])], 0
        ).swapaxes(0, 1)
        beyond.append(lax.ppermute(both, "energy", [(0, n - 1), (n - 1, 0)]))

    terms = [[[] for _ in range(atoms)] for _ in range(cores)]
    base = 0
    for count in chunks_of(half):
        sums = sandwich(
            offsets, occupation, right, left_near, groups, atoms, momenta, base, grid_total, edev, False, line, out_rows, count
        )
        base += count
        for s in range(atoms - 1, -1, -1):
            for t in range(cores):
                block = sums[s * cores + t]
                if s or t:
                    pairs = [
                        (i * cores + k, ((i + s) % atoms) * cores + (k + t) % cores)
                        for i in range(atoms)
                        for k in range(cores)
                    ]
                    block = lax.ppermute(block, ("atom", "kz"), pairs)
                terms[t][s].append(block)
    chunks = chunks_of(half)
    entries = [[[] for _ in range(half)] for _ in range(cores)]
    late = [[[] for _ in range(half)] for _ in range(cores)]
    early, last = Terms(), Terms()
    for t in range(cores):
        for s in range(atoms):
            first = 0
            for chunk, block in enumerate(terms[t][s]):
                held = (last, late) if s and chunk == len(chunks) - 1 else (early, entries)
                held[0].append(block)
                for row in range(chunks[chunk]):
                    held[1][t][first + row].append((block, row))
                first += chunks[chunk]
    total = gathered(entries, half, early)
    return gathered(late, half, last, [total] + beyond)


def solution(mesh):
    return jax.shard_map(
        shards,
        mesh=mesh,
        in_specs=(P(("grp", "kz"), "energy", "atom", None), P("atom", None, None), P(), P(), P()),
        out_specs=P(("grp", "atom", "kz"), "energy", None),
        check_vma=False,
    )
```

```python
import functools

import jax
import jax.numpy as jnp
from jax import lax
from jax.experimental import pallas as pl
from jax.experimental.pallas import tpu as pltpu
from jax.sharding import PartitionSpec as P


MODES = 3
REACH = 2
PIECES = 2


def chunks_of(half):
    return [1] * half


def halves(x):
    high = x.astype(jnp.bfloat16)
    return high, (x - high.astype(jnp.float32)).astype(jnp.bfloat16)


def side_by_side(out, mode, x):
    high, low = halves(x)
    depth = x.shape[1]
    out[mode, :, pl.ds(0, depth)] = high
    out[mode, :, pl.ds(depth, depth)] = high
    out[mode, :, pl.ds(2 * depth, depth)] = low


def prepare(atoms, parts, cores, owners, couplings, *refs):
    right_high, right_low, far, near, held, sems = refs[-6:]
    pieces = refs[:-6]
    atom, core, part = (lax.axis_index(a) for a in ("atom", "kz", "grp"))
    table_rows = couplings.shape[0]
    for mode in range(MODES):
        row = lax.rem(owners[mode], table_rows)
        behind = lax.rem(atom - lax.div(owners[mode], table_rows) + atoms, atoms)

        @pl.when(behind == 0)
        def _(mode=mode, row=row):
            pltpu.make_async_copy(couplings.at[row], held.at[mode], sems.at[mode]).start()

        for s in range(1, atoms):

            @pl.when(behind == s)
            def _(mode=mode, row=row, s=s):
                for d in range(parts):
                    for o in range(cores):
                        piece = pieces[((s - 1) * parts + d) * cores + o]
                        strip = piece.shape[1]
                        at = lax.rem(part - d + parts, parts) * cores + lax.rem(core - o + cores, cores)
                        rows = pl.ds(pl.multiple_of(at * strip, 8), strip)
                        pltpu.make_async_copy(piece.at[row], held.at[mode, rows], sems.at[mode]).start()

    @pl.loop(0, MODES)
    def _(mode):
        pltpu.make_async_copy(held.at[mode], held.at[mode], sems.at[mode]).wait()
        right_high[mode], right_low[mode] = halves(held[mode].T)
        rows, depth = far.shape[1], near.shape[2] // 3
        side_by_side(far, mode, held[mode, pl.ds(pl.multiple_of(atom * rows, 8), rows), :])
        side_by_side(near, mode, held[mode, :, pl.ds(pl.multiple_of(atom * depth, 128), depth)])


def guard(steps, out):
    for mode in range(MODES):
        out[mode] = steps[mode]


def add_momenta(theirs, first, green, *refs):
    out, held, total, arrived, left = refs[-5:]
    given = refs[:-5]
    momenta, count, size = green.shape[0], held.shape[0], held.shape[2]
    core = lax.axis_index("kz")
    base = (1 - core if theirs else core) * count
    for e in range(count):
        for k in range(momenta):
            pltpu.make_async_copy(green.at[k, base + e, pl.ds(first, size)], held.at[e, k], arrived.at[e]).start()
        for ref in given:
            pltpu.make_async_copy(ref.at[e], held.at[e, momenta], arrived.at[e]).start()

    @pl.loop(0, count)
    def _(e):
        pltpu.make_async_copy(held.at[e], held.at[e], arrived.at[e]).wait()
        value = held[e, 0]
        for k in range(1, held.shape[1]):
            value = value + held[e, k]
        total[e] = value
        pltpu.make_async_copy(total.at[e], out.at[e], left.at[e]).start()

    for e in range(count):
        pltpu.make_async_copy(total.at[e], out.at[e], left.at[e]).wait()


def split_dot(n_groups, n_parts, n_atoms, momenta, base, grid_total, edev, far, line, steps, occupation, right_high, right_low, left, *refs):
    sources = [
        [refs[(g * 2 + h) * n_parts : (g * 2 + h + 1) * n_parts] for h in range(2)]
        for g in range(n_groups)
    ]
    outs = refs[n_groups * 2 * n_parts : -3]
    planes, inner, sems = refs[-3:]
    count, size = outs[0].shape[:2]
    rows = planes.shape[2]
    half_planes = edev // 2
    place, core, atom = (lax.axis_index(a) for a in ("energy", "kz", "atom"))
    blocks = grid_total // edev
    target = blocks - 1 - place if far else place
    base = base + core * half_planes

    def source_of(energy, mode, side):
        step = steps[mode] if side == 0 else -steps[mode]
        source = lax.rem(target * edev + base + energy + step + grid_total, grid_total)
        rel = lax.div(source, edev) - place
        if far:
            valid = rel == 0
        elif line:
            valid = jnp.abs(rel) <= REACH
        else:
            rel = lax.rem(rel + REACH + blocks, blocks) - REACH
            valid = rel <= REACH
        group = jnp.where(valid, rel + n_groups // 2, n_groups // 2)
        return valid, group, lax.rem(source, edev)

    def fetch(energy, buffer):
        for mode in range(MODES):
            for side in range(2):
                _, group, plane = source_of(energy, mode, side)
                other = jnp.where(lax.div(plane, half_planes) == core, 0, 1)
                at = lax.rem(plane, half_planes)
                slot = mode * 2 + side
                for g in range(n_groups):

                    @pl.when(group == g)
                    def _(g=g, at=at, slot=slot, other=other):
                        for h in range(2):

                            @pl.when(other == h)
                            def _(h=h):
                                first = 0
                                for ref in sources[g][h]:
                                    depth = ref.shape[1]
                                    start = first
                                    if far:
                                        per = rows // n_atoms
                                        behind = lax.rem(atom - first // per + n_atoms, n_atoms)
                                        start = pl.multiple_of(behind * per + first % per, 8)
                                    pltpu.make_async_copy(
                                        ref.at[at], planes.at[buffer, slot, pl.ds(start, depth)], sems.at[buffer, slot]
                                    ).start()
                                    first += depth

    fetch(0, 0)

    @pl.loop(0, count)
    def _(energy):
        buffer = lax.rem(energy, 2)

        if count > 1:

            @pl.when(energy + 1 < count)
            def _():
                fetch(energy + 1, 1 - buffer)

        dot = functools.partial(jnp.dot, preferred_element_type=jnp.float32)

        @pl.loop(0, MODES)
        def _(mode):
            scales = []
            for side in range(2):
                held = planes.at[buffer, mode * 2 + side]
                pltpu.make_async_copy(held, held, sems.at[buffer, mode * 2 + side]).wait()
                scale = (occupation[mode] + (1.0 - side)) * (1.0 / momenta)
                scales.append(jnp.where(source_of(energy, mode, side)[0], scale, 0.0))
            combined = scales[0] * planes[buffer, 2 * mode] + scales[1] * planes[buffer, 2 * mode + 1]
            high, low = halves(combined)
            product = dot(high, right_high[mode]) + dot(low, right_high[mode]) + dot(high, right_low[mode])
            high, low = halves(product)
            inner[pl.ds(0, rows)] = high
            inner[pl.ds(rows, rows)] = low
            inner[pl.ds(2 * rows, rows)] = high
            for index, out in enumerate(outs):
                s, t = index // 2, index % 2
                block = lax.rem(core + t, 2)
                if not far:
                    block = block + 2 * lax.rem(atom + s, n_atoms)
                where = pl.ds(pl.multiple_of(block * size, 8), size)
                total = dot(left[mode, where], inner[...])

                @pl.when(mode == 0)
                def _(out=out, total=total):
                    out[energy] = total

                @pl.when(mode > 0)
                def _(out=out, total=total):
                    out[energy] += total


def sandwich(steps, occupation, right, left, groups, n_atoms, momenta, base, grid_total, edev, far, line, out_rows, count):
    order = right[0].shape[-1]
    flat = [part for group in groups for half in group for part in half]
    rows = sum(part.shape[1] for part in groups[0][0])
    n_out = left.shape[1] // out_rows
    buffers = min(count, 2)
    held = 4 * (2 * MODES * buffers + 6) * rows * order + 2 * 3 * MODES * rows * order + (6 << 20)
    held += 4 * left.shape[1] * order * (count + 3) + 4 * MODES * order * order + 2 * left.size
    flops = count * 2 * 3 * MODES * (rows * order * order + left.shape[1] * rows * order)
    return pl.pallas_call(
        functools.partial(split_dot, len(groups), len(groups[0][0]), n_atoms, momenta, base, grid_total, edev, far, line),
        out_shape=[jax.ShapeDtypeStruct((count, out_rows, order), jnp.float32)] * n_out,
        in_specs=[pl.BlockSpec(memory_space=pltpu.SMEM)] * 2
        + [pl.BlockSpec(memory_space=pltpu.VMEM)] * 3
        + [pl.BlockSpec(memory_space=pltpu.HBM)] * len(flat),
        out_specs=[pl.BlockSpec(memory_space=pltpu.VMEM)] * n_out,
        scratch_shapes=[
            pltpu.VMEM((buffers, 2 * MODES, rows, order), jnp.float32),
            pltpu.VMEM((3 * rows, order), jnp.bfloat16),
            pltpu.SemaphoreType.DMA((2, 2 * MODES)),
        ],
        compiler_params=pltpu.CompilerParams(vmem_limit_bytes=held),
        cost_estimate=pl.CostEstimate(
            flops=flops,
            bytes_accessed=count * 4 * (2 * MODES * rows * order + left.shape[1] * order),
            transcendentals=0,
        ),
        name="far_sandwich" if far else "near_sandwich",
    )(steps, occupation, right[0], right[1], left, *flat)


def gather_early(layout, count, *refs):
    out = refs[-1]
    core = lax.axis_index("kz")
    group = 16
    for own in range(2):

        @pl.when(core == own)
        def _(own=own):
            @pl.loop(0, out.shape[0] // group)
            def _(at):
                rows = pl.ds(pl.multiple_of(at * group, group), group)
                for half, energies in enumerate(layout):
                    where = (own if half == 0 else 1 - own) * count
                    for j, terms in enumerate(energies):
                        total = None
                        for ref, row in terms:
                            total = refs[ref][row, rows] if total is None else total + refs[ref][row, rows]
                        out[rows, where + j, :] = total


def gather_late(layout, count, whole, *refs):
    out, total, sem = refs[-3:]
    full = refs[-3 - whole : -3]
    core = lax.axis_index("kz")
    group = 16

    @pl.loop(0, total.shape[0] // group)
    def _(at):
        rows = pl.ds(pl.multiple_of(at * group, group), group)
        value = full[0][rows]
        for ref in full[1:]:
            value = value + ref[rows]
        total[rows] = value
        for own in range(2):

            @pl.when(core == own)
            def _(own=own):
                for half, energies in enumerate(layout):
                    where = (own if half == 0 else 1 - own) * count
                    for j, terms in enumerate(energies):
                        if terms:
                            value = total[rows, where + j, :]
                            for ref, row in terms:
                                value = value + refs[ref][row, rows]
                            total[rows, where + j, :] = value

        pltpu.make_async_copy(total.at[rows], out.at[rows], sem).start()

    pltpu.make_async_copy(total, out, sem).wait()


def gathered(layout, count, arrays, before=()):
    terms = [[[(arrays.index(x), row) for x, row in entry] for entry in energies] for energies in layout]
    out_rows, order = arrays[0].shape[1:]
    arrays = list(arrays) + list(before)
    shape = (out_rows, 2 * count, order)
    size = 4 * sum(x.size for x in arrays) + 4 * 2 * count * out_rows * order
    vmem = pl.BlockSpec(memory_space=pltpu.VMEM)
    if before:
        kernel = functools.partial(gather_late, terms, count, len(before))
        scratch = [pltpu.VMEM(shape, jnp.float32), pltpu.SemaphoreType.DMA]
    else:
        kernel, scratch = functools.partial(gather_early, terms, count), []
    return pl.pallas_call(
        kernel,
        out_shape=jax.ShapeDtypeStruct(shape, jnp.float32),
        in_specs=[vmem] * len(arrays),
        out_specs=pl.BlockSpec(memory_space=pltpu.HBM) if before else vmem,
        scratch_shapes=scratch,
        cost_estimate=pl.CostEstimate(flops=size // 4, bytes_accessed=size, transcendentals=0),
    )(*arrays)


class Terms(list):
    def index(self, x):
        return next(i for i, y in enumerate(self) if y is x)


def shards(green, couplings, occupation, offsets, owners):
    momenta_here, edev, brows, order = green.shape
    n, atoms, cores = lax.axis_size("energy"), lax.axis_size("atom"), lax.axis_size("kz")
    momenta = momenta_here * cores
    grid_total = n * edev
    parts = lax.axis_size("grp")
    _, core, part = (lax.axis_index(a) for a in ("atom", "kz", "grp"))
    line = n == 2 * REACH
    half = edev // cores
    swap = [(i, (i + 1) % cores) for i in range(cores)]
    around = [[(i, (i + s) % atoms) for i in range(atoms)] for s in range(atoms)]

    size = brows // PIECES

    def summed(theirs, piece, *more):
        return pl.pallas_call(
            functools.partial(add_momenta, theirs, piece * size),
            out_shape=jax.ShapeDtypeStruct((half, size, order), jnp.float32),
            in_specs=[pl.BlockSpec(memory_space=pltpu.HBM)] * (1 + len(more)),
            out_specs=pl.BlockSpec(memory_space=pltpu.HBM),
            scratch_shapes=[
                pltpu.VMEM((half, momenta_here + len(more), size, order), jnp.float32),
                pltpu.VMEM((half, size, order), jnp.float32),
                pltpu.SemaphoreType.DMA((half,)),
                pltpu.SemaphoreType.DMA((half,)),
            ],
            compiler_params=pltpu.CompilerParams(vmem_limit_bytes=67_000_000),
            cost_estimate=pl.CostEstimate(
                flops=momenta_here * half * size * order,
                bytes_accessed=4 * (momenta_here + 1 + len(more)) * half * size * order,
                transcendentals=0,
            ),
            name="add_momenta",
        )(green, *more)

    own = []
    for piece in range(PIECES):
        given = summed(True, piece)
        given = lax.ppermute(given, "kz", swap)
        own.append(summed(False, piece, given))

    if line:
        up = [[(i, i + 1) for i in range(d, n - 1)] for d in range(REACH)]
        down = [[(i, i - 1) for i in range(n - 1 - d, 0, -1)] for d in range(REACH)]
    else:
        up = [[(i, (i + 1) % n) for i in range(n)]] * REACH
        down = [[(i, (i - 1) % n) for i in range(n)]] * REACH
    streams = {0: own}
    for d in range(1, REACH + 1):
        streams[-d] = [lax.ppermute(x, "energy", up[d - 1]) for x in streams[1 - d]]
        streams[d] = [lax.ppermute(x, "energy", down[d - 1]) for x in streams[d - 1]]
    groups = []
    for d in range(-REACH, REACH + 1):
        axes, pairs = "kz", swap
        if line and abs(d) == REACH:
            axes = ("energy", "kz")
            pairs = [
                (i * cores + k, i * cores + (k + 1) % cores) for i in range(n) if 0 <= i + d < n for k in range(cores)
            ]
        groups.append((streams[d], [lax.ppermute(x, axes, pairs) for x in streams[d]]))

    table_rows = couplings.shape[0]
    strip = order // (cores * parts)
    mine = lax.dynamic_slice(couplings, (0, (part * cores + core) * strip, 0), (table_rows, strip, order))
    others = []
    for s in range(1, atoms):
        got = lax.ppermute(mine, "atom", around[s])
        ahead = [got] + [
            lax.ppermute(got, "grp", [(i, (i + d) % parts) for i in range(parts)]) for d in range(1, parts)
        ]
        others.append([(x, lax.ppermute(x, "kz", swap)) for x in ahead])
    out_rows = order // (atoms * cores)
    flat = [x for pieces in others for both in pieces for x in both]
    hbm, vmem = pl.BlockSpec(memory_space=pltpu.HBM), pl.BlockSpec(memory_space=pltpu.VMEM)
    shapes = [(order, order), (order, order), (cores * out_rows, 3 * order), (order, 3 * brows)]
    *right, left_far, left_near = pl.pallas_call(
        functools.partial(prepare, atoms, parts, cores),
        out_shape=[jax.ShapeDtypeStruct((MODES,) + shape, jnp.bfloat16) for shape in shapes],
        in_specs=[pl.BlockSpec(memory_space=pltpu.SMEM)] + [hbm] * (1 + len(flat)),
        out_specs=[vmem] * len(shapes),
        scratch_shapes=[pltpu.VMEM((MODES, order, order), jnp.float32), pltpu.SemaphoreType.DMA((MODES,))],
        compiler_params=pltpu.CompilerParams(vmem_limit_bytes=32 << 20),
        cost_estimate=pl.CostEstimate(
            flops=8 * MODES * order * order, bytes_accessed=10 * MODES * order * order, transcendentals=0
        ),
        name="prepare",
    )(owners, couplings, *flat)

    beyond = []
    if line:
        got = [lax.ppermute(x, "atom", around[s]) for s in range(1, atoms) for x in own]
        whole = (
            list(own) + got,
            groups[REACH][1] + [lax.ppermute(x, "kz", swap) for x in got],
        )
        smem = pl.BlockSpec(memory_space=pltpu.SMEM)
        held = pl.pallas_call(
            guard,
            out_shape=jax.ShapeDtypeStruct(offsets.shape, offsets.dtype),
            in_specs=[smem],
            out_specs=smem,
            name="guard",
        )(offsets)
        sums = sandwich(
            held, occupation, right, left_far, [whole], atoms, momenta, 0, grid_total, edev, True, line, out_rows, half
        )
        swapped = lax.ppermute(sums[1], "kz", swap)
        both = jnp.concatenate(
            [jnp.where(core == 0, sums[0], swapped), jnp.where(core == 0, swapped, sums[0])], 0
        ).swapaxes(0, 1)
        beyond.append(lax.ppermute(both, "energy", [(0, n - 1), (n - 1, 0)]))

    terms = [[[] for _ in range(atoms)] for _ in range(cores)]
    base = 0
    for count in chunks_of(half):
        sums = sandwich(
            offsets, occupation, right, left_near, groups, atoms, momenta, base, grid_total, edev, False, line, out_rows, count
        )
        base += count
        for s in range(atoms - 1, -1, -1):
            for t in range(cores):
                block = sums[s * cores + t]
                if s or t:
                    pairs = [
                        (i * cores + k, ((i + s) % atoms) * cores + (k + t) % cores)
                        for i in range(atoms)
                        for k in range(cores)
                    ]
                    block = lax.ppermute(block, ("atom", "kz"), pairs)
                terms[t][s].append(block)
    chunks = chunks_of(half)
    entries = [[[] for _ in range(half)] for _ in range(cores)]
    late = [[[] for _ in range(half)] for _ in range(cores)]
    early, last = Terms(), Terms()
    for t in range(cores):
        for s in range(atoms):
            first = 0
            for chunk, block in enumerate(terms[t][s]):
                held = (last, late) if s and chunk == len(chunks) - 1 else (early, entries)
                held[0].append(block)
                for row in range(chunks[chunk]):
                    held[1][t][first + row].append((block, row))
                first += chunks[chunk]
    total = gathered(entries, half, early)
    return gathered(late, half, last, [total] + beyond)


def solution(mesh):
    return jax.shard_map(
        shards,
        mesh=mesh,
        in_specs=(P(("grp", "kz"), "energy", "atom", None), P("atom", None, None), P(), P(), P()),
        out_specs=P(("grp", "atom", "kz"), "energy", None),
        check_vma=False,
    )
```

```python
import functools

import jax
import jax.numpy as jnp
from jax import lax
from jax.experimental import pallas as pl
from jax.experimental.pallas import tpu as pltpu
from jax.sharding import PartitionSpec as P


MODES = 3
REACH = 2
PIECES = 2


def chunks_of(half):
    return [1] * half


def halves(x):
    high = x.astype(jnp.bfloat16)
    return high, (x - high.astype(jnp.float32)).astype(jnp.bfloat16)


def side_by_side(out, mode, x):
    high, low = halves(x)
    depth = x.shape[1]
    out[mode, :, pl.ds(0, depth)] = high
    out[mode, :, pl.ds(depth, depth)] = high
    out[mode, :, pl.ds(2 * depth, depth)] = low


def prepare(atoms, parts, cores, owners, couplings, *refs):
    right_high, right_low, far, near, held, sems = refs[-6:]
    pieces = refs[:-6]
    atom, core, part = (lax.axis_index(a) for a in ("atom", "kz", "grp"))
    table_rows = couplings.shape[0]
    for mode in range(MODES):
        row = lax.rem(owners[mode], table_rows)
        behind = lax.rem(atom - lax.div(owners[mode], table_rows) + atoms, atoms)

        @pl.when(behind == 0)
        def _(mode=mode, row=row):
            pltpu.make_async_copy(couplings.at[row], held.at[mode], sems.at[mode]).start()

        for s in range(1, atoms):

            @pl.when(behind == s)
            def _(mode=mode, row=row, s=s):
                for d in range(parts):
                    for o in range(cores):
                        piece = pieces[((s - 1) * parts + d) * cores + o]
                        strip = piece.shape[1]
                        at = lax.rem(part - d + parts, parts) * cores + lax.rem(core - o + cores, cores)
                        rows = pl.ds(pl.multiple_of(at * strip, 8), strip)
                        pltpu.make_async_copy(piece.at[row], held.at[mode, rows], sems.at[mode]).start()

    @pl.loop(0, MODES)
    def _(mode):
        pltpu.make_async_copy(held.at[mode], held.at[mode], sems.at[mode]).wait()
        right_high[mode], right_low[mode] = halves(held[mode].T)
        rows, depth = far.shape[1], near.shape[2] // 3
        side_by_side(far, mode, held[mode, pl.ds(pl.multiple_of(atom * rows, 8), rows), :])
        side_by_side(near, mode, held[mode, :, pl.ds(pl.multiple_of(atom * depth, 128), depth)])


def guard(steps, out):
    for mode in range(MODES):
        out[mode] = steps[mode]


def add_momenta(theirs, first, green, *refs):
    out, held, total, arrived, left = refs[-5:]
    given = refs[:-5]
    momenta, count, size = green.shape[0], held.shape[0], held.shape[2]
    core = lax.axis_index("kz")
    base = (1 - core if theirs else core) * count
    for e in range(count):
        for k in range(momenta):
            pltpu.make_async_copy(green.at[k, base + e, pl.ds(first, size)], held.at[e, k], arrived.at[e]).start()
        for ref in given:
            pltpu.make_async_copy(ref.at[e], held.at[e, momenta], arrived.at[e]).start()

    @pl.loop(0, count)
    def _(e):
        pltpu.make_async_copy(held.at[e], held.at[e], arrived.at[e]).wait()
        value = held[e, 0]
        for k in range(1, held.shape[1]):
            value = value + held[e, k]
        total[e] = value
        pltpu.make_async_copy(total.at[e], out.at[e], left.at[e]).start()

    for e in range(count):
        pltpu.make_async_copy(total.at[e], out.at[e], left.at[e]).wait()


def split_dot(n_groups, n_parts, n_atoms, momenta, base, grid_total, edev, far, line, steps, occupation, right_high, right_low, left, *refs):
    sources = [
        [refs[(g * 2 + h) * n_parts : (g * 2 + h + 1) * n_parts] for h in range(2)]
        for g in range(n_groups)
    ]
    outs = refs[n_groups * 2 * n_parts : -3]
    planes, inner, sems = refs[-3:]
    count, size = outs[0].shape[:2]
    rows = planes.shape[2]
    half_planes = edev // 2
    place, core, atom = (lax.axis_index(a) for a in ("energy", "kz", "atom"))
    blocks = grid_total // edev
    target = blocks - 1 - place if far else place
    base = base + core * half_planes

    def source_of(energy, mode, side):
        step = steps[mode] if side == 0 else -steps[mode]
        source = lax.rem(target * edev + base + energy + step + grid_total, grid_total)
        rel = lax.div(source, edev) - place
        if far:
            valid = rel == 0
        elif line:
            valid = jnp.abs(rel) <= REACH
        else:
            rel = lax.rem(rel + REACH + blocks, blocks) - REACH
            valid = rel <= REACH
        group = jnp.where(valid, rel + n_groups // 2, n_groups // 2)
        return valid, group, lax.rem(source, edev)

    def fetch(energy, buffer):
        for mode in range(MODES):
            for side in range(2):
                _, group, plane = source_of(energy, mode, side)
                other = jnp.where(lax.div(plane, half_planes) == core, 0, 1)
                at = lax.rem(plane, half_planes)
                slot = mode * 2 + side
                for g in range(n_groups):

                    @pl.when(group == g)
                    def _(g=g, at=at, slot=slot, other=other):
                        for h in range(2):

                            @pl.when(other == h)
                            def _(h=h):
                                first = 0
                                for ref in sources[g][h]:
                                    depth = ref.shape[1]
                                    start = first
                                    if far:
                                        per = rows // n_atoms
                                        behind = lax.rem(atom - first // per + n_atoms, n_atoms)
                                        start = pl.multiple_of(behind * per + first % per, 8)
                                    pltpu.make_async_copy(
                                        ref.at[at], planes.at[buffer, slot, pl.ds(start, depth)], sems.at[buffer, slot]
                                    ).start()
                                    first += depth

    fetch(0, 0)

    @pl.loop(0, count)
    def _(energy):
        buffer = lax.rem(energy, 2)

        if count > 1:

            @pl.when(energy + 1 < count)
            def _():
                fetch(energy + 1, 1 - buffer)

        dot = functools.partial(jnp.dot, preferred_element_type=jnp.float32)
        for mode in range(MODES):
            scales = []
            for side in range(2):
                slot = mode * 2 + side
                held = planes.at[buffer, slot]
                pltpu.make_async_copy(held, held, sems.at[buffer, slot]).wait()
                scales.append(jnp.where(source_of(energy, mode, side)[0], (occupation[mode] + (1.0 - side)) * (1.0 / momenta), 0.0))
            combined = scales[0] * planes[buffer, 2 * mode] + scales[1] * planes[buffer, 2 * mode + 1]
            high = combined.astype(jnp.bfloat16)
            low = (combined - high.astype(jnp.float32)).astype(jnp.bfloat16)
            product = dot(high, right_high[mode]) + dot(low, right_high[mode]) + dot(high, right_low[mode])
            high = product.astype(jnp.bfloat16)
            low = (product - high.astype(jnp.float32)).astype(jnp.bfloat16)
            inner[mode, pl.ds(0, rows)] = high
            inner[mode, pl.ds(rows, rows)] = low
            inner[mode, pl.ds(2 * rows, rows)] = high
        for index, out in enumerate(outs):
            s, t = index // 2, index % 2
            block = lax.rem(core + t, 2)
            if not far:
                block = block + 2 * lax.rem(atom + s, n_atoms)
            where = pl.ds(pl.multiple_of(block * size, 8), size)
            total = dot(left[0, where], inner[0])
            for mode in range(1, MODES):
                total = total + dot(left[mode, where], inner[mode])
            out[energy] = total


def sandwich(steps, occupation, right, left, groups, n_atoms, momenta, base, grid_total, edev, far, line, out_rows, count):
    order = right[0].shape[-1]
    flat = [part for group in groups for half in group for part in half]
    rows = sum(part.shape[1] for part in groups[0][0])
    n_out = left.shape[1] // out_rows
    buffers = min(count, 2)
    held = 4 * (2 * MODES * buffers + 6) * rows * order + 2 * 3 * MODES * rows * order + (6 << 20)
    held += 4 * left.shape[1] * order * (count + 3) + 4 * MODES * order * order + 2 * left.size
    flops = count * 2 * 3 * MODES * (rows * order * order + left.shape[1] * rows * order)
    return pl.pallas_call(
        functools.partial(split_dot, len(groups), len(groups[0][0]), n_atoms, momenta, base, grid_total, edev, far, line),
        out_shape=[jax.ShapeDtypeStruct((count, out_rows, order), jnp.float32)] * n_out,
        in_specs=[pl.BlockSpec(memory_space=pltpu.SMEM)] * 2
        + [pl.BlockSpec(memory_space=pltpu.VMEM)] * 3
        + [pl.BlockSpec(memory_space=pltpu.HBM)] * len(flat),
        out_specs=[pl.BlockSpec(memory_space=pltpu.VMEM)] * n_out,
        scratch_shapes=[
            pltpu.VMEM((buffers, 2 * MODES, rows, order), jnp.float32),
            pltpu.VMEM((MODES, 3 * rows, order), jnp.bfloat16),
            pltpu.SemaphoreType.DMA((2, 2 * MODES)),
        ],
        compiler_params=pltpu.CompilerParams(vmem_limit_bytes=held),
        cost_estimate=pl.CostEstimate(
            flops=flops,
            bytes_accessed=count * 4 * (2 * MODES * rows * order + left.shape[1] * order),
            transcendentals=0,
        ),
        name="far_sandwich" if far else "near_sandwich",
    )(steps, occupation, right[0], right[1], left, *flat)


def gather_early(layout, count, *refs):
    out = refs[-1]
    core = lax.axis_index("kz")
    group = 16
    for own in range(2):

        @pl.when(core == own)
        def _(own=own):
            @pl.loop(0, out.shape[0] // group)
            def _(at):
                rows = pl.ds(pl.multiple_of(at * group, group), group)
                for half, energies in enumerate(layout):
                    where = (own if half == 0 else 1 - own) * count
                    for j, terms in enumerate(energies):
                        total = None
                        for ref, row in terms:
                            total = refs[ref][row, rows] if total is None else total + refs[ref][row, rows]
                        out[rows, where + j, :] = total


def gather_late(layout, count, whole, *refs):
    out, total, sem = refs[-3:]
    full = refs[-3 - whole : -3]
    core = lax.axis_index("kz")
    group = 16

    @pl.loop(0, total.shape[0] // group)
    def _(at):
        rows = pl.ds(pl.multiple_of(at * group, group), group)
        value = full[0][rows]
        for ref in full[1:]:
            value = value + ref[rows]
        total[rows] = value
        for own in range(2):

            @pl.when(core == own)
            def _(own=own):
                for half, energies in enumerate(layout):
                    where = (own if half == 0 else 1 - own) * count
                    for j, terms in enumerate(energies):
                        if terms:
                            value = total[rows, where + j, :]
                            for ref, row in terms:
                                value = value + refs[ref][row, rows]
                            total[rows, where + j, :] = value

        pltpu.make_async_copy(total.at[rows], out.at[rows], sem).start()

    pltpu.make_async_copy(total, out, sem).wait()


def gathered(layout, count, arrays, before=()):
    terms = [[[(arrays.index(x), row) for x, row in entry] for entry in energies] for energies in layout]
    out_rows, order = arrays[0].shape[1:]
    arrays = list(arrays) + list(before)
    shape = (out_rows, 2 * count, order)
    size = 4 * sum(x.size for x in arrays) + 4 * 2 * count * out_rows * order
    vmem = pl.BlockSpec(memory_space=pltpu.VMEM)
    if before:
        kernel = functools.partial(gather_late, terms, count, len(before))
        scratch = [pltpu.VMEM(shape, jnp.float32), pltpu.SemaphoreType.DMA]
    else:
        kernel, scratch = functools.partial(gather_early, terms, count), []
    return pl.pallas_call(
        kernel,
        out_shape=jax.ShapeDtypeStruct(shape, jnp.float32),
        in_specs=[vmem] * len(arrays),
        out_specs=pl.BlockSpec(memory_space=pltpu.HBM) if before else vmem,
        scratch_shapes=scratch,
        compiler_params=pltpu.CompilerParams(vmem_limit_bytes=8 << 20),
        cost_estimate=pl.CostEstimate(flops=size // 4, bytes_accessed=size, transcendentals=0),
    )(*arrays)


class Terms(list):
    def index(self, x):
        return next(i for i, y in enumerate(self) if y is x)


def shards(green, couplings, occupation, offsets, owners):
    momenta_here, edev, brows, order = green.shape
    n, atoms, cores = lax.axis_size("energy"), lax.axis_size("atom"), lax.axis_size("kz")
    momenta = momenta_here * cores
    grid_total = n * edev
    parts = lax.axis_size("grp")
    _, core, part = (lax.axis_index(a) for a in ("atom", "kz", "grp"))
    line = n == 2 * REACH
    half = edev // cores
    swap = [(i, (i + 1) % cores) for i in range(cores)]
    around = [[(i, (i + s) % atoms) for i in range(atoms)] for s in range(atoms)]

    size = brows // PIECES

    def summed(theirs, piece, *more):
        return pl.pallas_call(
            functools.partial(add_momenta, theirs, piece * size),
            out_shape=jax.ShapeDtypeStruct((half, size, order), jnp.float32),
            in_specs=[pl.BlockSpec(memory_space=pltpu.HBM)] * (1 + len(more)),
            out_specs=pl.BlockSpec(memory_space=pltpu.HBM),
            scratch_shapes=[
                pltpu.VMEM((half, momenta_here + len(more), size, order), jnp.float32),
                pltpu.VMEM((half, size, order), jnp.float32),
                pltpu.SemaphoreType.DMA((half,)),
                pltpu.SemaphoreType.DMA((half,)),
            ],
            compiler_params=pltpu.CompilerParams(vmem_limit_bytes=67_000_000),
            cost_estimate=pl.CostEstimate(
                flops=momenta_here * half * size * order,
                bytes_accessed=4 * (momenta_here + 1 + len(more)) * half * size * order,
                transcendentals=0,
            ),
            name="add_momenta",
        )(green, *more)

    own = []
    for piece in range(PIECES):
        given = summed(True, piece)
        given = lax.ppermute(given, "kz", swap)
        own.append(summed(False, piece, given))

    if line:
        up = [[(i, i + 1) for i in range(d, n - 1)] for d in range(REACH)]
        down = [[(i, i - 1) for i in range(n - 1 - d, 0, -1)] for d in range(REACH)]
    else:
        up = [[(i, (i + 1) % n) for i in range(n)]] * REACH
        down = [[(i, (i - 1) % n) for i in range(n)]] * REACH
    streams = {0: own}
    for d in range(1, REACH + 1):
        streams[-d] = [lax.ppermute(x, "energy", up[d - 1]) for x in streams[1 - d]]
        streams[d] = [lax.ppermute(x, "energy", down[d - 1]) for x in streams[d - 1]]
    groups = []
    for d in range(-REACH, REACH + 1):
        axes, pairs = "kz", swap
        if line and abs(d) == REACH:
            axes = ("energy", "kz")
            pairs = [
                (i * cores + k, i * cores + (k + 1) % cores) for i in range(n) if 0 <= i + d < n for k in range(cores)
            ]
        groups.append((streams[d], [lax.ppermute(x, axes, pairs) for x in streams[d]]))

    table_rows = couplings.shape[0]
    strip = order // (cores * parts)
    mine = lax.dynamic_slice(couplings, (0, (part * cores + core) * strip, 0), (table_rows, strip, order))
    others = []
    for s in range(1, atoms):
        got = lax.ppermute(mine, "atom", around[s])
        ahead = [got] + [
            lax.ppermute(got, "grp", [(i, (i + d) % parts) for i in range(parts)]) for d in range(1, parts)
        ]
        others.append([(x, lax.ppermute(x, "kz", swap)) for x in ahead])
    out_rows = order // (atoms * cores)
    flat = [x for pieces in others for both in pieces for x in both]
    hbm, vmem = pl.BlockSpec(memory_space=pltpu.HBM), pl.BlockSpec(memory_space=pltpu.VMEM)
    shapes = [(order, order), (order, order), (cores * out_rows, 3 * order), (order, 3 * brows)]
    *right, left_far, left_near = pl.pallas_call(
        functools.partial(prepare, atoms, parts, cores),
        out_shape=[jax.ShapeDtypeStruct((MODES,) + shape, jnp.bfloat16) for shape in shapes],
        in_specs=[pl.BlockSpec(memory_space=pltpu.SMEM)] + [hbm] * (1 + len(flat)),
        out_specs=[vmem] * len(shapes),
        scratch_shapes=[pltpu.VMEM((MODES, order, order), jnp.float32), pltpu.SemaphoreType.DMA((MODES,))],
        compiler_params=pltpu.CompilerParams(vmem_limit_bytes=32 << 20),
        cost_estimate=pl.CostEstimate(
            flops=8 * MODES * order * order, bytes_accessed=10 * MODES * order * order, transcendentals=0
        ),
        name="prepare",
    )(owners, couplings, *flat)

    beyond = []
    if line:
        got = [lax.ppermute(x, "atom", around[s]) for s in range(1, atoms) for x in own]
        whole = (
            list(own) + got,
            groups[REACH][1] + [lax.ppermute(x, "kz", swap) for x in got],
        )
        smem = pl.BlockSpec(memory_space=pltpu.SMEM)
        held = pl.pallas_call(
            guard,
            out_shape=jax.ShapeDtypeStruct(offsets.shape, offsets.dtype),
            in_specs=[smem],
            out_specs=smem,
            compiler_params=pltpu.CompilerParams(vmem_limit_bytes=1 << 20),
            name="guard",
        )(offsets)
        sums = sandwich(
            held, occupation, right, left_far, [whole], atoms, momenta, 0, grid_total, edev, True, line, out_rows, half
        )
        swapped = lax.ppermute(sums[1], "kz", swap)
        both = jnp.concatenate(
            [jnp.where(core == 0, sums[0], swapped), jnp.where(core == 0, swapped, sums[0])], 0
        ).swapaxes(0, 1)
        beyond.append(lax.ppermute(both, "energy", [(0, n - 1)]))
        beyond.append(lax.ppermute(both, "energy", [(n - 1, 0)]))

    terms = [[[] for _ in range(atoms)] for _ in range(cores)]
    base = 0
    for count in chunks_of(half):
        sums = sandwich(
            offsets, occupation, right, left_near, groups, atoms, momenta, base, grid_total, edev, False, line, out_rows, count
        )
        base += count
        for s in range(atoms - 1, -1, -1):
            for t in range(cores):
                block = sums[s * cores + t]
                if s or t:
                    pairs = [
                        (i * cores + k, ((i + s) % atoms) * cores + (k + t) % cores)
                        for i in range(atoms)
                        for k in range(cores)
                    ]
                    block = lax.ppermute(block, ("atom", "kz"), pairs)
                terms[t][s].append(block)
    chunks = chunks_of(half)
    entries = [[[] for _ in range(half)] for _ in range(cores)]
    late = [[[] for _ in range(half)] for _ in range(cores)]
    early, last = Terms(), Terms()
    for t in range(cores):
        for s in range(atoms):
            first = 0
            for chunk, block in enumerate(terms[t][s]):
                held = (last, late) if s and chunk == len(chunks) - 1 else (early, entries)
                held[0].append(block)
                for row in range(chunks[chunk]):
                    held[1][t][first + row].append((block, row))
                first += chunks[chunk]
    total = gathered(entries, half, early)
    return gathered(late, half, last, [total] + beyond)


def solution(mesh):
    return jax.shard_map(
        shards,
        mesh=mesh,
        in_specs=(P(("grp", "kz"), "energy", "atom", None), P("atom", None, None), P(), P(), P()),
        out_specs=P(("grp", "atom", "kz"), "energy", None),
        check_vma=False,
    )
```

```python
import functools

import jax
import jax.numpy as jnp
from jax import lax
from jax.experimental import pallas as pl
from jax.experimental.pallas import tpu as pltpu
from jax.sharding import PartitionSpec as P


MODES = 3
REACH = 2
PIECES = 2


def chunks_of(half):
    return [1] * half


def halves(x):
    high = x.astype(jnp.bfloat16)
    return high, (x - high.astype(jnp.float32)).astype(jnp.bfloat16)


def side_by_side(out, mode, x):
    high, low = halves(x)
    depth = x.shape[1]
    out[mode, :, pl.ds(0, depth)] = high
    out[mode, :, pl.ds(depth, depth)] = high
    out[mode, :, pl.ds(2 * depth, depth)] = low


def prepare(atoms, parts, cores, owners, couplings, *refs):
    right_high, right_low, far, near, held, sems = refs[-6:]
    pieces = refs[:-6]
    atom, core, part = (lax.axis_index(a) for a in ("atom", "kz", "grp"))
    table_rows = couplings.shape[0]
    for mode in range(MODES):
        row = lax.rem(owners[mode], table_rows)
        behind = lax.rem(atom - lax.div(owners[mode], table_rows) + atoms, atoms)

        @pl.when(behind == 0)
        def _(mode=mode, row=row):
            pltpu.make_async_copy(couplings.at[row], held.at[mode], sems.at[mode]).start()

        for s in range(1, atoms):

            @pl.when(behind == s)
            def _(mode=mode, row=row, s=s):
                for d in range(parts):
                    for o in range(cores):
                        piece = pieces[((s - 1) * parts + d) * cores + o]
                        strip = piece.shape[1]
                        at = lax.rem(part - d + parts, parts) * cores + lax.rem(core - o + cores, cores)
                        rows = pl.ds(pl.multiple_of(at * strip, 8), strip)
                        pltpu.make_async_copy(piece.at[row], held.at[mode, rows], sems.at[mode]).start()

    @pl.loop(0, MODES)
    def _(mode):
        pltpu.make_async_copy(held.at[mode], held.at[mode], sems.at[mode]).wait()
        right_high[mode], right_low[mode] = halves(held[mode].T)
        rows, depth = far.shape[1], near.shape[2] // 3
        side_by_side(far, mode, held[mode, pl.ds(pl.multiple_of(atom * rows, 8), rows), :])
        side_by_side(near, mode, held[mode, :, pl.ds(pl.multiple_of(atom * depth, 128), depth)])


def guard(steps, out):
    for mode in range(MODES):
        out[mode] = steps[mode]


def add_momenta(theirs, first, green, *refs):
    out, held, total, arrived, left = refs[-5:]
    given = refs[:-5]
    if theirs:
        total = out
    momenta, count, size = green.shape[0], held.shape[0], held.shape[2]
    core = lax.axis_index("kz")
    base = (1 - core if theirs else core) * count
    for e in range(count):
        for k in range(momenta):
            pltpu.make_async_copy(green.at[k, base + e, pl.ds(first, size)], held.at[e, k], arrived.at[e]).start()
        for ref in given:
            pltpu.make_async_copy(ref.at[e], held.at[e, momenta], arrived.at[e]).start()

    @pl.loop(0, count)
    def _(e):
        pltpu.make_async_copy(held.at[e], held.at[e], arrived.at[e]).wait()
        value = held[e, 0]
        for k in range(1, held.shape[1]):
            value = value + held[e, k]
        total[e] = value
        if not theirs:
            pltpu.make_async_copy(total.at[e], out.at[e], left.at[e]).start()

    for e in range(0 if theirs else count):
        pltpu.make_async_copy(total.at[e], out.at[e], left.at[e]).wait()


def split_dot(n_groups, n_parts, n_atoms, momenta, base, grid_total, edev, far, line, steps, occupation, right_high, right_low, left, *refs):
    sources = [
        [refs[(g * 2 + h) * n_parts : (g * 2 + h + 1) * n_parts] for h in range(2)]
        for g in range(n_groups)
    ]
    outs = refs[n_groups * 2 * n_parts : -4]
    planes, inner, total, sems = refs[-4:]
    count, size = outs[0].shape[:2]
    rows = planes.shape[2]
    half_planes = edev // 2
    place, core, atom = (lax.axis_index(a) for a in ("energy", "kz", "atom"))
    blocks = grid_total // edev
    target = blocks - 1 - place if far else place
    base = base + core * half_planes

    def source_of(energy, mode, side):
        step = steps[mode] if side == 0 else -steps[mode]
        source = lax.rem(target * edev + base + energy + step + grid_total, grid_total)
        rel = lax.div(source, edev) - place
        if far:
            valid = rel == 0
        elif line:
            valid = jnp.abs(rel) <= REACH
        else:
            rel = lax.rem(rel + REACH + blocks, blocks) - REACH
            valid = rel <= REACH
        group = jnp.where(valid, rel + n_groups // 2, n_groups // 2)
        return valid, group, lax.rem(source, edev)

    def fetch(energy, buffer):
        for mode in range(MODES):
            for side in range(2):
                _, group, plane = source_of(energy, mode, side)
                other = jnp.where(lax.div(plane, half_planes) == core, 0, 1)
                at = lax.rem(plane, half_planes)
                slot = mode * 2 + side
                for g in range(n_groups):

                    @pl.when(group == g)
                    def _(g=g, at=at, slot=slot, other=other):
                        for h in range(2):

                            @pl.when(other == h)
                            def _(h=h):
                                first = 0
                                for ref in sources[g][h]:
                                    depth = ref.shape[1]
                                    start = first
                                    if far:
                                        per = rows // n_atoms
                                        behind = lax.rem(atom - first // per + n_atoms, n_atoms)
                                        start = pl.multiple_of(behind * per + first % per, 8)
                                    pltpu.make_async_copy(
                                        ref.at[at], planes.at[buffer, slot, pl.ds(start, depth)], sems.at[buffer, slot]
                                    ).start()
                                    first += depth

    fetch(0, 0)

    @pl.loop(0, count)
    def _(energy):
        buffer = lax.rem(energy, 2)

        if count > 1:

            @pl.when(energy + 1 < count)
            def _():
                fetch(energy + 1, 1 - buffer)

        dot = functools.partial(jnp.dot, preferred_element_type=jnp.float32)
        for mode in range(MODES):
            scales = []
            for side in range(2):
                slot = mode * 2 + side
                held = planes.at[buffer, slot]
                pltpu.make_async_copy(held, held, sems.at[buffer, slot]).wait()
                scales.append(jnp.where(source_of(energy, mode, side)[0], (occupation[mode] + (1.0 - side)) * (1.0 / momenta), 0.0))
            combined = scales[0] * planes[buffer, 2 * mode] + scales[1] * planes[buffer, 2 * mode + 1]
            if far:
                high, low = halves(combined)
                inner[mode, pl.ds(0, rows)] = high
                inner[mode, pl.ds(rows, rows)] = low
                inner[mode, pl.ds(2 * rows, rows)] = high
                high, low = halves(dot(left[mode], inner[mode]))
                term = dot(high, right_high[mode]) + dot(low, right_high[mode]) + dot(high, right_low[mode])
                total[...] = term if mode == 0 else total[...] + term
                continue
            high = combined.astype(jnp.bfloat16)
            low = (combined - high.astype(jnp.float32)).astype(jnp.bfloat16)
            product = dot(high, right_high[mode]) + dot(low, right_high[mode]) + dot(high, right_low[mode])
            high = product.astype(jnp.bfloat16)
            low = (product - high.astype(jnp.float32)).astype(jnp.bfloat16)
            inner[mode, pl.ds(0, rows)] = high
            inner[mode, pl.ds(rows, rows)] = low
            inner[mode, pl.ds(2 * rows, rows)] = high
        for index, out in enumerate(outs):
            s, t = index // 2, index % 2
            block = lax.rem(core + t, 2)
            if far:
                out[energy] = total[pl.ds(pl.multiple_of(block * size, 8), size)]
                continue
            block = block + 2 * lax.rem(atom + s, n_atoms)
            where = pl.ds(pl.multiple_of(block * size, 8), size)
            result = dot(left[0, where], inner[0])
            for mode in range(1, MODES):
                result = result + dot(left[mode, where], inner[mode])
            out[energy] = result


def sandwich(steps, occupation, right, left, groups, n_atoms, momenta, base, grid_total, edev, far, line, out_rows, count):
    order = right[0].shape[-1]
    flat = [part for group in groups for half in group for part in half]
    rows = sum(part.shape[1] for part in groups[0][0])
    n_out = left.shape[1] // out_rows
    buffers = min(count, 2)
    held = 4 * (2 * MODES * buffers + 6) * rows * order + 2 * 3 * MODES * rows * order + (6 << 20)
    held += 4 * left.shape[1] * order * (count + 3) + 4 * MODES * order * order + 2 * left.size
    flops = count * 2 * 3 * MODES * (rows * order * order + left.shape[1] * rows * order)
    return pl.pallas_call(
        functools.partial(split_dot, len(groups), len(groups[0][0]), n_atoms, momenta, base, grid_total, edev, far, line),
        out_shape=[jax.ShapeDtypeStruct((count, out_rows, order), jnp.float32)] * n_out,
        in_specs=[pl.BlockSpec(memory_space=pltpu.SMEM)] * 2
        + [pl.BlockSpec(memory_space=pltpu.VMEM)] * 3
        + [pl.BlockSpec(memory_space=pltpu.HBM)] * len(flat),
        out_specs=[pl.BlockSpec(memory_space=pltpu.VMEM)] * n_out,
        scratch_shapes=[
            pltpu.VMEM((buffers, 2 * MODES, rows, order), jnp.float32),
            pltpu.VMEM((MODES, 3 * rows, order), jnp.bfloat16),
            pltpu.VMEM((left.shape[1] if far else 8, order), jnp.float32),
            pltpu.SemaphoreType.DMA((2, 2 * MODES)),
        ],
        compiler_params=pltpu.CompilerParams(vmem_limit_bytes=held),
        cost_estimate=pl.CostEstimate(
            flops=flops,
            bytes_accessed=count * 4 * (2 * MODES * rows * order + left.shape[1] * order),
            transcendentals=0,
        ),
        name="far_sandwich" if far else "near_sandwich",
    )(steps, occupation, right[0], right[1], left, *flat)


def gather_early(layout, count, *refs):
    out = refs[-1]
    core = lax.axis_index("kz")
    group = 16
    for own in range(2):

        @pl.when(core == own)
        def _(own=own):
            @pl.loop(0, out.shape[0] // group)
            def _(at):
                rows = pl.ds(pl.multiple_of(at * group, group), group)
                for half, energies in enumerate(layout):
                    where = (own if half == 0 else 1 - own) * count
                    for j, terms in enumerate(energies):
                        total = None
                        for ref, row in terms:
                            total = refs[ref][row, rows] if total is None else total + refs[ref][row, rows]
                        out[rows, where + j, :] = total


def gather_late(layout, count, whole, *refs):
    out, total, sem = refs[-3:]
    full = refs[-3 - whole : -3]
    core = lax.axis_index("kz")
    group = 16

    @pl.loop(0, total.shape[0] // group)
    def _(at):
        rows = pl.ds(pl.multiple_of(at * group, group), group)
        value = full[0][rows]
        for ref in full[1:]:
            value = value + ref[rows]
        total[rows] = value
        for own in range(2):

            @pl.when(core == own)
            def _(own=own):
                for half, energies in enumerate(layout):
                    where = (own if half == 0 else 1 - own) * count
                    for j, terms in enumerate(energies):
                        if terms:
                            value = total[rows, where + j, :]
                            for ref, row in terms:
                                value = value + refs[ref][row, rows]
                            total[rows, where + j, :] = value

        pltpu.make_async_copy(total.at[rows], out.at[rows], sem).start()

    pltpu.make_async_copy(total, out, sem).wait()


def gathered(layout, count, arrays, before=()):
    terms = [[[(arrays.index(x), row) for x, row in entry] for entry in energies] for energies in layout]
    out_rows, order = arrays[0].shape[1:]
    arrays = list(arrays) + list(before)
    shape = (out_rows, 2 * count, order)
    size = 4 * sum(x.size for x in arrays) + 4 * 2 * count * out_rows * order
    vmem = pl.BlockSpec(memory_space=pltpu.VMEM)
    if before:
        kernel = functools.partial(gather_late, terms, count, len(before))
        scratch = [pltpu.VMEM(shape, jnp.float32), pltpu.SemaphoreType.DMA]
    else:
        kernel, scratch = functools.partial(gather_early, terms, count), []
    return pl.pallas_call(
        kernel,
        out_shape=jax.ShapeDtypeStruct(shape, jnp.float32),
        in_specs=[vmem] * len(arrays),
        out_specs=pl.BlockSpec(memory_space=pltpu.HBM) if before else vmem,
        scratch_shapes=scratch,
        compiler_params=pltpu.CompilerParams(vmem_limit_bytes=8 << 20),
        cost_estimate=pl.CostEstimate(flops=size // 4, bytes_accessed=size, transcendentals=0),
    )(*arrays)


class Terms(list):
    def index(self, x):
        return next(i for i, y in enumerate(self) if y is x)


def shards(green, couplings, occupation, offsets, owners):
    momenta_here, edev, brows, order = green.shape
    n, atoms, cores = lax.axis_size("energy"), lax.axis_size("atom"), lax.axis_size("kz")
    momenta = momenta_here * cores
    grid_total = n * edev
    parts = lax.axis_size("grp")
    _, core, part = (lax.axis_index(a) for a in ("atom", "kz", "grp"))
    line = n == 2 * REACH
    half = edev // cores
    swap = [(i, (i + 1) % cores) for i in range(cores)]
    around = [[(i, (i + s) % atoms) for i in range(atoms)] for s in range(atoms)]

    size = brows // PIECES

    def summed(theirs, piece, *more):
        return pl.pallas_call(
            functools.partial(add_momenta, theirs, piece * size),
            out_shape=jax.ShapeDtypeStruct((half, size, order), jnp.float32),
            in_specs=[pl.BlockSpec(memory_space=pltpu.HBM)] * (1 + len(more)),
            out_specs=pl.BlockSpec(memory_space=pltpu.VMEM if theirs else pltpu.HBM),
            scratch_shapes=[
                pltpu.VMEM((half, momenta_here + len(more), size, order), jnp.float32),
                pltpu.VMEM((8, order) if theirs else (half, size, order), jnp.float32),
                pltpu.SemaphoreType.DMA((half,)),
                pltpu.SemaphoreType.DMA((half,)),
            ],
            compiler_params=pltpu.CompilerParams(vmem_limit_bytes=8 << 20 if theirs else 67_000_000),
            cost_estimate=pl.CostEstimate(
                flops=momenta_here * half * size * order,
                bytes_accessed=4 * (momenta_here + 1 + len(more)) * half * size * order,
                transcendentals=0,
            ),
            name="add_momenta",
        )(green, *more)

    own = []
    for piece in range(PIECES):
        given = summed(True, piece)
        given = lax.ppermute(given, "kz", swap)
        own.append(summed(False, piece, given))

    if line:
        up = [[(i, i + 1) for i in range(d, n - 1)] for d in range(REACH)]
        down = [[(i, i - 1) for i in range(n - 1 - d, 0, -1)] for d in range(REACH)]
    else:
        up = [[(i, (i + 1) % n) for i in range(n)]] * REACH
        down = [[(i, (i - 1) % n) for i in range(n)]] * REACH
    streams = {0: own}
    for d in range(1, REACH + 1):
        streams[-d] = [lax.ppermute(x, "energy", up[d - 1]) for x in streams[1 - d]]
        streams[d] = [lax.ppermute(x, "energy", down[d - 1]) for x in streams[d - 1]]
    groups = []
    for d in range(-REACH, REACH + 1):
        axes, pairs = "kz", swap
        if line and abs(d) == REACH:
            axes = ("energy", "kz")
            pairs = [
                (i * cores + k, i * cores + (k + 1) % cores) for i in range(n) if 0 <= i + d < n for k in range(cores)
            ]
        groups.append((streams[d], [lax.ppermute(x, axes, pairs) for x in streams[d]]))

    table_rows = couplings.shape[0]
    strip = order // (cores * parts)
    mine = lax.dynamic_slice(couplings, (0, (part * cores + core) * strip, 0), (table_rows, strip, order))
    others = []
    for s in range(1, atoms):
        got = lax.ppermute(mine, "atom", around[s])
        ahead = [got] + [
            lax.ppermute(got, "grp", [(i, (i + d) % parts) for i in range(parts)]) for d in range(1, parts)
        ]
        others.append([(x, lax.ppermute(x, "kz", swap)) for x in ahead])
    out_rows = order // (atoms * cores)
    flat = [x for pieces in others for both in pieces for x in both]
    hbm, vmem = pl.BlockSpec(memory_space=pltpu.HBM), pl.BlockSpec(memory_space=pltpu.VMEM)
    shapes = [(order, order), (order, order), (cores * out_rows, 3 * order), (order, 3 * brows)]
    *right, left_far, left_near = pl.pallas_call(
        functools.partial(prepare, atoms, parts, cores),
        out_shape=[jax.ShapeDtypeStruct((MODES,) + shape, jnp.bfloat16) for shape in shapes],
        in_specs=[pl.BlockSpec(memory_space=pltpu.SMEM)] + [hbm] * (1 + len(flat)),
        out_specs=[vmem] * len(shapes),
        scratch_shapes=[pltpu.VMEM((MODES, order, order), jnp.float32), pltpu.SemaphoreType.DMA((MODES,))],
        compiler_params=pltpu.CompilerParams(vmem_limit_bytes=32 << 20),
        cost_estimate=pl.CostEstimate(
            flops=8 * MODES * order * order, bytes_accessed=10 * MODES * order * order, transcendentals=0
        ),
        name="prepare",
    )(owners, couplings, *flat)

    beyond = []
    if line:
        got = [lax.ppermute(x, "atom", around[s]) for s in range(1, atoms) for x in own]
        whole = (
            list(own) + got,
            groups[REACH][1] + [lax.ppermute(x, "kz", swap) for x in got],
        )
        smem = pl.BlockSpec(memory_space=pltpu.SMEM)
        held = pl.pallas_call(
            guard,
            out_shape=jax.ShapeDtypeStruct(offsets.shape, offsets.dtype),
            in_specs=[smem],
            out_specs=smem,
            compiler_params=pltpu.CompilerParams(vmem_limit_bytes=1 << 20),
            name="guard",
        )(offsets)
        sums = sandwich(
            held, occupation, right, left_far, [whole], atoms, momenta, 0, grid_total, edev, True, line, out_rows, half
        )
        swapped = lax.ppermute(sums[1], "kz", swap)
        both = jnp.concatenate(
            [jnp.where(core == 0, sums[0], swapped), jnp.where(core == 0, swapped, sums[0])], 0
        ).swapaxes(0, 1)
        beyond.append(lax.ppermute(both, "energy", [(0, n - 1)]))
        beyond.append(lax.ppermute(both, "energy", [(n - 1, 0)]))

    terms = [[[] for _ in range(atoms)] for _ in range(cores)]
    base = 0
    for count in chunks_of(half):
        sums = sandwich(
            offsets, occupation, right, left_near, groups, atoms, momenta, base, grid_total, edev, False, line, out_rows, count
        )
        base += count
        for s in range(atoms - 1, -1, -1):
            for t in range(cores):
                block = sums[s * cores + t]
                if s or t:
                    pairs = [
                        (i * cores + k, ((i + s) % atoms) * cores + (k + t) % cores)
                        for i in range(atoms)
                        for k in range(cores)
                    ]
                    block = lax.ppermute(block, ("atom", "kz"), pairs)
                terms[t][s].append(block)
    chunks = chunks_of(half)
    entries = [[[] for _ in range(half)] for _ in range(cores)]
    late = [[[] for _ in range(half)] for _ in range(cores)]
    early, last = Terms(), Terms()
    for t in range(cores):
        for s in range(atoms):
            first = 0
            for chunk, block in enumerate(terms[t][s]):
                held = (last, late) if s and chunk == len(chunks) - 1 else (early, entries)
                held[0].append(block)
                for row in range(chunks[chunk]):
                    held[1][t][first + row].append((block, row))
                first += chunks[chunk]
    total = gathered(entries, half, early)
    return gathered(late, half, last, [total] + beyond)


def solution(mesh):
    return jax.shard_map(
        shards,
        mesh=mesh,
        in_specs=(P(("grp", "kz"), "energy", "atom", None), P("atom", None, None), P(), P(), P()),
        out_specs=P(("grp", "atom", "kz"), "energy", None),
        check_vma=False,
    )
```

```python
import functools

import jax
import jax.numpy as jnp
from jax import lax
from jax.experimental import pallas as pl
from jax.experimental.pallas import tpu as pltpu
from jax.sharding import PartitionSpec as P


MODES = 3
REACH = 2
PIECES = 2


def chunks_of(half):
    return [1] * half


def halves(x):
    high = x.astype(jnp.bfloat16)
    return high, (x - high.astype(jnp.float32)).astype(jnp.bfloat16)


def side_by_side(out, mode, x):
    high, low = halves(x)
    depth = x.shape[1]
    out[mode, :, pl.ds(0, depth)] = high
    out[mode, :, pl.ds(depth, depth)] = high
    out[mode, :, pl.ds(2 * depth, depth)] = low


def prepare(atoms, parts, cores, owners, couplings, *refs):
    right_high, right_low, far, near, held, sems = refs[-6:]
    pieces = refs[:-6]
    atom, core, part = (lax.axis_index(a) for a in ("atom", "kz", "grp"))
    table_rows = couplings.shape[0]
    for mode in range(MODES):
        row = lax.rem(owners[mode], table_rows)
        behind = lax.rem(atom - lax.div(owners[mode], table_rows) + atoms, atoms)

        @pl.when(behind == 0)
        def _(mode=mode, row=row):
            pltpu.make_async_copy(couplings.at[row], held.at[mode], sems.at[mode]).start()

        for s in range(1, atoms):

            @pl.when(behind == s)
            def _(mode=mode, row=row, s=s):
                for d in range(parts):
                    for o in range(cores):
                        piece = pieces[((s - 1) * parts + d) * cores + o]
                        strip = piece.shape[1]
                        at = lax.rem(part - d + parts, parts) * cores + lax.rem(core - o + cores, cores)
                        rows = pl.ds(pl.multiple_of(at * strip, 8), strip)
                        pltpu.make_async_copy(piece.at[row], held.at[mode, rows], sems.at[mode]).start()

    @pl.loop(0, MODES)
    def _(mode):
        pltpu.make_async_copy(held.at[mode], held.at[mode], sems.at[mode]).wait()
        right_high[mode], right_low[mode] = halves(held[mode].T)
        rows, depth = far.shape[1], near.shape[2] // 3
        side_by_side(far, mode, held[mode, pl.ds(pl.multiple_of(atom * rows, 8), rows), :])
        side_by_side(near, mode, held[mode, :, pl.ds(pl.multiple_of(atom * depth, 128), depth)])


def guard(steps, out):
    for mode in range(MODES):
        out[mode] = steps[mode]


def add_momenta(theirs, first, green, *refs):
    out, held, total, arrived, left = refs[-5:]
    given = refs[:-5]
    momenta, count, size = green.shape[0], held.shape[0], held.shape[2]
    core = lax.axis_index("kz")
    base = (1 - core if theirs else core) * count
    for e in range(count):
        for k in range(momenta):
            pltpu.make_async_copy(green.at[k, base + e, pl.ds(first, size)], held.at[e, k], arrived.at[e]).start()
        for ref in given:
            pltpu.make_async_copy(ref.at[e], held.at[e, momenta], arrived.at[e]).start()

    @pl.loop(0, count)
    def _(e):
        pltpu.make_async_copy(held.at[e], held.at[e], arrived.at[e]).wait()
        value = held[e, 0]
        for k in range(1, held.shape[1]):
            value = value + held[e, k]
        total[e] = value
        pltpu.make_async_copy(total.at[e], out.at[e], left.at[e]).start()

    for e in range(count):
        pltpu.make_async_copy(total.at[e], out.at[e], left.at[e]).wait()


def split_dot(n_groups, n_parts, n_atoms, momenta, base, grid_total, edev, far, line, steps, occupation, right_high, right_low, left, *refs):
    sources = [
        [refs[(g * 2 + h) * n_parts : (g * 2 + h + 1) * n_parts] for h in range(2)]
        for g in range(n_groups)
    ]
    outs = refs[n_groups * 2 * n_parts : -4]
    planes, inner, total, sems = refs[-4:]
    count, size = outs[0].shape[:2]
    rows = planes.shape[2]
    half_planes = edev // 2
    place, core, atom = (lax.axis_index(a) for a in ("energy", "kz", "atom"))
    blocks = grid_total // edev
    target = blocks - 1 - place if far else place
    base = base + core * half_planes

    def source_of(energy, mode, side):
        step = steps[mode] if side == 0 else -steps[mode]
        source = lax.rem(target * edev + base + energy + step + grid_total, grid_total)
        rel = lax.div(source, edev) - place
        if far:
            valid = rel == 0
        elif line:
            valid = jnp.abs(rel) <= REACH
        else:
            rel = lax.rem(rel + REACH + blocks, blocks) - REACH
            valid = rel <= REACH
        group = jnp.where(valid, rel + n_groups // 2, n_groups // 2)
        return valid, group, lax.rem(source, edev)

    def fetch(energy, buffer):
        for mode in range(MODES):
            for side in range(2):
                _, group, plane = source_of(energy, mode, side)
                other = jnp.where(lax.div(plane, half_planes) == core, 0, 1)
                at = lax.rem(plane, half_planes)
                slot = mode * 2 + side
                for g in range(n_groups):

                    @pl.when(group == g)
                    def _(g=g, at=at, slot=slot, other=other):
                        for h in range(2):

                            @pl.when(other == h)
                            def _(h=h):
                                first = 0
                                for ref in sources[g][h]:
                                    depth = ref.shape[1]
                                    start = first
                                    if far:
                                        per = rows // n_atoms
                                        behind = lax.rem(atom - first // per + n_atoms, n_atoms)
                                        start = pl.multiple_of(behind * per + first % per, 8)
                                    pltpu.make_async_copy(
                                        ref.at[at], planes.at[buffer, slot, pl.ds(start, depth)], sems.at[buffer, slot]
                                    ).start()
                                    first += depth

    fetch(0, 0)

    @pl.loop(0, count)
    def _(energy):
        buffer = lax.rem(energy, 2)

        if count > 1:

            @pl.when(energy + 1 < count)
            def _():
                fetch(energy + 1, 1 - buffer)

        dot = functools.partial(jnp.dot, preferred_element_type=jnp.float32)
        for mode in range(MODES):
            scales = []
            for side in range(2):
                slot = mode * 2 + side
                held = planes.at[buffer, slot]
                pltpu.make_async_copy(held, held, sems.at[buffer, slot]).wait()
                scales.append(jnp.where(source_of(energy, mode, side)[0], (occupation[mode] + (1.0 - side)) * (1.0 / momenta), 0.0))
            combined = scales[0] * planes[buffer, 2 * mode] + scales[1] * planes[buffer, 2 * mode + 1]
            if far:
                high, low = halves(combined)
                inner[mode, pl.ds(0, rows)] = high
                inner[mode, pl.ds(rows, rows)] = low
                inner[mode, pl.ds(2 * rows, rows)] = high
                high, low = halves(dot(left[mode], inner[mode]))
                term = dot(high, right_high[mode]) + dot(low, right_high[mode]) + dot(high, right_low[mode])
                total[...] = term if mode == 0 else total[...] + term
                continue
            high = combined.astype(jnp.bfloat16)
            low = (combined - high.astype(jnp.float32)).astype(jnp.bfloat16)
            product = dot(high, right_high[mode]) + dot(low, right_high[mode]) + dot(high, right_low[mode])
            high = product.astype(jnp.bfloat16)
            low = (product - high.astype(jnp.float32)).astype(jnp.bfloat16)
            inner[mode, pl.ds(0, rows)] = high
            inner[mode, pl.ds(rows, rows)] = low
            inner[mode, pl.ds(2 * rows, rows)] = high
        for index, out in enumerate(outs):
            s, t = index // 2, index % 2
            block = lax.rem(core + t, 2)
            if far:
                out[energy] = total[pl.ds(pl.multiple_of(block * size, 8), size)]
                continue
            block = block + 2 * lax.rem(atom + s, n_atoms)
            where = pl.ds(pl.multiple_of(block * size, 8), size)
            result = dot(left[0, where], inner[0])
            for mode in range(1, MODES):
                result = result + dot(left[mode, where], inner[mode])
            out[energy] = result


def sandwich(steps, occupation, right, left, groups, n_atoms, momenta, base, grid_total, edev, far, line, out_rows, count):
    order = right[0].shape[-1]
    flat = [part for group in groups for half in group for part in half]
    rows = sum(part.shape[1] for part in groups[0][0])
    n_out = left.shape[1] // out_rows
    buffers = min(count, 2)
    held = 4 * (2 * MODES * buffers + 6) * rows * order + 2 * 3 * MODES * rows * order + (6 << 20)
    held += 4 * left.shape[1] * order * (count + 3) + 4 * MODES * order * order + 2 * left.size
    flops = count * 2 * 3 * MODES * (rows * order * order + left.shape[1] * rows * order)
    return pl.pallas_call(
        functools.partial(split_dot, len(groups), len(groups[0][0]), n_atoms, momenta, base, grid_total, edev, far, line),
        out_shape=[jax.ShapeDtypeStruct((count, out_rows, order), jnp.float32)] * n_out,
        in_specs=[pl.BlockSpec(memory_space=pltpu.SMEM)] * 2
        + [pl.BlockSpec(memory_space=pltpu.VMEM)] * 3
        + [pl.BlockSpec(memory_space=pltpu.HBM)] * len(flat),
        out_specs=[pl.BlockSpec(memory_space=pltpu.VMEM)] * n_out,
        scratch_shapes=[
            pltpu.VMEM((buffers, 2 * MODES, rows, order), jnp.float32),
            pltpu.VMEM((MODES, 3 * rows, order), jnp.bfloat16),
            pltpu.VMEM((left.shape[1] if far else 8, order), jnp.float32),
            pltpu.SemaphoreType.DMA((2, 2 * MODES)),
        ],
        compiler_params=pltpu.CompilerParams(vmem_limit_bytes=held),
        cost_estimate=pl.CostEstimate(
            flops=flops,
            bytes_accessed=count * 4 * (2 * MODES * rows * order + left.shape[1] * order),
            transcendentals=0,
        ),
        name="far_sandwich" if far else "near_sandwich",
    )(steps, occupation, right[0], right[1], left, *flat)


def gather_early(layout, count, *refs):
    out = refs[-1]
    core = lax.axis_index("kz")
    group = 16
    for own in range(2):

        @pl.when(core == own)
        def _(own=own):
            @pl.loop(0, out.shape[0] // group)
            def _(at):
                rows = pl.ds(pl.multiple_of(at * group, group), group)
                for half, energies in enumerate(layout):
                    where = (own if half == 0 else 1 - own) * count
                    for j, terms in enumerate(energies):
                        total = None
                        for ref, row in terms:
                            total = refs[ref][row, rows] if total is None else total + refs[ref][row, rows]
                        out[rows, where + j, :] = total


def gather_late(layout, count, whole, *refs):
    out, total, sem = refs[-3:]
    full = refs[-3 - whole : -3]
    core = lax.axis_index("kz")
    group = 16

    @pl.loop(0, total.shape[0] // group)
    def _(at):
        rows = pl.ds(pl.multiple_of(at * group, group), group)
        value = full[0][rows]
        for ref in full[1:]:
            value = value + ref[rows]
        total[rows] = value
        for own in range(2):

            @pl.when(core == own)
            def _(own=own):
                for half, energies in enumerate(layout):
                    where = (own if half == 0 else 1 - own) * count
                    for j, terms in enumerate(energies):
                        if terms:
                            value = total[rows, where + j, :]
                            for ref, row in terms:
                                value = value + refs[ref][row, rows]
                            total[rows, where + j, :] = value

        pltpu.make_async_copy(total.at[rows], out.at[rows], sem).start()

    pltpu.make_async_copy(total, out, sem).wait()


def gathered(layout, count, arrays, before=()):
    terms = [[[(arrays.index(x), row) for x, row in entry] for entry in energies] for energies in layout]
    out_rows, order = arrays[0].shape[1:]
    arrays = list(arrays) + list(before)
    shape = (out_rows, 2 * count, order)
    size = 4 * sum(x.size for x in arrays) + 4 * 2 * count * out_rows * order
    vmem = pl.BlockSpec(memory_space=pltpu.VMEM)
    if before:
        kernel = functools.partial(gather_late, terms, count, len(before))
        scratch = [pltpu.VMEM(shape, jnp.float32), pltpu.SemaphoreType.DMA]
    else:
        kernel, scratch = functools.partial(gather_early, terms, count), []
    return pl.pallas_call(
        kernel,
        out_shape=jax.ShapeDtypeStruct(shape, jnp.float32),
        in_specs=[vmem] * len(arrays),
        out_specs=pl.BlockSpec(memory_space=pltpu.HBM) if before else vmem,
        scratch_shapes=scratch,
        compiler_params=pltpu.CompilerParams(vmem_limit_bytes=8 << 20),
        cost_estimate=pl.CostEstimate(flops=size // 4, bytes_accessed=size, transcendentals=0),
    )(*arrays)


class Terms(list):
    def index(self, x):
        return next(i for i, y in enumerate(self) if y is x)


def shards(green, couplings, occupation, offsets, owners):
    momenta_here, edev, brows, order = green.shape
    n, atoms, cores = lax.axis_size("energy"), lax.axis_size("atom"), lax.axis_size("kz")
    momenta = momenta_here * cores
    grid_total = n * edev
    parts = lax.axis_size("grp")
    _, core, part = (lax.axis_index(a) for a in ("atom", "kz", "grp"))
    line = n == 2 * REACH
    half = edev // cores
    swap = [(i, (i + 1) % cores) for i in range(cores)]
    around = [[(i, (i + s) % atoms) for i in range(atoms)] for s in range(atoms)]

    size = brows // PIECES

    def summed(theirs, piece, *more):
        return pl.pallas_call(
            functools.partial(add_momenta, theirs, piece * size),
            out_shape=jax.ShapeDtypeStruct((half, size, order), jnp.float32),
            in_specs=[pl.BlockSpec(memory_space=pltpu.HBM)] * (1 + len(more)),
            out_specs=pl.BlockSpec(memory_space=pltpu.HBM),
            scratch_shapes=[
                pltpu.VMEM((half, momenta_here + len(more), size, order), jnp.float32),
                pltpu.VMEM((half, size, order), jnp.float32),
                pltpu.SemaphoreType.DMA((half,)),
                pltpu.SemaphoreType.DMA((half,)),
            ],
            compiler_params=pltpu.CompilerParams(vmem_limit_bytes=67_000_000),
            cost_estimate=pl.CostEstimate(
                flops=momenta_here * half * size * order,
                bytes_accessed=4 * (momenta_here + 1 + len(more)) * half * size * order,
                transcendentals=0,
            ),
            name="add_momenta",
        )(green, *more)

    own = []
    for piece in range(PIECES):
        given = summed(True, piece)
        given = lax.ppermute(given, "kz", swap)
        own.append(summed(False, piece, given))

    if line:
        up = [[(i, i + 1) for i in range(d, n - 1)] for d in range(REACH)]
        down = [[(i, i - 1) for i in range(n - 1 - d, 0, -1)] for d in range(REACH)]
    else:
        up = [[(i, (i + 1) % n) for i in range(n)]] * REACH
        down = [[(i, (i - 1) % n) for i in range(n)]] * REACH
    streams = {0: own}
    for d in range(1, REACH + 1):
        streams[-d] = [lax.ppermute(x, "energy", up[d - 1]) for x in streams[1 - d]]
        streams[d] = [lax.ppermute(x, "energy", down[d - 1]) for x in streams[d - 1]]
    groups = []
    for d in range(-REACH, REACH + 1):
        axes, pairs = "kz", swap
        if line and abs(d) == REACH:
            axes = ("energy", "kz")
            pairs = [
                (i * cores + k, i * cores + (k + 1) % cores) for i in range(n) if 0 <= i + d < n for k in range(cores)
            ]
        groups.append((streams[d], [lax.ppermute(x, axes, pairs) for x in streams[d]]))

    table_rows = couplings.shape[0]
    strip = order // (cores * parts)
    mine = lax.dynamic_slice(couplings, (0, (part * cores + core) * strip, 0), (table_rows, strip, order))
    others = []
    for s in range(1, atoms):
        got = lax.ppermute(mine, "atom", around[s])
        ahead = [got] + [
            lax.ppermute(got, "grp", [(i, (i + d) % parts) for i in range(parts)]) for d in range(1, parts)
        ]
        others.append([(x, lax.ppermute(x, "kz", swap)) for x in ahead])
    out_rows = order // (atoms * cores)
    flat = [x for pieces in others for both in pieces for x in both]
    hbm, vmem = pl.BlockSpec(memory_space=pltpu.HBM), pl.BlockSpec(memory_space=pltpu.VMEM)
    shapes = [(order, order), (order, order), (cores * out_rows, 3 * order), (order, 3 * brows)]
    *right, left_far, left_near = pl.pallas_call(
        functools.partial(prepare, atoms, parts, cores),
        out_shape=[jax.ShapeDtypeStruct((MODES,) + shape, jnp.bfloat16) for shape in shapes],
        in_specs=[pl.BlockSpec(memory_space=pltpu.SMEM)] + [hbm] * (1 + len(flat)),
        out_specs=[vmem] * len(shapes),
        scratch_shapes=[pltpu.VMEM((MODES, order, order), jnp.float32), pltpu.SemaphoreType.DMA((MODES,))],
        compiler_params=pltpu.CompilerParams(vmem_limit_bytes=32 << 20),
        cost_estimate=pl.CostEstimate(
            flops=8 * MODES * order * order, bytes_accessed=10 * MODES * order * order, transcendentals=0
        ),
        name="prepare",
    )(owners, couplings, *flat)

    beyond = []
    if line:
        got = [lax.ppermute(x, "atom", around[s]) for s in range(1, atoms) for x in own]
        whole = (
            list(own) + got,
            groups[REACH][1] + [lax.ppermute(x, "kz", swap) for x in got],
        )
        smem = pl.BlockSpec(memory_space=pltpu.SMEM)
        held = pl.pallas_call(
            guard,
            out_shape=jax.ShapeDtypeStruct(offsets.shape, offsets.dtype),
            in_specs=[smem],
            out_specs=smem,
            compiler_params=pltpu.CompilerParams(vmem_limit_bytes=1 << 20),
            name="guard",
        )(offsets)
        sums = sandwich(
            held, occupation, right, left_far, [whole], atoms, momenta, 0, grid_total, edev, True, line, out_rows, half
        )
        swapped = lax.ppermute(sums[1], "kz", swap)
        both = jnp.concatenate(
            [jnp.where(core == 0, sums[0], swapped), jnp.where(core == 0, swapped, sums[0])], 0
        ).swapaxes(0, 1)
        beyond.append(lax.ppermute(both, "energy", [(0, n - 1)]))
        beyond.append(lax.ppermute(both, "energy", [(n - 1, 0)]))

    terms = [[[] for _ in range(atoms)] for _ in range(cores)]
    base = 0
    for count in chunks_of(half):
        sums = sandwich(
            offsets, occupation, right, left_near, groups, atoms, momenta, base, grid_total, edev, False, line, out_rows, count
        )
        base += count
        for s in range(atoms - 1, -1, -1):
            for t in range(cores):
                block = sums[s * cores + t]
                if s or t:
                    pairs = [
                        (i * cores + k, ((i + s) % atoms) * cores + (k + t) % cores)
                        for i in range(atoms)
                        for k in range(cores)
                    ]
                    block = lax.ppermute(block, ("atom", "kz"), pairs)
                terms[t][s].append(block)
    chunks = chunks_of(half)
    entries = [[[] for _ in range(half)] for _ in range(cores)]
    late = [[[] for _ in range(half)] for _ in range(cores)]
    early, last = Terms(), Terms()
    for t in range(cores):
        for s in range(atoms):
            first = 0
            for chunk, block in enumerate(terms[t][s]):
                held = (last, late) if s and chunk == len(chunks) - 1 else (early, entries)
                held[0].append(block)
                for row in range(chunks[chunk]):
                    held[1][t][first + row].append((block, row))
                first += chunks[chunk]
    total = gathered(entries, half, early)
    return gathered(late, half, last, [total] + beyond)


def solution(mesh):
    return jax.shard_map(
        shards,
        mesh=mesh,
        in_specs=(P(("grp", "kz"), "energy", "atom", None), P("atom", None, None), P(), P(), P()),
        out_specs=P(("grp", "atom", "kz"), "energy", None),
        check_vma=False,
    )
```

```python
import functools

import jax
import jax.numpy as jnp
from jax import lax
from jax.experimental import pallas as pl
from jax.experimental.pallas import tpu as pltpu
from jax.sharding import PartitionSpec as P


MODES = 3
REACH = 2
PIECES = 2


def chunks_of(half, order):
    middle = order // 2
    return [(0, 1, 0, middle), (0, 1, middle, order - middle)] + [(e, 1, 0, order) for e in range(1, half)]


def halves(x):
    high = x.astype(jnp.bfloat16)
    return high, (x - high.astype(jnp.float32)).astype(jnp.bfloat16)


def side_by_side(out, mode, x):
    high, low = halves(x)
    depth = x.shape[1]
    out[mode, :, pl.ds(0, depth)] = high
    out[mode, :, pl.ds(depth, depth)] = high
    out[mode, :, pl.ds(2 * depth, depth)] = low


def prepare(atoms, parts, cores, owners, couplings, *refs):
    right_high, right_low, far, near, held, sems = refs[-6:]
    pieces = refs[:-6]
    atom, core, part = (lax.axis_index(a) for a in ("atom", "kz", "grp"))
    table_rows = couplings.shape[0]
    for mode in range(MODES):
        row = lax.rem(owners[mode], table_rows)
        behind = lax.rem(atom - lax.div(owners[mode], table_rows) + atoms, atoms)

        @pl.when(behind == 0)
        def _(mode=mode, row=row):
            pltpu.make_async_copy(couplings.at[row], held.at[mode], sems.at[mode]).start()

        for s in range(1, atoms):

            @pl.when(behind == s)
            def _(mode=mode, row=row, s=s):
                for d in range(parts):
                    for o in range(cores):
                        piece = pieces[((s - 1) * parts + d) * cores + o]
                        strip = piece.shape[1]
                        at = lax.rem(part - d + parts, parts) * cores + lax.rem(core - o + cores, cores)
                        rows = pl.ds(pl.multiple_of(at * strip, 8), strip)
                        pltpu.make_async_copy(piece.at[row], held.at[mode, rows], sems.at[mode]).start()

    @pl.loop(0, MODES)
    def _(mode):
        pltpu.make_async_copy(held.at[mode], held.at[mode], sems.at[mode]).wait()
        right_high[mode], right_low[mode] = halves(held[mode].T)
        rows, depth = far.shape[1], near.shape[2] // 3
        side_by_side(far, mode, held[mode, pl.ds(pl.multiple_of(atom * rows, 8), rows), :])
        side_by_side(near, mode, held[mode, :, pl.ds(pl.multiple_of(atom * depth, 128), depth)])


def guard(steps, out):
    for mode in range(MODES):
        out[mode] = steps[mode]


def add_momenta(theirs, first, green, *refs):
    out, held, total, arrived, left = refs[-5:]
    given = refs[:-5]
    momenta, count, size = green.shape[0], held.shape[0], held.shape[2]
    core = lax.axis_index("kz")
    base = (1 - core if theirs else core) * count
    for e in range(count):
        for k in range(momenta):
            pltpu.make_async_copy(green.at[k, base + e, pl.ds(first, size)], held.at[e, k], arrived.at[e]).start()
        for ref in given:
            pltpu.make_async_copy(ref.at[e], held.at[e, momenta], arrived.at[e]).start()

    @pl.loop(0, count)
    def _(e):
        pltpu.make_async_copy(held.at[e], held.at[e], arrived.at[e]).wait()
        value = held[e, 0]
        for k in range(1, held.shape[1]):
            value = value + held[e, k]
        total[e] = value
        pltpu.make_async_copy(total.at[e], out.at[e], left.at[e]).start()

    for e in range(count):
        pltpu.make_async_copy(total.at[e], out.at[e], left.at[e]).wait()


def split_dot(n_groups, n_parts, n_atoms, momenta, base, columns, grid_total, edev, far, line, steps, occupation, right_high, right_low, left, *refs):
    sources = [
        [refs[(g * 2 + h) * n_parts : (g * 2 + h + 1) * n_parts] for h in range(2)]
        for g in range(n_groups)
    ]
    outs = refs[n_groups * 2 * n_parts : -4]
    planes, inner, total, sems = refs[-4:]
    count, size = outs[0].shape[:2]
    rows = planes.shape[2]
    half_planes = edev // 2
    place, core, atom = (lax.axis_index(a) for a in ("energy", "kz", "atom"))
    blocks = grid_total // edev
    target = blocks - 1 - place if far else place
    base = base + core * half_planes

    def source_of(energy, mode, side):
        step = steps[mode] if side == 0 else -steps[mode]
        source = lax.rem(target * edev + base + energy + step + grid_total, grid_total)
        rel = lax.div(source, edev) - place
        if far:
            valid = rel == 0
        elif line:
            valid = jnp.abs(rel) <= REACH
        else:
            rel = lax.rem(rel + REACH + blocks, blocks) - REACH
            valid = rel <= REACH
        group = jnp.where(valid, rel + n_groups // 2, n_groups // 2)
        return valid, group, lax.rem(source, edev)

    def fetch(energy, buffer):
        for mode in range(MODES):
            for side in range(2):
                _, group, plane = source_of(energy, mode, side)
                other = jnp.where(lax.div(plane, half_planes) == core, 0, 1)
                at = lax.rem(plane, half_planes)
                slot = mode * 2 + side
                for g in range(n_groups):

                    @pl.when(group == g)
                    def _(g=g, at=at, slot=slot, other=other):
                        for h in range(2):

                            @pl.when(other == h)
                            def _(h=h):
                                first = 0
                                for ref in sources[g][h]:
                                    depth = ref.shape[1]
                                    start = first
                                    if far:
                                        per = rows // n_atoms
                                        behind = lax.rem(atom - first // per + n_atoms, n_atoms)
                                        start = pl.multiple_of(behind * per + first % per, 8)
                                    pltpu.make_async_copy(
                                        ref.at[at], planes.at[buffer, slot, pl.ds(start, depth)], sems.at[buffer, slot]
                                    ).start()
                                    first += depth

    fetch(0, 0)

    @pl.loop(0, count)
    def _(energy):
        buffer = lax.rem(energy, 2)

        if count > 1:

            @pl.when(energy + 1 < count)
            def _():
                fetch(energy + 1, 1 - buffer)

        dot = functools.partial(jnp.dot, preferred_element_type=jnp.float32)
        for mode in range(MODES):
            scales = []
            for side in range(2):
                slot = mode * 2 + side
                held = planes.at[buffer, slot]
                pltpu.make_async_copy(held, held, sems.at[buffer, slot]).wait()
                scales.append(jnp.where(source_of(energy, mode, side)[0], (occupation[mode] + (1.0 - side)) * (1.0 / momenta), 0.0))
            combined = scales[0] * planes[buffer, 2 * mode] + scales[1] * planes[buffer, 2 * mode + 1]
            if far:
                high, low = halves(combined)
                inner[mode, pl.ds(0, rows)] = high
                inner[mode, pl.ds(rows, rows)] = low
                inner[mode, pl.ds(2 * rows, rows)] = high
                high, low = halves(dot(left[mode], inner[mode]))
                term = dot(high, right_high[mode]) + dot(low, right_high[mode]) + dot(high, right_low[mode])
                total[...] = term if mode == 0 else total[...] + term
                continue
            high = combined.astype(jnp.bfloat16)
            low = (combined - high.astype(jnp.float32)).astype(jnp.bfloat16)
            first, second = right_high[mode, :, columns], right_low[mode, :, columns]
            product = dot(high, first) + dot(low, first) + dot(high, second)
            high = product.astype(jnp.bfloat16)
            low = (product - high.astype(jnp.float32)).astype(jnp.bfloat16)
            inner[mode, pl.ds(0, rows)] = high
            inner[mode, pl.ds(rows, rows)] = low
            inner[mode, pl.ds(2 * rows, rows)] = high
        for index, out in enumerate(outs):
            s, t = index // 2, index % 2
            block = lax.rem(core + t, 2)
            if far:
                out[energy] = total[pl.ds(pl.multiple_of(block * size, 8), size)]
                continue
            block = block + 2 * lax.rem(atom + s, n_atoms)
            where = pl.ds(pl.multiple_of(block * size, 8), size)
            result = dot(left[0, where], inner[0])
            for mode in range(1, MODES):
                result = result + dot(left[mode, where], inner[mode])
            out[energy] = result


def sandwich(steps, occupation, right, left, groups, n_atoms, momenta, base, grid_total, edev, far, line, out_rows, count, first=0, width=None):
    order = right[0].shape[-1]
    width = width or order
    flat = [part for group in groups for half in group for part in half]
    rows = sum(part.shape[1] for part in groups[0][0])
    n_out = left.shape[1] // out_rows
    buffers = min(count, 2)
    held = 4 * (2 * MODES * buffers + 6) * rows * order + 2 * 3 * MODES * rows * order + (6 << 20)
    held += 4 * left.shape[1] * order * (count + 3) + 4 * MODES * order * order + 2 * left.size
    flops = count * 2 * 3 * MODES * (rows * order * width + left.shape[1] * rows * width)
    return pl.pallas_call(
        functools.partial(split_dot, len(groups), len(groups[0][0]), n_atoms, momenta, base, pl.ds(first, width), grid_total, edev, far, line),
        out_shape=[jax.ShapeDtypeStruct((count, out_rows, width), jnp.float32)] * n_out,
        in_specs=[pl.BlockSpec(memory_space=pltpu.SMEM)] * 2
        + [pl.BlockSpec(memory_space=pltpu.VMEM)] * 3
        + [pl.BlockSpec(memory_space=pltpu.HBM)] * len(flat),
        out_specs=[pl.BlockSpec(memory_space=pltpu.VMEM)] * n_out,
        scratch_shapes=[
            pltpu.VMEM((buffers, 2 * MODES, rows, order), jnp.float32),
            pltpu.VMEM((MODES, 3 * rows, width), jnp.bfloat16),
            pltpu.VMEM((left.shape[1] if far else 8, order), jnp.float32),
            pltpu.SemaphoreType.DMA((2, 2 * MODES)),
        ],
        compiler_params=pltpu.CompilerParams(vmem_limit_bytes=held),
        cost_estimate=pl.CostEstimate(
            flops=flops,
            bytes_accessed=count * 4 * (2 * MODES * rows * order + left.shape[1] * order),
            transcendentals=0,
        ),
        name="far_sandwich" if far else "near_sandwich",
    )(steps, occupation, right[0], right[1], left, *flat)


def beside(refs, term, rows):
    return jnp.concatenate([refs[ref][row, rows] for ref, row in term], axis=1)


def gather_early(layout, count, *refs):
    out = refs[-1]
    core = lax.axis_index("kz")
    group = 16
    for own in range(2):

        @pl.when(core == own)
        def _(own=own):
            @pl.loop(0, out.shape[0] // group)
            def _(at):
                rows = pl.ds(pl.multiple_of(at * group, group), group)
                for half, energies in enumerate(layout):
                    where = (own if half == 0 else 1 - own) * count
                    for j, terms in enumerate(energies):
                        total = None
                        for term in terms:
                            value = beside(refs, term, rows)
                            total = value if total is None else total + value
                        out[rows, where + j, :] = total


def gather_late(layout, count, whole, *refs):
    out, total, sem = refs[-3:]
    full = refs[-3 - whole : -3]
    core = lax.axis_index("kz")
    group = 16

    @pl.loop(0, total.shape[0] // group)
    def _(at):
        rows = pl.ds(pl.multiple_of(at * group, group), group)
        value = full[0][rows]
        for ref in full[1:]:
            value = value + ref[rows]
        total[rows] = value
        for own in range(2):

            @pl.when(core == own)
            def _(own=own):
                for half, energies in enumerate(layout):
                    where = (own if half == 0 else 1 - own) * count
                    for j, terms in enumerate(energies):
                        if terms:
                            value = total[rows, where + j, :]
                            for term in terms:
                                value = value + beside(refs, term, rows)
                            total[rows, where + j, :] = value

        pltpu.make_async_copy(total.at[rows], out.at[rows], sem).start()

    pltpu.make_async_copy(total, out, sem).wait()


def gathered(layout, count, order, arrays, before=()):
    terms = [
        [[[(arrays.index(x), row) for x, row in term] for term in entry] for entry in energies] for energies in layout
    ]
    out_rows = arrays[0].shape[1]
    arrays = list(arrays) + list(before)
    shape = (out_rows, 2 * count, order)
    size = 4 * sum(x.size for x in arrays) + 4 * 2 * count * out_rows * order
    vmem = pl.BlockSpec(memory_space=pltpu.VMEM)
    if before:
        kernel = functools.partial(gather_late, terms, count, len(before))
        scratch = [pltpu.VMEM(shape, jnp.float32), pltpu.SemaphoreType.DMA]
    else:
        kernel, scratch = functools.partial(gather_early, terms, count), []
    return pl.pallas_call(
        kernel,
        out_shape=jax.ShapeDtypeStruct(shape, jnp.float32),
        in_specs=[vmem] * len(arrays),
        out_specs=pl.BlockSpec(memory_space=pltpu.HBM) if before else vmem,
        scratch_shapes=scratch,
        compiler_params=pltpu.CompilerParams(vmem_limit_bytes=8 << 20),
        cost_estimate=pl.CostEstimate(flops=size // 4, bytes_accessed=size, transcendentals=0),
    )(*arrays)


class Terms(list):
    def index(self, x):
        return next(i for i, y in enumerate(self) if y is x)


def shards(green, couplings, occupation, offsets, owners):
    momenta_here, edev, brows, order = green.shape
    n, atoms, cores = lax.axis_size("energy"), lax.axis_size("atom"), lax.axis_size("kz")
    momenta = momenta_here * cores
    grid_total = n * edev
    parts = lax.axis_size("grp")
    _, core, part = (lax.axis_index(a) for a in ("atom", "kz", "grp"))
    line = n == 2 * REACH
    half = edev // cores
    swap = [(i, (i + 1) % cores) for i in range(cores)]
    around = [[(i, (i + s) % atoms) for i in range(atoms)] for s in range(atoms)]

    size = brows // PIECES

    def summed(theirs, piece, *more):
        return pl.pallas_call(
            functools.partial(add_momenta, theirs, piece * size),
            out_shape=jax.ShapeDtypeStruct((half, size, order), jnp.float32),
            in_specs=[pl.BlockSpec(memory_space=pltpu.HBM)] * (1 + len(more)),
            out_specs=pl.BlockSpec(memory_space=pltpu.HBM),
            scratch_shapes=[
                pltpu.VMEM((half, momenta_here + len(more), size, order), jnp.float32),
                pltpu.VMEM((half, size, order), jnp.float32),
                pltpu.SemaphoreType.DMA((half,)),
                pltpu.SemaphoreType.DMA((half,)),
            ],
            compiler_params=pltpu.CompilerParams(vmem_limit_bytes=67_000_000),
            cost_estimate=pl.CostEstimate(
                flops=momenta_here * half * size * order,
                bytes_accessed=4 * (momenta_here + 1 + len(more)) * half * size * order,
                transcendentals=0,
            ),
            name="add_momenta",
        )(green, *more)

    own = []
    for piece in range(PIECES):
        given = summed(True, piece)
        given = lax.ppermute(given, "kz", swap)
        own.append(summed(False, piece, given))

    if line:
        up = [[(i, i + 1) for i in range(d, n - 1)] for d in range(REACH)]
        down = [[(i, i - 1) for i in range(n - 1 - d, 0, -1)] for d in range(REACH)]
    else:
        up = [[(i, (i + 1) % n) for i in range(n)]] * REACH
        down = [[(i, (i - 1) % n) for i in range(n)]] * REACH
    streams = {0: own}
    for d in range(1, REACH + 1):
        streams[-d] = [lax.ppermute(x, "energy", up[d - 1]) for x in streams[1 - d]]
        streams[d] = [lax.ppermute(x, "energy", down[d - 1]) for x in streams[d - 1]]
    groups = []
    for d in range(-REACH, REACH + 1):
        axes, pairs = "kz", swap
        if line and abs(d) == REACH:
            axes = ("energy", "kz")
            pairs = [
                (i * cores + k, i * cores + (k + 1) % cores) for i in range(n) if 0 <= i + d < n for k in range(cores)
            ]
        groups.append((streams[d], [lax.ppermute(x, axes, pairs) for x in streams[d]]))

    table_rows = couplings.shape[0]
    strip = order // (cores * parts)
    mine = lax.dynamic_slice(couplings, (0, (part * cores + core) * strip, 0), (table_rows, strip, order))
    others = []
    for s in range(1, atoms):
        got = lax.ppermute(mine, "atom", around[s])
        ahead = [got] + [
            lax.ppermute(got, "grp", [(i, (i + d) % parts) for i in range(parts)]) for d in range(1, parts)
        ]
        others.append([(x, lax.ppermute(x, "kz", swap)) for x in ahead])
    out_rows = order // (atoms * cores)
    flat = [x for pieces in others for both in pieces for x in both]
    hbm, vmem = pl.BlockSpec(memory_space=pltpu.HBM), pl.BlockSpec(memory_space=pltpu.VMEM)
    shapes = [(order, order), (order, order), (cores * out_rows, 3 * order), (order, 3 * brows)]
    *right, left_far, left_near = pl.pallas_call(
        functools.partial(prepare, atoms, parts, cores),
        out_shape=[jax.ShapeDtypeStruct((MODES,) + shape, jnp.bfloat16) for shape in shapes],
        in_specs=[pl.BlockSpec(memory_space=pltpu.SMEM)] + [hbm] * (1 + len(flat)),
        out_specs=[vmem] * len(shapes),
        scratch_shapes=[pltpu.VMEM((MODES, order, order), jnp.float32), pltpu.SemaphoreType.DMA((MODES,))],
        compiler_params=pltpu.CompilerParams(vmem_limit_bytes=32 << 20),
        cost_estimate=pl.CostEstimate(
            flops=8 * MODES * order * order, bytes_accessed=10 * MODES * order * order, transcendentals=0
        ),
        name="prepare",
    )(owners, couplings, *flat)

    beyond = []
    if line:
        got = [lax.ppermute(x, "atom", around[s]) for s in range(1, atoms) for x in own]
        whole = (
            list(own) + got,
            groups[REACH][1] + [lax.ppermute(x, "kz", swap) for x in got],
        )
        smem = pl.BlockSpec(memory_space=pltpu.SMEM)
        held = pl.pallas_call(
            guard,
            out_shape=jax.ShapeDtypeStruct(offsets.shape, offsets.dtype),
            in_specs=[smem],
            out_specs=smem,
            compiler_params=pltpu.CompilerParams(vmem_limit_bytes=1 << 20),
            name="guard",
        )(offsets)
        sums = sandwich(
            held, occupation, right, left_far, [whole], atoms, momenta, 0, grid_total, edev, True, line, out_rows, half
        )
        swapped = lax.ppermute(sums[1], "kz", swap)
        both = jnp.concatenate(
            [jnp.where(core == 0, sums[0], swapped), jnp.where(core == 0, swapped, sums[0])], 0
        ).swapaxes(0, 1)
        beyond.append(lax.ppermute(both, "energy", [(0, n - 1)]))
        beyond.append(lax.ppermute(both, "energy", [(n - 1, 0)]))

    chunks = chunks_of(half, order)
    entries = [[[[] for _ in range(atoms)] for _ in range(half)] for _ in range(cores)]
    early, last = Terms(), Terms()
    for chunk, (energy, count, first, width) in enumerate(chunks):
        sums = sandwich(
            offsets, occupation, right, left_near, groups, atoms, momenta, energy, grid_total, edev, False, line, out_rows,
            count, first, width,
        )
        for s in range(atoms - 1, -1, -1):
            for t in range(cores):
                block = sums[s * cores + t]
                if s or t:
                    pairs = [
                        (i * cores + k, ((i + s) % atoms) * cores + (k + t) % cores)
                        for i in range(atoms)
                        for k in range(cores)
                    ]
                    block = lax.ppermute(block, ("atom", "kz"), pairs)
                (last if s and chunk == len(chunks) - 1 else early).append(block)
                for row in range(count):
                    entries[t][energy + row][s].append((block, row))
    final = {id(x) for x in last}

    def chosen(late):
        return [
            [[term for term in terms if (id(term[-1][0]) in final) == late] for terms in energies] for energies in entries
        ]

    total = gathered(chosen(False), half, order, early)
    return gathered(chosen(True), half, order, last, [total] + beyond)


def solution(mesh):
    return jax.shard_map(
        shards,
        mesh=mesh,
        in_specs=(P(("grp", "kz"), "energy", "atom", None), P("atom", None, None), P(), P(), P()),
        out_specs=P(("grp", "atom", "kz"), "energy", None),
        check_vma=False,
    )
```

```python
import functools

import jax
import jax.numpy as jnp
from jax import lax
from jax.experimental import pallas as pl
from jax.experimental.pallas import tpu as pltpu
from jax.sharding import PartitionSpec as P


MODES = 3
REACH = 2
PIECES = 2


def chunks_of(half):
    return [1] * half


def quotient(x, n):
    return lax.shift_right_logical(x, jnp.int32(n.bit_length() - 1)) if n & (n - 1) == 0 else lax.div(x, n)


def remainder(x, n):
    return x & (n - 1) if n & (n - 1) == 0 else lax.rem(x, n)


def halves(x):
    high = x.astype(jnp.bfloat16)
    return high, (x - high.astype(jnp.float32)).astype(jnp.bfloat16)


def side_by_side(out, mode, x):
    high, low = halves(x)
    depth = x.shape[1]
    out[mode, :, pl.ds(0, depth)] = high
    out[mode, :, pl.ds(depth, depth)] = high
    out[mode, :, pl.ds(2 * depth, depth)] = low


def prepare(atoms, parts, cores, owners, couplings, *refs):
    right_high, right_low, far, near, held, sems = refs[-6:]
    pieces = refs[:-6]
    atom, core, part = (lax.axis_index(a) for a in ("atom", "kz", "grp"))
    table_rows = couplings.shape[0]
    for mode in range(MODES):
        row = lax.rem(owners[mode], table_rows)
        behind = lax.rem(atom - lax.div(owners[mode], table_rows) + atoms, atoms)

        @pl.when(behind == 0)
        def _(mode=mode, row=row):
            pltpu.make_async_copy(couplings.at[row], held.at[mode], sems.at[mode]).start()

        for s in range(1, atoms):

            @pl.when(behind == s)
            def _(mode=mode, row=row, s=s):
                for d in range(parts):
                    for o in range(cores):
                        piece = pieces[((s - 1) * parts + d) * cores + o]
                        strip = piece.shape[1]
                        at = lax.rem(part - d + parts, parts) * cores + lax.rem(core - o + cores, cores)
                        rows = pl.ds(pl.multiple_of(at * strip, 8), strip)
                        pltpu.make_async_copy(piece.at[row], held.at[mode, rows], sems.at[mode]).start()

    @pl.loop(0, MODES)
    def _(mode):
        pltpu.make_async_copy(held.at[mode], held.at[mode], sems.at[mode]).wait()
        right_high[mode], right_low[mode] = halves(held[mode].T)
        rows, depth = far.shape[1], near.shape[2] // 3
        side_by_side(far, mode, held[mode, pl.ds(pl.multiple_of(atom * rows, 8), rows), :])
        side_by_side(near, mode, held[mode, :, pl.ds(pl.multiple_of(atom * depth, 128), depth)])


def guard(steps, out):
    for mode in range(MODES):
        out[mode] = steps[mode]


def add_momenta(theirs, first, green, *refs):
    out, held, total, arrived, left = refs[-5:]
    given = refs[:-5]
    momenta, count, size = green.shape[0], held.shape[0], held.shape[2]
    core = lax.axis_index("kz")
    base = (1 - core if theirs else core) * count
    for e in range(count):
        for k in range(momenta):
            pltpu.make_async_copy(green.at[k, base + e, pl.ds(first, size)], held.at[e, k], arrived.at[e]).start()
        for ref in given:
            pltpu.make_async_copy(ref.at[e], held.at[e, momenta], arrived.at[e]).start()

    @pl.loop(0, count)
    def _(e):
        pltpu.make_async_copy(held.at[e], held.at[e], arrived.at[e]).wait()
        value = held[e, 0]
        for k in range(1, held.shape[1]):
            value = value + held[e, k]
        total[e] = value
        pltpu.make_async_copy(total.at[e], out.at[e], left.at[e]).start()

    for e in range(count):
        pltpu.make_async_copy(total.at[e], out.at[e], left.at[e]).wait()


def split_dot(n_groups, n_parts, n_atoms, momenta, base, grid_total, edev, far, line, steps, occupation, right_high, right_low, left, *refs):
    sources = [
        [refs[(g * 2 + h) * n_parts : (g * 2 + h + 1) * n_parts] for h in range(2)]
        for g in range(n_groups)
    ]
    outs = refs[n_groups * 2 * n_parts : -4]
    planes, inner, total, sems = refs[-4:]
    count, size = outs[0].shape[:2]
    rows = planes.shape[2]
    half_planes = edev // 2
    place, core, atom = (lax.axis_index(a) for a in ("energy", "kz", "atom"))
    blocks = grid_total // edev
    target = blocks - 1 - place if far else place
    base = base + core * half_planes

    def source_of(energy, mode, side):
        step = steps[mode] if side == 0 else -steps[mode]
        source = remainder(target * edev + base + energy + step + grid_total, grid_total)
        rel = quotient(source, edev) - place
        if far:
            valid = rel == 0
        elif line:
            valid = jnp.abs(rel) <= REACH
        else:
            rel = remainder(rel + REACH + blocks, blocks) - REACH
            valid = rel <= REACH
        group = jnp.where(valid, rel + n_groups // 2, n_groups // 2)
        return valid, group, remainder(source, edev)

    def fetch(energy, buffer):
        for mode in range(MODES):
            for side in range(2):
                _, group, plane = source_of(energy, mode, side)
                other = jnp.where(quotient(plane, half_planes) == core, 0, 1)
                at = remainder(plane, half_planes)
                slot = mode * 2 + side
                for g in range(n_groups):

                    @pl.when(group == g)
                    def _(g=g, at=at, slot=slot, other=other):
                        for h in range(2):

                            @pl.when(other == h)
                            def _(h=h):
                                first = 0
                                for ref in sources[g][h]:
                                    depth = ref.shape[1]
                                    start = first
                                    if far:
                                        per = rows // n_atoms
                                        behind = lax.rem(atom - first // per + n_atoms, n_atoms)
                                        start = pl.multiple_of(behind * per + first % per, 8)
                                    pltpu.make_async_copy(
                                        ref.at[at], planes.at[buffer, slot, pl.ds(start, depth)], sems.at[buffer, slot]
                                    ).start()
                                    first += depth

    fetch(0, 0)

    @pl.loop(0, count)
    def _(energy):
        buffer = energy & 1

        if count > 1:

            @pl.when(energy + 1 < count)
            def _():
                fetch(energy + 1, 1 - buffer)

        dot = functools.partial(jnp.dot, preferred_element_type=jnp.float32)
        scales = [
            jnp.where(source_of(energy, mode, side)[0], (occupation[mode] + (1.0 - side)) * (1.0 / momenta), 0.0)
            for mode in range(MODES)
            for side in range(2)
        ]
        for mode in range(MODES):
            for slot in (2 * mode, 2 * mode + 1):
                held = planes.at[buffer, slot]
                pltpu.make_async_copy(held, held, sems.at[buffer, slot]).wait()
            combined = scales[2 * mode] * planes[buffer, 2 * mode] + scales[2 * mode + 1] * planes[buffer, 2 * mode + 1]
            if far:
                high, low = halves(combined)
                inner[mode, pl.ds(0, rows)] = high
                inner[mode, pl.ds(rows, rows)] = low
                inner[mode, pl.ds(2 * rows, rows)] = high
                high, low = halves(dot(left[mode], inner[mode]))
                term = dot(high, right_high[mode]) + dot(low, right_high[mode]) + dot(high, right_low[mode])
                total[...] = term if mode == 0 else total[...] + term
                continue
            high = combined.astype(jnp.bfloat16)
            low = (combined - high.astype(jnp.float32)).astype(jnp.bfloat16)
            product = dot(high, right_high[mode]) + dot(low, right_high[mode]) + dot(high, right_low[mode])
            high = product.astype(jnp.bfloat16)
            low = (product - high.astype(jnp.float32)).astype(jnp.bfloat16)
            inner[mode, pl.ds(0, rows)] = high
            inner[mode, pl.ds(rows, rows)] = low
            inner[mode, pl.ds(2 * rows, rows)] = high
        for index, out in enumerate(outs):
            s, t = index // 2, index % 2
            block = lax.rem(core + t, 2)
            if far:
                out[energy] = total[pl.ds(pl.multiple_of(block * size, 8), size)]
                continue
            block = block + 2 * lax.rem(atom + s, n_atoms)
            where = pl.ds(pl.multiple_of(block * size, 8), size)
            result = dot(left[0, where], inner[0])
            for mode in range(1, MODES):
                result = result + dot(left[mode, where], inner[mode])
            out[energy] = result


def sandwich(steps, occupation, right, left, groups, n_atoms, momenta, base, grid_total, edev, far, line, out_rows, count):
    order = right[0].shape[-1]
    flat = [part for group in groups for half in group for part in half]
    rows = sum(part.shape[1] for part in groups[0][0])
    n_out = left.shape[1] // out_rows
    buffers = min(count, 2)
    held = 4 * (2 * MODES * buffers + 6) * rows * order + 2 * 3 * MODES * rows * order + (6 << 20)
    held += 4 * left.shape[1] * order * (count + 3) + 4 * MODES * order * order + 2 * left.size
    flops = count * 2 * 3 * MODES * (rows * order * order + left.shape[1] * rows * order)
    return pl.pallas_call(
        functools.partial(split_dot, len(groups), len(groups[0][0]), n_atoms, momenta, base, grid_total, edev, far, line),
        out_shape=[jax.ShapeDtypeStruct((count, out_rows, order), jnp.float32)] * n_out,
        in_specs=[pl.BlockSpec(memory_space=pltpu.SMEM)] * 2
        + [pl.BlockSpec(memory_space=pltpu.VMEM)] * 3
        + [pl.BlockSpec(memory_space=pltpu.HBM)] * len(flat),
        out_specs=[pl.BlockSpec(memory_space=pltpu.VMEM)] * n_out,
        scratch_shapes=[
            pltpu.VMEM((buffers, 2 * MODES, rows, order), jnp.float32),
            pltpu.VMEM((MODES, 3 * rows, order), jnp.bfloat16),
            pltpu.VMEM((left.shape[1] if far else 8, order), jnp.float32),
            pltpu.SemaphoreType.DMA((2, 2 * MODES)),
        ],
        compiler_params=pltpu.CompilerParams(vmem_limit_bytes=held),
        cost_estimate=pl.CostEstimate(
            flops=flops,
            bytes_accessed=count * 4 * (2 * MODES * rows * order + left.shape[1] * order),
            transcendentals=0,
        ),
        name="far_sandwich" if far else "near_sandwich",
    )(steps, occupation, right[0], right[1], left, *flat)


def gather_early(layout, count, *refs):
    out = refs[-1]
    core = lax.axis_index("kz")
    group = 16
    for own in range(2):

        @pl.when(core == own)
        def _(own=own):
            @pl.loop(0, out.shape[0] // group)
            def _(at):
                rows = pl.ds(pl.multiple_of(at * group, group), group)
                for half, energies in enumerate(layout):
                    where = (own if half == 0 else 1 - own) * count
                    for j, terms in enumerate(energies):
                        total = None
                        for ref, row in terms:
                            total = refs[ref][row, rows] if total is None else total + refs[ref][row, rows]
                        out[rows, where + j, :] = total


def gather_late(layout, count, whole, *refs):
    out, total, sem = refs[-3:]
    full = refs[-3 - whole : -3]
    core = lax.axis_index("kz")
    group = 16

    @pl.loop(0, total.shape[0] // group)
    def _(at):
        rows = pl.ds(pl.multiple_of(at * group, group), group)
        value = full[0][rows]
        for ref in full[1:]:
            value = value + ref[rows]
        total[rows] = value
        for own in range(2):

            @pl.when(core == own)
            def _(own=own):
                for half, energies in enumerate(layout):
                    where = (own if half == 0 else 1 - own) * count
                    for j, terms in enumerate(energies):
                        if terms:
                            value = total[rows, where + j, :]
                            for ref, row in terms:
                                value = value + refs[ref][row, rows]
                            total[rows, where + j, :] = value

        pltpu.make_async_copy(total.at[rows], out.at[rows], sem).start()

    pltpu.make_async_copy(total, out, sem).wait()


def gathered(layout, count, arrays, before=()):
    terms = [[[(arrays.index(x), row) for x, row in entry] for entry in energies] for energies in layout]
    out_rows, order = arrays[0].shape[1:]
    arrays = list(arrays) + list(before)
    shape = (out_rows, 2 * count, order)
    size = 4 * sum(x.size for x in arrays) + 4 * 2 * count * out_rows * order
    vmem = pl.BlockSpec(memory_space=pltpu.VMEM)
    if before:
        kernel = functools.partial(gather_late, terms, count, len(before))
        scratch = [pltpu.VMEM(shape, jnp.float32), pltpu.SemaphoreType.DMA]
    else:
        kernel, scratch = functools.partial(gather_early, terms, count), []
    return pl.pallas_call(
        kernel,
        out_shape=jax.ShapeDtypeStruct(shape, jnp.float32),
        in_specs=[vmem] * len(arrays),
        out_specs=pl.BlockSpec(memory_space=pltpu.HBM) if before else vmem,
        scratch_shapes=scratch,
        compiler_params=pltpu.CompilerParams(vmem_limit_bytes=8 << 20),
        cost_estimate=pl.CostEstimate(flops=size // 4, bytes_accessed=size, transcendentals=0),
    )(*arrays)


class Terms(list):
    def index(self, x):
        return next(i for i, y in enumerate(self) if y is x)


def shards(green, couplings, occupation, offsets, owners):
    momenta_here, edev, brows, order = green.shape
    n, atoms, cores = lax.axis_size("energy"), lax.axis_size("atom"), lax.axis_size("kz")
    momenta = momenta_here * cores
    grid_total = n * edev
    parts = lax.axis_size("grp")
    _, core, part = (lax.axis_index(a) for a in ("atom", "kz", "grp"))
    line = n == 2 * REACH
    half = edev // cores
    swap = [(i, (i + 1) % cores) for i in range(cores)]
    around = [[(i, (i + s) % atoms) for i in range(atoms)] for s in range(atoms)]

    size = brows // PIECES

    def summed(theirs, piece, *more):
        return pl.pallas_call(
            functools.partial(add_momenta, theirs, piece * size),
            out_shape=jax.ShapeDtypeStruct((half, size, order), jnp.float32),
            in_specs=[pl.BlockSpec(memory_space=pltpu.HBM)] * (1 + len(more)),
            out_specs=pl.BlockSpec(memory_space=pltpu.HBM),
            scratch_shapes=[
                pltpu.VMEM((half, momenta_here + len(more), size, order), jnp.float32),
                pltpu.VMEM((half, size, order), jnp.float32),
                pltpu.SemaphoreType.DMA((half,)),
                pltpu.SemaphoreType.DMA((half,)),
            ],
            compiler_params=pltpu.CompilerParams(vmem_limit_bytes=67_000_000),
            cost_estimate=pl.CostEstimate(
                flops=momenta_here * half * size * order,
                bytes_accessed=4 * (momenta_here + 1 + len(more)) * half * size * order,
                transcendentals=0,
            ),
            name="add_momenta",
        )(green, *more)

    own = []
    for piece in range(PIECES):
        given = summed(True, piece)
        given = lax.ppermute(given, "kz", swap)
        kept = summed(False, piece)
        own.append(kept + given)

    if line:
        up = [[(i, i + 1) for i in range(d, n - 1)] for d in range(REACH)]
        down = [[(i, i - 1) for i in range(n - 1 - d, 0, -1)] for d in range(REACH)]
    else:
        up = [[(i, (i + 1) % n) for i in range(n)]] * REACH
        down = [[(i, (i - 1) % n) for i in range(n)]] * REACH
    streams = {0: own}
    for d in range(1, REACH + 1):
        streams[-d] = [lax.ppermute(x, "energy", up[d - 1]) for x in streams[1 - d]]
        streams[d] = [lax.ppermute(x, "energy", down[d - 1]) for x in streams[d - 1]]
    groups = []
    for d in range(-REACH, REACH + 1):
        axes, pairs = "kz", swap
        if line and abs(d) == REACH:
            axes = ("energy", "kz")
            pairs = [
                (i * cores + k, i * cores + (k + 1) % cores) for i in range(n) if 0 <= i + d < n for k in range(cores)
            ]
        groups.append((streams[d], [lax.ppermute(x, axes, pairs) for x in streams[d]]))

    table_rows = couplings.shape[0]
    strip = order // (cores * parts)
    mine = lax.dynamic_slice(couplings, (0, (part * cores + core) * strip, 0), (table_rows, strip, order))
    others = []
    for s in range(1, atoms):
        got = lax.ppermute(mine, "atom", around[s])
        ahead = [got] + [
            lax.ppermute(got, "grp", [(i, (i + d) % parts) for i in range(parts)]) for d in range(1, parts)
        ]
        others.append([(x, lax.ppermute(x, "kz", swap)) for x in ahead])
    out_rows = order // (atoms * cores)
    flat = [x for pieces in others for both in pieces for x in both]
    hbm, vmem = pl.BlockSpec(memory_space=pltpu.HBM), pl.BlockSpec(memory_space=pltpu.VMEM)
    shapes = [(order, order), (order, order), (cores * out_rows, 3 * order), (order, 3 * brows)]
    *right, left_far, left_near = pl.pallas_call(
        functools.partial(prepare, atoms, parts, cores),
        out_shape=[jax.ShapeDtypeStruct((MODES,) + shape, jnp.bfloat16) for shape in shapes],
        in_specs=[pl.BlockSpec(memory_space=pltpu.SMEM)] + [hbm] * (1 + len(flat)),
        out_specs=[vmem] * len(shapes),
        scratch_shapes=[pltpu.VMEM((MODES, order, order), jnp.float32), pltpu.SemaphoreType.DMA((MODES,))],
        compiler_params=pltpu.CompilerParams(vmem_limit_bytes=32 << 20),
        cost_estimate=pl.CostEstimate(
            flops=8 * MODES * order * order, bytes_accessed=10 * MODES * order * order, transcendentals=0
        ),
        name="prepare",
    )(owners, couplings, *flat)

    beyond = []
    if line:
        got = [lax.ppermute(x, "atom", around[s]) for s in range(1, atoms) for x in own]
        whole = (
            list(own) + got,
            groups[REACH][1] + [lax.ppermute(x, "kz", swap) for x in got],
        )
        smem = pl.BlockSpec(memory_space=pltpu.SMEM)
        held = pl.pallas_call(
            guard,
            out_shape=jax.ShapeDtypeStruct(offsets.shape, offsets.dtype),
            in_specs=[smem],
            out_specs=smem,
            compiler_params=pltpu.CompilerParams(vmem_limit_bytes=1 << 20),
            name="guard",
        )(offsets)
        sums = sandwich(
            held, occupation, right, left_far, [whole], atoms, momenta, 0, grid_total, edev, True, line, out_rows, half
        )
        swapped = lax.ppermute(sums[1], "kz", swap)
        both = jnp.concatenate(
            [jnp.where(core == 0, sums[0], swapped), jnp.where(core == 0, swapped, sums[0])], 0
        ).swapaxes(0, 1)
        beyond.append(lax.ppermute(both, "energy", [(0, n - 1)]))
        beyond.append(lax.ppermute(both, "energy", [(n - 1, 0)]))

    terms = [[[] for _ in range(atoms)] for _ in range(cores)]
    base = 0
    for count in chunks_of(half):
        sums = sandwich(
            offsets, occupation, right, left_near, groups, atoms, momenta, base, grid_total, edev, False, line, out_rows, count
        )
        base += count
        for s in range(atoms - 1, -1, -1):
            for t in range(cores):
                block = sums[s * cores + t]
                if s or t:
                    pairs = [
                        (i * cores + k, ((i + s) % atoms) * cores + (k + t) % cores)
                        for i in range(atoms)
                        for k in range(cores)
                    ]
                    block = lax.ppermute(block, ("atom", "kz"), pairs)
                terms[t][s].append(block)
    chunks = chunks_of(half)
    entries = [[[] for _ in range(half)] for _ in range(cores)]
    late = [[[] for _ in range(half)] for _ in range(cores)]
    early, last = Terms(), Terms()
    for t in range(cores):
        for s in range(atoms):
            first = 0
            for chunk, block in enumerate(terms[t][s]):
                held = (last, late) if s and chunk == len(chunks) - 1 else (early, entries)
                held[0].append(block)
                for row in range(chunks[chunk]):
                    held[1][t][first + row].append((block, row))
                first += chunks[chunk]
    total = gathered(entries, half, early)
    return gathered(late, half, last, [total] + beyond)


def solution(mesh):
    return jax.shard_map(
        shards,
        mesh=mesh,
        in_specs=(P(("grp", "kz"), "energy", "atom", None), P("atom", None, None), P(), P(), P()),
        out_specs=P(("grp", "atom", "kz"), "energy", None),
        check_vma=False,
    )
```

```python
import functools

import jax
import jax.numpy as jnp
from jax import lax
from jax.experimental import pallas as pl
from jax.experimental.pallas import tpu as pltpu
from jax.sharding import PartitionSpec as P


MODES = 3
REACH = 2
PIECES = 2


def chunks_of(half):
    return [1] * half


def quotient(x, n):
    return lax.shift_right_logical(x, jnp.int32(n.bit_length() - 1)) if n & (n - 1) == 0 else lax.div(x, n)


def remainder(x, n):
    return x & (n - 1) if n & (n - 1) == 0 else lax.rem(x, n)


def halves(x):
    high = x.astype(jnp.bfloat16)
    return high, (x - high.astype(jnp.float32)).astype(jnp.bfloat16)


def side_by_side(out, mode, x):
    high, low = halves(x)
    depth = x.shape[1]
    out[mode, :, pl.ds(0, depth)] = high
    out[mode, :, pl.ds(depth, depth)] = high
    out[mode, :, pl.ds(2 * depth, depth)] = low


def prepare(atoms, parts, cores, owners, couplings, *refs):
    right_high, right_low, far, near, held, sems = refs[-6:]
    pieces = refs[:-6]
    atom, core, part = (lax.axis_index(a) for a in ("atom", "kz", "grp"))
    table_rows = couplings.shape[0]
    for mode in range(MODES):
        row = lax.rem(owners[mode], table_rows)
        behind = lax.rem(atom - lax.div(owners[mode], table_rows) + atoms, atoms)

        @pl.when(behind == 0)
        def _(mode=mode, row=row):
            pltpu.make_async_copy(couplings.at[row], held.at[mode], sems.at[mode]).start()

        for s in range(1, atoms):

            @pl.when(behind == s)
            def _(mode=mode, row=row, s=s):
                for d in range(parts):
                    for o in range(cores):
                        piece = pieces[((s - 1) * parts + d) * cores + o]
                        strip = piece.shape[1]
                        at = lax.rem(part - d + parts, parts) * cores + lax.rem(core - o + cores, cores)
                        rows = pl.ds(pl.multiple_of(at * strip, 8), strip)
                        pltpu.make_async_copy(piece.at[row], held.at[mode, rows], sems.at[mode]).start()

    @pl.loop(0, MODES)
    def _(mode):
        pltpu.make_async_copy(held.at[mode], held.at[mode], sems.at[mode]).wait()
        right_high[mode], right_low[mode] = halves(held[mode].T)
        rows, depth = far.shape[1], near.shape[2] // 3
        side_by_side(far, mode, held[mode, pl.ds(pl.multiple_of(atom * rows, 8), rows), :])
        side_by_side(near, mode, held[mode, :, pl.ds(pl.multiple_of(atom * depth, 128), depth)])


def guard(steps, out):
    for mode in range(MODES):
        out[mode] = steps[mode]


def add_momenta(theirs, first, green, *refs):
    out, held, total, arrived, left = refs[-5:]
    given = refs[:-5]
    momenta, count, size = green.shape[0], held.shape[0], held.shape[2]
    core = lax.axis_index("kz")
    base = (1 - core if theirs else core) * count
    for e in range(count):
        for k in range(momenta):
            pltpu.make_async_copy(green.at[k, base + e, pl.ds(first, size)], held.at[e, k], arrived.at[e]).start()
        for ref in given:
            pltpu.make_async_copy(ref.at[e], held.at[e, momenta], arrived.at[e]).start()

    @pl.loop(0, count)
    def _(e):
        pltpu.make_async_copy(held.at[e], held.at[e], arrived.at[e]).wait()
        value = held[e, 0]
        for k in range(1, held.shape[1]):
            value = value + held[e, k]
        total[e] = value
        pltpu.make_async_copy(total.at[e], out.at[e], left.at[e]).start()

    for e in range(count):
        pltpu.make_async_copy(total.at[e], out.at[e], left.at[e]).wait()


def split_dot(n_groups, n_parts, n_atoms, momenta, base, grid_total, edev, far, line, steps, occupation, right_high, right_low, left, *refs):
    sources = [
        [refs[(g * 2 + h) * n_parts : (g * 2 + h + 1) * n_parts] for h in range(2)]
        for g in range(n_groups)
    ]
    outs = refs[n_groups * 2 * n_parts : -4]
    planes, inner, total, sems = refs[-4:]
    count, size = outs[0].shape[:2]
    rows = planes.shape[2]
    half_planes = edev // 2
    place, core, atom = (lax.axis_index(a) for a in ("energy", "kz", "atom"))
    blocks = grid_total // edev
    target = blocks - 1 - place if far else place
    base = base + core * half_planes

    def source_of(energy, mode, side):
        step = steps[mode] if side == 0 else -steps[mode]
        source = remainder(target * edev + base + energy + step + grid_total, grid_total)
        rel = quotient(source, edev) - place
        if far:
            valid = rel == 0
        elif line:
            valid = jnp.abs(rel) <= REACH
        else:
            rel = remainder(rel + REACH + blocks, blocks) - REACH
            valid = rel <= REACH
        group = jnp.where(valid, rel + n_groups // 2, n_groups // 2)
        return valid, group, remainder(source, edev)

    def fetch(energy, buffer):
        for mode in range(MODES):
            for side in range(2):
                _, group, plane = source_of(energy, mode, side)
                other = jnp.where(quotient(plane, half_planes) == core, 0, 1)
                at = remainder(plane, half_planes)
                slot = mode * 2 + side
                for g in range(n_groups):

                    @pl.when(group == g)
                    def _(g=g, at=at, slot=slot, other=other, mode=mode):
                        for h in range(2):

                            @pl.when(other == h)
                            def _(h=h):
                                first = 0
                                for ref in sources[g][h]:
                                    depth = ref.shape[1]
                                    start = first
                                    if far:
                                        per = rows // n_atoms
                                        behind = lax.rem(atom - first // per + n_atoms, n_atoms)
                                        start = pl.multiple_of(behind * per + first % per, 8)
                                    pltpu.make_async_copy(
                                        ref.at[at], planes.at[buffer, slot, pl.ds(start, depth)], sems.at[buffer, slot]
                                    ).start(priority=0 if mode == 0 else 1)
                                    first += depth

    fetch(0, 0)

    @pl.loop(0, count)
    def _(energy):
        buffer = energy & 1

        if count > 1:

            @pl.when(energy + 1 < count)
            def _():
                fetch(energy + 1, 1 - buffer)

        dot = functools.partial(jnp.dot, preferred_element_type=jnp.float32)
        scales = [
            jnp.where(source_of(energy, mode, side)[0], (occupation[mode] + (1.0 - side)) * (1.0 / momenta), 0.0)
            for mode in range(MODES)
            for side in range(2)
        ]
        for mode in range(MODES):
            for slot in (2 * mode, 2 * mode + 1):
                held = planes.at[buffer, slot]
                pltpu.make_async_copy(held, held, sems.at[buffer, slot]).wait()
            combined = scales[2 * mode] * planes[buffer, 2 * mode] + scales[2 * mode + 1] * planes[buffer, 2 * mode + 1]
            if far:
                high, low = halves(combined)
                inner[mode, pl.ds(0, rows)] = high
                inner[mode, pl.ds(rows, rows)] = low
                inner[mode, pl.ds(2 * rows, rows)] = high
                high, low = halves(dot(left[mode], inner[mode]))
                term = dot(high, right_high[mode]) + dot(low, right_high[mode]) + dot(high, right_low[mode])
                total[...] = term if mode == 0 else total[...] + term
                continue
            high = combined.astype(jnp.bfloat16)
            low = (combined - high.astype(jnp.float32)).astype(jnp.bfloat16)
            product = dot(high, right_high[mode]) + dot(low, right_high[mode]) + dot(high, right_low[mode])
            high = product.astype(jnp.bfloat16)
            low = (product - high.astype(jnp.float32)).astype(jnp.bfloat16)
            inner[mode, pl.ds(0, rows)] = high
            inner[mode, pl.ds(rows, rows)] = low
            inner[mode, pl.ds(2 * rows, rows)] = high
        for index, out in enumerate(outs):
            s, t = index // 2, index % 2
            block = lax.rem(core + t, 2)
            if far:
                out[energy] = total[pl.ds(pl.multiple_of(block * size, 8), size)]
                continue
            block = block + 2 * lax.rem(atom + s, n_atoms)
            where = pl.ds(pl.multiple_of(block * size, 8), size)
            result = dot(left[0, where], inner[0])
            for mode in range(1, MODES):
                result = result + dot(left[mode, where], inner[mode])
            out[energy] = result


def sandwich(steps, occupation, right, left, groups, n_atoms, momenta, base, grid_total, edev, far, line, out_rows, count):
    order = right[0].shape[-1]
    flat = [part for group in groups for half in group for part in half]
    rows = sum(part.shape[1] for part in groups[0][0])
    n_out = left.shape[1] // out_rows
    buffers = min(count, 2)
    held = 4 * (2 * MODES * buffers + 6) * rows * order + 2 * 3 * MODES * rows * order + (6 << 20)
    held += 4 * left.shape[1] * order * (count + 3) + 4 * MODES * order * order + 2 * left.size
    flops = count * 2 * 3 * MODES * (rows * order * order + left.shape[1] * rows * order)
    return pl.pallas_call(
        functools.partial(split_dot, len(groups), len(groups[0][0]), n_atoms, momenta, base, grid_total, edev, far, line),
        out_shape=[jax.ShapeDtypeStruct((count, out_rows, order), jnp.float32)] * n_out,
        in_specs=[pl.BlockSpec(memory_space=pltpu.SMEM)] * 2
        + [pl.BlockSpec(memory_space=pltpu.VMEM)] * 3
        + [pl.BlockSpec(memory_space=pltpu.HBM)] * len(flat),
        out_specs=[pl.BlockSpec(memory_space=pltpu.VMEM)] * n_out,
        scratch_shapes=[
            pltpu.VMEM((buffers, 2 * MODES, rows, order), jnp.float32),
            pltpu.VMEM((MODES, 3 * rows, order), jnp.bfloat16),
            pltpu.VMEM((left.shape[1] if far else 8, order), jnp.float32),
            pltpu.SemaphoreType.DMA((2, 2 * MODES)),
        ],
        compiler_params=pltpu.CompilerParams(vmem_limit_bytes=held),
        cost_estimate=pl.CostEstimate(
            flops=flops,
            bytes_accessed=count * 4 * (2 * MODES * rows * order + left.shape[1] * order),
            transcendentals=0,
        ),
        name="far_sandwich" if far else "near_sandwich",
    )(steps, occupation, right[0], right[1], left, *flat)


def gather_early(layout, count, *refs):
    out = refs[-1]
    core = lax.axis_index("kz")
    group = 16
    for own in range(2):

        @pl.when(core == own)
        def _(own=own):
            @pl.loop(0, out.shape[0] // group)
            def _(at):
                rows = pl.ds(pl.multiple_of(at * group, group), group)
                for half, energies in enumerate(layout):
                    where = (own if half == 0 else 1 - own) * count
                    for j, terms in enumerate(energies):
                        total = None
                        for ref, row in terms:
                            total = refs[ref][row, rows] if total is None else total + refs[ref][row, rows]
                        out[rows, where + j, :] = total


def gather_late(layout, count, whole, *refs):
    out, total, sem = refs[-3:]
    full = refs[-3 - whole : -3]
    core = lax.axis_index("kz")
    group = 32

    @pl.loop(0, total.shape[0] // group)
    def _(at):
        rows = pl.ds(pl.multiple_of(at * group, group), group)
        value = full[0][rows]
        for ref in full[1:]:
            value = value + ref[rows]
        total[rows] = value
        for own in range(2):

            @pl.when(core == own)
            def _(own=own):
                for half, energies in enumerate(layout):
                    where = (own if half == 0 else 1 - own) * count
                    for j, terms in enumerate(energies):
                        if terms:
                            value = total[rows, where + j, :]
                            for ref, row in terms:
                                value = value + refs[ref][row, rows]
                            total[rows, where + j, :] = value

        pltpu.make_async_copy(total.at[rows], out.at[rows], sem).start()

    pltpu.make_async_copy(total, out, sem).wait()


def gathered(layout, count, arrays, before=()):
    terms = [[[(arrays.index(x), row) for x, row in entry] for entry in energies] for energies in layout]
    out_rows, order = arrays[0].shape[1:]
    arrays = list(arrays) + list(before)
    shape = (out_rows, 2 * count, order)
    size = 4 * sum(x.size for x in arrays) + 4 * 2 * count * out_rows * order
    vmem = pl.BlockSpec(memory_space=pltpu.VMEM)
    if before:
        kernel = functools.partial(gather_late, terms, count, len(before))
        scratch = [pltpu.VMEM(shape, jnp.float32), pltpu.SemaphoreType.DMA]
    else:
        kernel, scratch = functools.partial(gather_early, terms, count), []
    return pl.pallas_call(
        kernel,
        out_shape=jax.ShapeDtypeStruct(shape, jnp.float32),
        in_specs=[vmem] * len(arrays),
        out_specs=pl.BlockSpec(memory_space=pltpu.HBM) if before else vmem,
        scratch_shapes=scratch,
        compiler_params=pltpu.CompilerParams(vmem_limit_bytes=8 << 20),
        cost_estimate=pl.CostEstimate(flops=size // 4, bytes_accessed=size, transcendentals=0),
    )(*arrays)


class Terms(list):
    def index(self, x):
        return next(i for i, y in enumerate(self) if y is x)


def shards(green, couplings, occupation, offsets, owners):
    momenta_here, edev, brows, order = green.shape
    n, atoms, cores = lax.axis_size("energy"), lax.axis_size("atom"), lax.axis_size("kz")
    momenta = momenta_here * cores
    grid_total = n * edev
    parts = lax.axis_size("grp")
    _, core, part = (lax.axis_index(a) for a in ("atom", "kz", "grp"))
    line = n == 2 * REACH
    half = edev // cores
    swap = [(i, (i + 1) % cores) for i in range(cores)]
    around = [[(i, (i + s) % atoms) for i in range(atoms)] for s in range(atoms)]

    size = brows // PIECES

    def summed(theirs, piece, *more):
        return pl.pallas_call(
            functools.partial(add_momenta, theirs, piece * size),
            out_shape=jax.ShapeDtypeStruct((half, size, order), jnp.float32),
            in_specs=[pl.BlockSpec(memory_space=pltpu.HBM)] * (1 + len(more)),
            out_specs=pl.BlockSpec(memory_space=pltpu.HBM),
            scratch_shapes=[
                pltpu.VMEM((half, momenta_here + len(more), size, order), jnp.float32),
                pltpu.VMEM((half, size, order), jnp.float32),
                pltpu.SemaphoreType.DMA((half,)),
                pltpu.SemaphoreType.DMA((half,)),
            ],
            compiler_params=pltpu.CompilerParams(vmem_limit_bytes=67_000_000),
            cost_estimate=pl.CostEstimate(
                flops=momenta_here * half * size * order,
                bytes_accessed=4 * (momenta_here + 1 + len(more)) * half * size * order,
                transcendentals=0,
            ),
            name="add_momenta",
        )(green, *more)

    own = []
    for piece in range(PIECES):
        given = summed(True, piece)
        given = lax.ppermute(given, "kz", swap)
        own.append(summed(False, piece, given))

    if line:
        up = [[(i, i + 1) for i in range(d, n - 1)] for d in range(REACH)]
        down = [[(i, i - 1) for i in range(n - 1 - d, 0, -1)] for d in range(REACH)]
    else:
        up = [[(i, (i + 1) % n) for i in range(n)]] * REACH
        down = [[(i, (i - 1) % n) for i in range(n)]] * REACH
    streams = {0: own}
    for d in range(1, REACH + 1):
        streams[-d] = [lax.ppermute(x, "energy", up[d - 1]) for x in streams[1 - d]]
        streams[d] = [lax.ppermute(x, "energy", down[d - 1]) for x in streams[d - 1]]
    groups = []
    for d in range(-REACH, REACH + 1):
        axes, pairs = "kz", swap
        if line and abs(d) == REACH:
            axes = ("energy", "kz")
            pairs = [
                (i * cores + k, i * cores + (k + 1) % cores) for i in range(n) if 0 <= i + d < n for k in range(cores)
            ]
        groups.append((streams[d], [lax.ppermute(x, axes, pairs) for x in streams[d]]))

    table_rows = couplings.shape[0]
    strip = order // (cores * parts)
    mine = lax.dynamic_slice(couplings, (0, (part * cores + core) * strip, 0), (table_rows, strip, order))
    others = []
    for s in range(1, atoms):
        got = lax.ppermute(mine, "atom", around[s])
        ahead = [got] + [
            lax.ppermute(got, "grp", [(i, (i + d) % parts) for i in range(parts)]) for d in range(1, parts)
        ]
        others.append([(x, lax.ppermute(x, "kz", swap)) for x in ahead])
    out_rows = order // (atoms * cores)
    flat = [x for pieces in others for both in pieces for x in both]
    hbm, vmem = pl.BlockSpec(memory_space=pltpu.HBM), pl.BlockSpec(memory_space=pltpu.VMEM)
    shapes = [(order, order), (order, order), (cores * out_rows, 3 * order), (order, 3 * brows)]
    *right, left_far, left_near = pl.pallas_call(
        functools.partial(prepare, atoms, parts, cores),
        out_shape=[jax.ShapeDtypeStruct((MODES,) + shape, jnp.bfloat16) for shape in shapes],
        in_specs=[pl.BlockSpec(memory_space=pltpu.SMEM)] + [hbm] * (1 + len(flat)),
        out_specs=[vmem] * len(shapes),
        scratch_shapes=[pltpu.VMEM((MODES, order, order), jnp.float32), pltpu.SemaphoreType.DMA((MODES,))],
        compiler_params=pltpu.CompilerParams(vmem_limit_bytes=32 << 20),
        cost_estimate=pl.CostEstimate(
            flops=8 * MODES * order * order, bytes_accessed=10 * MODES * order * order, transcendentals=0
        ),
        name="prepare",
    )(owners, couplings, *flat)

    beyond = []
    if line:
        got = [lax.ppermute(x, "atom", around[s]) for s in range(1, atoms) for x in own]
        whole = (
            list(own) + got,
            groups[REACH][1] + [lax.ppermute(x, "kz", swap) for x in got],
        )
        smem = pl.BlockSpec(memory_space=pltpu.SMEM)
        held = pl.pallas_call(
            guard,
            out_shape=jax.ShapeDtypeStruct(offsets.shape, offsets.dtype),
            in_specs=[smem],
            out_specs=smem,
            compiler_params=pltpu.CompilerParams(vmem_limit_bytes=1 << 20),
            name="guard",
        )(offsets)
        sums = sandwich(
            held, occupation, right, left_far, [whole], atoms, momenta, 0, grid_total, edev, True, line, out_rows, half
        )
        swapped = lax.ppermute(sums[1], "kz", swap)
        both = jnp.concatenate(
            [jnp.where(core == 0, sums[0], swapped), jnp.where(core == 0, swapped, sums[0])], 0
        ).swapaxes(0, 1)
        beyond.append(lax.ppermute(both, "energy", [(0, n - 1)]))
        beyond.append(lax.ppermute(both, "energy", [(n - 1, 0)]))

    terms = [[[] for _ in range(atoms)] for _ in range(cores)]
    base = 0
    for count in chunks_of(half):
        sums = sandwich(
            offsets, occupation, right, left_near, groups, atoms, momenta, base, grid_total, edev, False, line, out_rows, count
        )
        base += count
        for s in range(atoms - 1, -1, -1):
            for t in range(cores):
                block = sums[s * cores + t]
                if s or t:
                    pairs = [
                        (i * cores + k, ((i + s) % atoms) * cores + (k + t) % cores)
                        for i in range(atoms)
                        for k in range(cores)
                    ]
                    block = lax.ppermute(block, ("atom", "kz"), pairs)
                terms[t][s].append(block)
    chunks = chunks_of(half)
    entries = [[[] for _ in range(half)] for _ in range(cores)]
    late = [[[] for _ in range(half)] for _ in range(cores)]
    early, last = Terms(), Terms()
    for t in range(cores):
        for s in range(atoms):
            first = 0
            for chunk, block in enumerate(terms[t][s]):
                held = (last, late) if s and chunk == len(chunks) - 1 else (early, entries)
                held[0].append(block)
                for row in range(chunks[chunk]):
                    held[1][t][first + row].append((block, row))
                first += chunks[chunk]
    total = gathered(entries, half, early)
    return gathered(late, half, last, [total] + beyond)


def solution(mesh):
    return jax.shard_map(
        shards,
        mesh=mesh,
        in_specs=(P(("grp", "kz"), "energy", "atom", None), P("atom", None, None), P(), P(), P()),
        out_specs=P(("grp", "atom", "kz"), "energy", None),
        check_vma=False,
    )
```
